32 devices in a mesh: dp: 4 (over z), row: 2 (over y), col: 4 (over x, core).
Axes of the slice: x: 2, y: 2, z: 4, core: 2. Of those that a mesh axis runs over, the one named last changes fastest.
Arguments:
- inputs: bfloat16 [2048, 1024], P(('dp', 'col'), 'row'), may hold values from -6 to 6
- positions: int32 [8, 256], P(('dp', 'row')), may hold values from 0 to 2047, as said below
- segments: int32 [8, 256], P(('dp', 'row')), may hold values from 0 to 3, as said below
- cotangent: bfloat16 [2048, 1024], P(('dp', 'col'), 'row'), may hold values from -6 to 6
- w_query: bfloat16 [2, 1024, 2048], P(None, 'row', 'col'), may hold values from -0.1875 to 0.1875
- w_key: bfloat16 [2, 1024, 1024], P(None, 'row', 'col'), may hold values from -0.1875 to 0.1875
- w_value: bfloat16 [2, 1024, 1024], P(None, 'row', 'col'), may hold values from -0.1875 to 0.1875
- w_output: bfloat16 [2, 2048, 1024], P(None, 'col', 'row'), may hold values from -1 to 1
- w_gate: bfloat16 [2, 1024, 3072], P(None, 'row', 'col'), may hold values from -0.1875 to 0.1875
- w_up: bfloat16 [2, 1024, 3072], P(None, 'row', 'col'), may hold values from -0.1875 to 0.1875
- w_down: bfloat16 [2, 3072, 1024], P(None, 'col', 'row'), may hold values from -0.109375 to 0.109375
- attn_gain: float32 [2, 1024], replicated, may hold values from 0.25 to 1.75
- mlp_gain: float32 [2, 1024], replicated, may hold values from 0.25 to 1.75
- query_gain: float32 [2, 128], replicated, may hold values from 0.25 to 1.75
- key_gain: float32 [2, 128], replicated, may hold values from 0.25 to 1.75
Outputs:
- outputs: float32 [2048, 1024], P(('dp', 'col'), 'row')
- d_inputs: float32 [2048, 1024], P(('dp', 'col'), 'row')
- grad_w_query: float32 [2, 1024, 2048], P(None, ('row', 'dp'), 'col')
- grad_w_key: float32 [2, 1024, 1024], P(None, ('row', 'dp'), 'col')
- grad_w_value: float32 [2, 1024, 1024], P(None, ('row', 'dp'), 'col')
- grad_w_output: float32 [2, 2048, 1024], P(None, ('col', 'dp'), 'row')
- grad_w_gate: float32 [2, 1024, 3072], P(None, ('row', 'dp'), 'col')
- grad_w_up: float32 [2, 1024, 3072], P(None, ('row', 'dp'), 'col')
- grad_w_down: float32 [2, 3072, 1024], P(None, ('col', 'dp'), 'row')
- grad_attn_gain: float32 [2, 1024], replicated
- grad_mlp_gain: float32 [2, 1024], replicated
- grad_query_gain: float32 [2, 128], replicated
- grad_key_gain: float32 [2, 128], replicated
The draws below stay inside these ranges and needn't reach their ends.
Inputs may be any that keep to these rules, and one draw needn't show every extreme that they name: `segments`: segment numbers never fall along a sequence. `positions`: within a document, each token's position is one more than its predecessor's.
All inputs are finite; a program needn't handle non-finite values.
Results may differ from the reference program's by a relative error of at most 0.024.
Values may be sent and summed in bfloat16 or wider, within the bound.
No kernel may reach another device: no remote copies, remote signals or barrier semaphores. Data moves between devices by JAX's collectives and lax.ppermute only.
A program may use at most 128 MiB of HBM per device.

```python
import math
import jax
import jax.numpy as jnp
from jax import lax

D = 1024
H = 16
KV = 8
HD = 128
FF = 3072
SEQ = 256
LAYERS = 2
SEQ_DEV = 2
NSEQ = 8
TOKENS = 2048
N_DP = 4


def segment_cuts(key):
    return jnp.sort(jax.random.randint(jax.random.fold_in(key, 11), (NSEQ, 3), 1, SEQ), axis=1)


def draw_segments(key, part):
    seg_cuts = segment_cuts(key)
    token_order = jnp.arange(SEQ, dtype=jnp.int32)
    reached = token_order[None, :, None] >= seg_cuts[:, None, :]
    return jnp.sum(reached.astype(jnp.int32), axis=2).astype(jnp.int32)


def draw_positions(key, part):
    seg_cuts = segment_cuts(key)
    token_order = jnp.arange(SEQ, dtype=jnp.int32)
    reached = token_order[None, :, None] >= seg_cuts[:, None, :]
    seg_start = jnp.max(jnp.where(reached, seg_cuts[:, None, :], 0), axis=2)
    first_cut = seg_cuts[:, :1]
    top_offset = 2048 - first_cut
    drawn = jax.random.randint(jax.random.fold_in(key, 12), (NSEQ, 1), 0, top_offset + 1)
    row_order = jnp.arange(NSEQ, dtype=jnp.int32)[:, None]
    carried = jnp.where(row_order == 0, top_offset, drawn)
    first_doc = jnp.logical_not(reached[:, :, 0])
    return (token_order[None, :] - seg_start + jnp.where(first_doc, carried, 0)).astype(jnp.int32)


def block_scale(stream_key, extent, pieces, low, high):
    def one(position, parts):
        steps = jax.random.uniform(jax.random.fold_in(jax.random.fold_in(stream_key, 6), position), (parts,), jnp.float32, low / len(pieces), high / len(pieces))
        return jnp.repeat(jnp.exp(steps), extent[position] // parts).reshape((-1,) + (1,) * (len(extent) - position - 1))

    factor_of = one(*pieces[0])
    for cut in pieces[1:]:
        factor_of = factor_of * one(*cut)
    return factor_of


def normal_values(stream_key, dims, scale, reach, cuts=(), held_as=jnp.bfloat16):
    loudness = block_scale(stream_key, dims, cuts, -0.22, 0.18) if cuts else 1.0
    values = jax.random.normal(stream_key, dims, jnp.float32) * scale * loudness
    return jnp.minimum(jnp.maximum(values, -reach), reach).astype(held_as)


def setup_inputs(seed: int = 0) -> dict:
    splits = jax.random.split(jax.random.key(seed), 16)
    return {
        "inputs": normal_values(splits[0], (TOKENS, D), 1.0, 6.0, ((0, 16), (1, 2))),
        "positions": draw_positions(jax.random.fold_in(splits[15], 71), 0),
        "segments": draw_segments(jax.random.fold_in(splits[15], 71), 0),
        "cotangent": normal_values(splits[3], (TOKENS, D), 1.0, 6.0, ((0, 16), (1, 2))),
        "w_query": normal_values(splits[4], (LAYERS, D, H * HD), D ** -0.5, 0.1875, ((1, 2), (2, 4))),
        "w_key": normal_values(splits[5], (LAYERS, D, KV * HD), D ** -0.5, 0.1875, ((1, 2), (2, 4))),
        "w_value": normal_values(splits[6], (LAYERS, D, KV * HD), D ** -0.5, 0.1875, ((1, 2), (2, 4))),
        "w_output": normal_values(splits[7], (LAYERS, H * HD, D), (H * HD // 64) ** -0.5, 1.0, ((1, 4), (2, 2))),
        "w_gate": normal_values(splits[8], (LAYERS, D, FF), D ** -0.5, 0.1875, ((1, 2), (2, 4))),
        "w_up": normal_values(splits[9], (LAYERS, D, FF), D ** -0.5, 0.1875, ((1, 2), (2, 4))),
        "w_down": normal_values(splits[10], (LAYERS, FF, D), FF ** -0.5, 0.109375, ((1, 4), (2, 2))),
        "attn_gain": jnp.clip(1.0 + 0.15 * jax.random.normal(splits[11], (LAYERS, D), jnp.float32), 0.25, 1.75),
        "mlp_gain": jnp.clip(1.0 + 0.15 * jax.random.normal(splits[12], (LAYERS, D), jnp.float32), 0.25, 1.75),
        "query_gain": jnp.clip(1.0 + 0.15 * jax.random.normal(splits[13], (LAYERS, HD), jnp.float32), 0.25, 1.75),
        "key_gain": jnp.clip(1.0 + 0.15 * jax.random.normal(splits[14], (LAYERS, HD), jnp.float32), 0.25, 1.75),
    }


EPS = 1e-06
THETA = 1000000.0

def matmul_plain(left_side, right_side):
    return jnp.dot(left_side, right_side, preferred_element_type=jnp.float32)

def matmul_right_t(left_side, right_side):
    return lax.dot_general(left_side, right_side, (((1,), (1,)), ((), ())), preferred_element_type=jnp.float32)

def matmul_left_t(left_side, right_side):
    return lax.dot_general(left_side, right_side, (((0,), (0,)), ((), ())), preferred_element_type=jnp.float32)

def rope_tables(positions):
    half_dim = HD // 2
    frequencies = THETA ** (-2.0 * jnp.arange(half_dim, dtype=jnp.float32) / HD)
    angles = positions.reshape(-1).astype(jnp.float32)[:, None] * frequencies[None, :]
    return (jnp.cos(angles), jnp.sin(angles))

def rotate_forward(values, cos_table, sin_table):
    half_dim = values.shape[-1] // 2
    first_half = values[..., :half_dim]
    second_half = values[..., half_dim:]
    cos_part = cos_table[:, None, :]
    sin_part = sin_table[:, None, :]
    return jnp.concatenate([first_half * cos_part - second_half * sin_part, second_half * cos_part + first_half * sin_part], axis=-1)

def rotate_backward(values, cos_table, sin_table):
    half_dim = values.shape[-1] // 2
    first_half = values[..., :half_dim]
    second_half = values[..., half_dim:]
    cos_part = cos_table[:, None, :]
    sin_part = sin_table[:, None, :]
    return jnp.concatenate([first_half * cos_part + second_half * sin_part, second_half * cos_part - first_half * sin_part], axis=-1)

def head_norm(values, gain):
    inv_scale = lax.rsqrt(lax.optimization_barrier(jnp.mean(values * values, axis=-1, keepdims=True)) + EPS)
    return (values * inv_scale * gain, inv_scale)

def head_norm_backward(d_normed, values, inv_scale, gain):
    scaled = d_normed * gain
    grad_gain = lax.optimization_barrier(jnp.sum(d_normed * values * inv_scale, axis=(0, 1)))
    projection = lax.optimization_barrier(jnp.mean(scaled * values, axis=-1, keepdims=True))
    return (inv_scale * scaled - values * inv_scale * inv_scale * inv_scale * projection, grad_gain)

def norm_backward(d_normed, residual, inv_scale, gain):
    scaled = d_normed * gain
    grad_gain = lax.optimization_barrier(jnp.sum(d_normed * residual * inv_scale, axis=0))
    projection = lax.optimization_barrier(jnp.mean(scaled * residual, axis=-1, keepdims=True))
    return (inv_scale * scaled - residual * inv_scale * inv_scale * inv_scale * projection, grad_gain)

def sequence_mask(seg_ids):
    token_order = jnp.arange(seg_ids.shape[0])
    return (seg_ids[:, None] == seg_ids[None, :]) & (token_order[None, :] <= token_order[:, None])

def as_float(values):
    return values.astype(jnp.float32)

def attend_forward(seq_items):
    rot_queries, rot_keys, values, allowed = seq_items
    score_scale = 1.0 / math.sqrt(HD)
    scores = jnp.einsum('qkgd,skd->kgqs', as_float(rot_queries), as_float(rot_keys)) * score_scale
    exp_terms = jnp.where(allowed, jnp.exp(scores), 0.0)
    exp_total = lax.optimization_barrier(jnp.sum(exp_terms, axis=-1, keepdims=True))
    soft_probs = (exp_terms / exp_total).astype(jnp.bfloat16)
    attended = jnp.einsum('kgqs,skd->qkgd', as_float(soft_probs), as_float(values))
    return (attended.astype(jnp.bfloat16), jnp.log(exp_total[..., 0]))

def attend_backward(seq_items):
    rot_queries, rot_keys, values, allowed, attended, log_total, d_attended = seq_items
    score_scale = 1.0 / math.sqrt(HD)
    scores = jnp.einsum('qkgd,skd->kgqs', as_float(rot_queries), as_float(rot_keys)) * score_scale
    p_full = jnp.where(allowed, jnp.exp(scores - log_total[..., None]), 0.0)
    p_round = p_full.astype(jnp.bfloat16)
    d_values = jnp.einsum('kgqs,qkgd->skd', as_float(p_round), as_float(d_attended))
    d_probs = jnp.einsum('qkgd,skd->kgqs', as_float(d_attended), as_float(values))
    row_delta = jnp.einsum('qkgd,qkgd->kgq', as_float(d_attended), as_float(attended))
    d_scores = (p_full * (d_probs - row_delta[..., None])).astype(jnp.bfloat16)
    d_rot_q = jnp.einsum('kgqs,skd->qkgd', as_float(d_scores), as_float(rot_keys)) * score_scale
    d_rot_k = jnp.einsum('kgqs,qkgd->skd', as_float(d_scores), as_float(rot_queries)) * score_scale
    return (d_rot_q, d_rot_k, d_values)

def block_forward(residual, cos_table, sin_table, seq_masks, weights):
    w_q, w_k, w_v, w_o, w_g, w_u, w_d, gain_attn, gain_mlp, gain_q, gain_k = weights
    num_rows = residual.shape[0]
    seq_count = num_rows // SEQ
    group = H // KV
    inv_attn = lax.rsqrt(lax.optimization_barrier(jnp.mean(residual * residual, axis=1, keepdims=True)) + EPS)
    normed1 = (residual * inv_attn * gain_attn).astype(jnp.bfloat16)
    queries = matmul_plain(normed1, w_q).reshape(num_rows, H, HD)
    keys_raw = matmul_plain(normed1, w_k).reshape(num_rows, KV, HD)
    values = matmul_plain(normed1, w_v).astype(jnp.bfloat16).reshape(num_rows, KV, HD)
    normed_q, inv_q = head_norm(queries, gain_q)
    normed_k, inv_k = head_norm(keys_raw, gain_k)
    rot_q = rotate_forward(normed_q, cos_table, sin_table).astype(jnp.bfloat16)
    rot_k = rotate_forward(normed_k, cos_table, sin_table).astype(jnp.bfloat16)
    attn_seq, log_total = lax.map(attend_forward, (rot_q.reshape(seq_count, SEQ, KV, group, HD), rot_k.reshape(seq_count, SEQ, KV, HD), values.reshape(seq_count, SEQ, KV, HD), seq_masks))
    attn = attn_seq.reshape(num_rows, H * HD)
    middle = residual + matmul_plain(attn, w_o)
    inv_mlp = lax.rsqrt(lax.optimization_barrier(jnp.mean(middle * middle, axis=1, keepdims=True)) + EPS)
    normed2 = (middle * inv_mlp * gain_mlp).astype(jnp.bfloat16)
    gate_pre = matmul_plain(normed2, w_g)
    up_proj = matmul_plain(normed2, w_u)
    hidden = (gate_pre * jax.nn.sigmoid(gate_pre) * up_proj).astype(jnp.bfloat16)
    output = middle + matmul_plain(hidden, w_d)
    cache = (residual, inv_attn, normed1, queries, keys_raw, inv_q, inv_k, rot_q, rot_k, values, attn, log_total, middle, inv_mlp, normed2, gate_pre, up_proj, hidden)
    return (output, cache)

def block_backward(d_out, cache, weights, cos_table, sin_table, seq_masks):
    w_q, w_k, w_v, w_o, w_g, w_u, w_d, gain_attn, gain_mlp, gain_q, gain_k = weights
    residual, inv_attn, normed1, queries, keys_raw, inv_q, inv_k, rot_q, rot_k, values, attn, log_total, middle, inv_mlp, normed2, gate_pre, up_proj, hidden = cache
    num_rows = residual.shape[0]
    seq_count = num_rows // SEQ
    group = H // KV
    d_out_round = d_out.astype(jnp.bfloat16)
    grad_down = matmul_left_t(hidden, d_out_round)
    d_hidden = matmul_right_t(d_out_round, w_d)
    sig_gate = jax.nn.sigmoid(gate_pre)
    d_gate = (d_hidden * up_proj * sig_gate * (1.0 + gate_pre * (1.0 - sig_gate))).astype(jnp.bfloat16)
    d_up = (d_hidden * gate_pre * sig_gate).astype(jnp.bfloat16)
    grad_gate = matmul_left_t(normed2, d_gate)
    grad_up = matmul_left_t(normed2, d_up)
    d_normed2 = matmul_right_t(d_gate, w_g) + matmul_right_t(d_up, w_u)
    d_middle_part, grad_mlp_gain = norm_backward(d_normed2, middle, inv_mlp, gain_mlp)
    d_middle = d_out + d_middle_part
    d_middle_round = d_middle.astype(jnp.bfloat16)
    grad_out = matmul_left_t(attn, d_middle_round)
    d_attn = matmul_right_t(d_middle_round, w_o).astype(jnp.bfloat16)
    d_rot_q, d_rot_k, d_values = lax.map(attend_backward, (rot_q.reshape(seq_count, SEQ, KV, group, HD), rot_k.reshape(seq_count, SEQ, KV, HD), values.reshape(seq_count, SEQ, KV, HD), seq_masks, attn.reshape(seq_count, SEQ, KV, group, HD), log_total, d_attn.reshape(seq_count, SEQ, KV, group, HD)))
    d_normed_q = rotate_backward(d_rot_q.reshape(num_rows, H, HD), cos_table, sin_table)
    d_normed_k = rotate_backward(d_rot_k.reshape(num_rows, KV, HD), cos_table, sin_table)
    d_queries, grad_q_gain = head_norm_backward(d_normed_q, queries, inv_q, gain_q)
    d_keys, grad_k_gain = head_norm_backward(d_normed_k, keys_raw, inv_k, gain_k)
    d_queries_round = d_queries.astype(jnp.bfloat16).reshape(num_rows, H * HD)
    d_keys_round = d_keys.astype(jnp.bfloat16).reshape(num_rows, KV * HD)
    d_values_round = d_values.astype(jnp.bfloat16).reshape(num_rows, KV * HD)
    grad_query = matmul_left_t(normed1, d_queries_round)
    grad_key = matmul_left_t(normed1, d_keys_round)
    grad_value = matmul_left_t(normed1, d_values_round)
    d_normed1 = matmul_right_t(d_queries_round, w_q) + matmul_right_t(d_keys_round, w_k) + matmul_right_t(d_values_round, w_v)
    d_resid_part, grad_attn_gain = norm_backward(d_normed1, residual, inv_attn, gain_attn)
    layer_grads = (grad_query, grad_key, grad_value, grad_out, grad_gate, grad_up, grad_down, grad_attn_gain, grad_mlp_gain, grad_q_gain, grad_k_gain)
    return (d_middle + d_resid_part, layer_grads)

def reference(inputs, positions, segments, cotangent, w_query, w_key, w_value, w_output, w_gate, w_up, w_down, attn_gain, mlp_gain, query_gain, key_gain):
    stacked = (w_query, w_key, w_value, w_output, w_gate, w_up, w_down, attn_gain, mlp_gain, query_gain, key_gain)
    block_tokens = SEQ_DEV * SEQ

    def one_block(carried, block_items):
        block_in, block_pos, block_seg, block_cot = block_items
        cos_table, sin_table = rope_tables(block_pos)
        seq_masks = jax.vmap(sequence_mask)(block_seg)
        residual = block_in.astype(jnp.float32)
        caches = []
        for layer_idx in range(LAYERS):
            layer_weights = tuple((item[layer_idx] for item in stacked))
            residual, cache = block_forward(residual, cos_table, sin_table, seq_masks, layer_weights)
            caches.append(cache)
        grad_flow = block_cot.astype(jnp.float32)
        layer_parts = [None] * LAYERS
        for layer_idx in reversed(range(LAYERS)):
            layer_weights = tuple((item[layer_idx] for item in stacked))
            grad_flow, layer_grads = block_backward(grad_flow, caches[layer_idx], layer_weights, cos_table, sin_table, seq_masks)
            layer_parts[layer_idx] = layer_grads
        summed = tuple((carried[slot_idx] + jnp.stack([layer_parts[layer_idx][slot_idx] for layer_idx in range(LAYERS)]) for slot_idx in range(11)))
        return (summed, (residual, grad_flow))
    initial = tuple((jnp.zeros(item.shape, jnp.float32) for item in stacked))
    block_inputs = (inputs.reshape(N_DP, block_tokens, D), positions.reshape(N_DP, SEQ_DEV, SEQ), segments.reshape(N_DP, SEQ_DEV, SEQ), cotangent.reshape(N_DP, block_tokens, D))
    grads, block_outs = lax.scan(one_block, initial, block_inputs)
    outputs = block_outs[0].reshape(TOKENS, D)
    d_inputs = block_outs[1].reshape(TOKENS, D)
    return (outputs, d_inputs, grads[0], grads[1], grads[2], grads[3], grads[4], grads[5], grads[6], grads[7], grads[8], grads[9], grads[10])
```

```python
import functools
import math

import jax
import jax.numpy as jnp
from jax import lax
from jax.experimental import pallas as pl
from jax.experimental.pallas import tpu as pltpu
from jax.sharding import PartitionSpec as P

HD = 128
SEQ = 256
EPS = 1e-06
THETA = 1000000.0
F32 = jnp.float32
BF16 = jnp.bfloat16


def dot_nn(a, b):
    return jnp.dot(a, b, preferred_element_type=F32)


def dot_nt(a, b):
    return lax.dot_general(a, b, (((1,), (1,)), ((), ())), preferred_element_type=F32)


def dot_tn(a, b):
    return lax.dot_general(a, b, (((0,), (0,)), ((), ())), preferred_element_type=F32)


def whole(shape):
    rank = len(shape)
    return pl.BlockSpec(tuple(shape), lambda *_: (0,) * rank)


def per_seq(shape):
    rest = len(shape) - 1
    return pl.BlockSpec((1,) + tuple(shape[1:]), lambda i, *_: (i,) + (0,) * rest)


def sds(shape, dtype):
    return jax.ShapeDtypeStruct(tuple(shape), dtype)


def call(kernel, grid, in_specs, out_specs, out_shape, flops, nbytes, row, args, scratch=()):
    return pl.pallas_call(
        kernel,
        grid_spec=pltpu.PrefetchScalarGridSpec(
            num_scalar_prefetch=1,
            grid=grid,
            in_specs=in_specs,
            out_specs=out_specs,
            scratch_shapes=list(scratch),
        ),
        out_shape=out_shape,
        cost_estimate=pl.CostEstimate(
            flops=int(flops), bytes_accessed=int(nbytes), transcendentals=0
        ),
    )(row, *args)


def both_halves(ref0, ref1, cols):
    return jnp.concatenate([ref0[0, :, cols], ref1[0, :, cols]], axis=0)


def rope_forward(v, cos2, sin2):
    return v * cos2 + pltpu.roll(v, v.shape[-1] // 2, 1) * sin2


def rope_backward(v, cos2, sin2):
    return v * cos2 - pltpu.roll(v, v.shape[-1] // 2, 1) * sin2


def head_inv(v):
    return lax.rsqrt(jnp.mean(v * v, axis=-1, keepdims=True) + EPS)


def feature_cols(row_ref, width):
    r = row_ref[0]
    own = pl.ds(pl.multiple_of(r * width, width), width)
    other = pl.ds(pl.multiple_of((1 - r) * width, width), width)
    return own, other


def norm_first_kernel(row_ref, a0, a1, gain, n0, n1):
    for src, dst in ((a0, n0), (a1, n1)):
        v = jnp.concatenate([src[0, 0], src[0, 1]], axis=-1).astype(F32)
        inv = lax.rsqrt(jnp.mean(v * v, axis=-1, keepdims=True) + EPS)
        dst[0] = (v * inv * gain[...]).astype(BF16)


def attn_fwd_kernel(
    row_ref, n0, n1, wq, wk, wv, rq, wo, ro, gq, gk, cos2, sin2, mask, p0, p1, qk_out, v_out, attn_out
):
    half = wq.shape[1]
    own, other = feature_cols(row_ref, half)
    qw = wq.shape[2]
    xo = both_halves(n0, n1, own)
    xt = both_halves(n0, n1, other)
    w_own = jnp.concatenate([wq[0], wk[0], wv[0]], axis=1)
    qkv = dot_nn(xo, w_own) + dot_nn(xt, rq[...])
    qk_out[0] = qkv[:, : qw + HD]
    v = qkv[:, qw + HD :].astype(BF16)
    v_out[0] = v
    c2 = cos2[0]
    s2 = sin2[0]
    k = qkv[:, qw : qw + HD]
    rot_k = rope_forward(k * head_inv(k) * gk[...], c2, s2).astype(BF16)
    allowed = mask[0] > 0
    parts = []
    for h in range(qw // HD):
        q = qkv[:, h * HD : (h + 1) * HD]
        rot_q = rope_forward(q * head_inv(q) * gq[...], c2, s2).astype(BF16)
        scores = dot_nt(rot_q, rot_k) * (1.0 / math.sqrt(HD))
        e = jnp.where(allowed, jnp.exp(scores), 0.0)
        total = jnp.sum(e, axis=-1, keepdims=True)
        probs = (e / total).astype(BF16)
        parts.append(dot_nn(probs, v).astype(BF16))
    attn = jnp.concatenate(parts, axis=1)
    attn_out[0] = attn
    hb = n0.shape[1]
    out_own = dot_nn(attn, wo[0]).astype(BF16)
    p0[0, :, own] = out_own[:hb]
    p1[0, :, own] = out_own[hb:]
    out_other = dot_nn(attn, ro[...]).astype(BF16)
    p0[0, :, other] = out_other[:hb]
    p1[0, :, other] = out_other[hb:]


def mlp_fwd_kernel(row_ref, n0, n1, wg, wu, rgu, wd, rd, p0, p1, gu_out, h_out):
    half = wg.shape[1]
    ff = wg.shape[2]
    own, other = feature_cols(row_ref, half)
    xo = both_halves(n0, n1, own)
    xt = both_halves(n0, n1, other)
    w_own = jnp.concatenate([wg[0], wu[0]], axis=1)
    gu = dot_nn(xo, w_own) + dot_nn(xt, rgu[...])
    gu_out[0] = gu
    gate = gu[:, :ff]
    hidden = (gate * jax.nn.sigmoid(gate) * gu[:, ff:]).astype(BF16)
    h_out[0] = hidden
    hb = n0.shape[1]
    out_own = dot_nn(hidden, wd[0]).astype(BF16)
    p0[0, :, own] = out_own[:hb]
    p1[0, :, own] = out_own[hb:]
    out_other = dot_nn(hidden, rd[...]).astype(BF16)
    p0[0, :, other] = out_other[:hb]
    p1[0, :, other] = out_other[hb:]


def mlp_bwd_kernel(row_ref, d0, d1, gu_in, wg, wu, rgu, wd, rd, p0, p1, dgu_out):
    half = wg.shape[1]
    ff = wg.shape[2]
    own, other = feature_cols(row_ref, half)
    do = both_halves(d0, d1, own)
    dt = both_halves(d0, d1, other)
    d_hidden = dot_nt(do, wd[0]) + dot_nt(dt, rd[...])
    gate = gu_in[0, :, :ff]
    up = gu_in[0, :, ff:]
    sig = jax.nn.sigmoid(gate)
    d_gate = (d_hidden * up * sig * (1.0 + gate * (1.0 - sig))).astype(BF16)
    d_up = (d_hidden * gate * sig).astype(BF16)
    dgu = jnp.concatenate([d_gate, d_up], axis=1)
    dgu_out[0] = dgu
    hb = d0.shape[1]
    w_own = jnp.concatenate([wg[0], wu[0]], axis=1)
    out_own = dot_nt(dgu, w_own).astype(BF16)
    p0[0, :, own] = out_own[:hb]
    p1[0, :, own] = out_own[hb:]
    out_other = dot_nt(dgu, rgu[...]).astype(BF16)
    p0[0, :, other] = out_other[:hb]
    p1[0, :, other] = out_other[hb:]


def attn_bwd_kernel(
    row_ref, d0, d1, qk_in, v_in, attn_in, wq, wk, wv, rq, wo, ro, gq, gk, cos2, sin2, mask,
    p0, p1, dqkv_out, gain_out,
):
    half = wq.shape[1]
    qw = wq.shape[2]
    scale = 1.0 / math.sqrt(HD)
    own, other = feature_cols(row_ref, half)
    do = both_halves(d0, d1, own)
    dt = both_halves(d0, d1, other)
    d_attn = (dot_nt(do, wo[0]) + dot_nt(dt, ro[...])).astype(BF16)
    c2 = cos2[0]
    s2 = sin2[0]
    v = v_in[0]
    k = qk_in[0, :, qw : qw + HD]
    inv_k = head_inv(k)
    rot_k = rope_forward(k * inv_k * gk[...], c2, s2).astype(BF16)
    allowed = mask[0] > 0
    d_v = None
    d_rk = None
    gain_q = None
    outs = []
    for h in range(qw // HD):
        cols = slice(h * HD, (h + 1) * HD)
        q = qk_in[0, :, cols]
        inv_q = head_inv(q)
        rot_q = rope_forward(q * inv_q * gq[...], c2, s2).astype(BF16)
        scores = dot_nt(rot_q, rot_k) * scale
        e = jnp.where(allowed, jnp.exp(scores), 0.0)
        p_full = e / jnp.sum(e, axis=-1, keepdims=True)
        da = d_attn[:, cols]
        delta = jnp.sum(
            da.astype(F32) * attn_in[0, :, cols].astype(F32), axis=-1, keepdims=True
        )
        d_probs = dot_nt(da, v)
        d_scores = (p_full * (d_probs - delta)).astype(BF16)
        dv_h = dot_tn(p_full.astype(BF16), da)
        drk_h = dot_tn(d_scores, rot_q) * scale
        d_v = dv_h if d_v is None else d_v + dv_h
        d_rk = drk_h if d_rk is None else d_rk + drk_h
        d_nq = rope_backward(dot_nn(d_scores, rot_k) * scale, c2, s2)
        gsum = jnp.sum(d_nq * q * inv_q, axis=0, keepdims=True)
        gain_q = gsum if gain_q is None else gain_q + gsum
        n = d_nq * gq[...]
        proj = jnp.mean(n * q, axis=-1, keepdims=True)
        outs.append((inv_q * n - q * (inv_q * inv_q * inv_q * proj)).astype(BF16))
    d_nk = rope_backward(d_rk, c2, s2)
    gain_k = jnp.sum(d_nk * k * inv_k, axis=0, keepdims=True)
    n = d_nk * gk[...]
    proj = jnp.mean(n * k, axis=-1, keepdims=True)
    outs.append((inv_k * n - k * (inv_k * inv_k * inv_k * proj)).astype(BF16))
    outs.append(d_v.astype(BF16))
    gain_out[0] = jnp.concatenate([gain_q, gain_k], axis=1)
    dqkv = jnp.concatenate(outs, axis=1)
    dqkv_out[0] = dqkv
    hb = d0.shape[1]
    w_own = jnp.concatenate([wq[0], wk[0], wv[0]], axis=1)
    out_own = dot_nt(dqkv, w_own).astype(BF16)
    p0[0, :, own] = out_own[:hb]
    p1[0, :, own] = out_own[hb:]
    out_other = dot_nt(dqkv, rq[...]).astype(BF16)
    p0[0, :, other] = out_other[:hb]
    p1[0, :, other] = out_other[hb:]


def token_rows(ref0, ref1, cols):
    pieces = []
    for s in range(ref0.shape[0]):
        pieces.append(ref0[s, :, cols])
        pieces.append(ref1[s, :, cols])
    return jnp.concatenate(pieces, axis=0)


def flat_rows(ref):
    return jnp.concatenate([ref[s] for s in range(ref.shape[0])], axis=0)


def mlp_wgrad_kernel(row_ref, n0, n1, d0, d1, dgu, h_own, h_rcv, out):
    n_dp = out.shape[0]
    half = n0.shape[2] // 2
    kb = half // n_dp
    own, other = feature_cols(row_ref, half)
    r = row_ref[0]
    dy = flat_rows(dgu)
    for slot, cols in ((0, own), (1, other)):
        g = dot_tn(token_rows(n0, n1, cols), dy).astype(BF16)
        for d in range(n_dp):
            out[d, slot * kb : (slot + 1) * kb, :] = g[d * kb : (d + 1) * kb]
    dcols = token_rows(d0, d1, own)
    width = out.shape[2]
    per = n_dp // 2
    for who, href in ((r, h_own), (1 - r, h_rcv)):
        g = dot_tn(flat_rows(href), dcols).astype(BF16)
        ub = g.shape[0] // per
        top = kb
        rest = width - half
        low = ub - top
        for j in range(per):
            blk = g[j * ub : (j + 1) * ub]
            d = who * per + j
            out[d, 2 * kb : 2 * kb + top, :half] = blk[:top]
            for m in range(half // rest):
                out[d, 2 * kb + m * low : 2 * kb + (m + 1) * low, half:] = blk[
                    top:, m * rest : (m + 1) * rest
                ]


def attn_wgrad_kernel(row_ref, n0, n1, d0, d1, dqkv, a_own, a_rcv, out):
    n_dp = out.shape[0]
    half = n0.shape[2] // 2
    kb = half // n_dp
    own, other = feature_cols(row_ref, half)
    r = row_ref[0]
    dy = flat_rows(dqkv)
    for slot, cols in ((0, own), (1, other)):
        g = dot_tn(token_rows(n0, n1, cols), dy).astype(BF16)
        for d in range(n_dp):
            out[d, slot * kb : (slot + 1) * kb, :] = g[d * kb : (d + 1) * kb]
    dcols = token_rows(d0, d1, own)
    per = n_dp // 2
    for who, aref in ((r, a_own), (1 - r, a_rcv)):
        g = dot_tn(flat_rows(aref), dcols).astype(BF16)
        ub = g.shape[0] // per
        for j in range(per):
            out[who * per + j, 2 * kb : 2 * kb + ub, :] = g[j * ub : (j + 1) * ub]


def norm_fwd_kernel(row_ref, x, t, gain, y_out, n_out):
    y = x[...]
    for i in range(t.shape[0]):
        y = y + t[i].astype(F32)
    y_out[...] = y
    inv = lax.rsqrt(jnp.mean(y * y, axis=-1, keepdims=True) + EPS)
    n_out[...] = (y * inv * gain[...]).astype(BF16)


def add_kernel(row_ref, x, t, y_out):
    y = x[...]
    for i in range(t.shape[0]):
        y = y + t[i].astype(F32)
    y_out[...] = y


def norm_bwd_kernel(row_ref, t, resid, d_res, gain, d_out, d_round, gain_out):
    dn = t[0].astype(F32)
    for i in range(1, t.shape[0]):
        dn = dn + t[i].astype(F32)
    x = resid[...]
    inv = lax.rsqrt(jnp.mean(x * x, axis=-1, keepdims=True) + EPS)
    gain_out[...] = jnp.sum(dn * x * inv, axis=0, keepdims=True)
    m = dn * gain[...]
    proj = jnp.mean(m * x, axis=-1, keepdims=True)
    d = d_res[...] + inv * m - x * (inv * inv * inv * proj)
    d_out[...] = d
    d_round[...] = d.astype(BF16)


def make_body(n_dp, n_row, n_col):
    pair = [(c, c ^ 1) for c in range(n_col)]
    swap = [(i, 1 - i) for i in range(n_row)]
    groups = [
        [c * n_row + i for c in range(k, n_col, 2) for i in range(n_row)] for k in range(2)
    ]
    plane = ("col", "row")

    def gather_same(v):
        return lax.all_gather(v, plane, axis=0, tiled=False, axis_index_groups=groups)

    def other_core(v):
        return lax.ppermute(v, "col", pair)

    def other_row(v):
        return lax.ppermute(v, "row", swap)

    def gather(v):
        own = gather_same(v).reshape(n_col // 2, n_row * v.shape[0], v.shape[1])
        return own, other_core(own)

    def scatter(p0, p1):
        got = other_core(p1)
        both = (p0.astype(F32) + got.astype(F32)).astype(BF16)
        blocks = (n_col // 2) * n_row
        both = both.reshape(blocks * (both.shape[0] * both.shape[1] // blocks), both.shape[2])
        moved = lax.all_to_all(both, plane, 0, 0, tiled=True, axis_index_groups=groups)
        return moved.reshape(blocks, -1, both.shape[1])

    def body(
        inputs, positions, segments, cotangent, w_query, w_key, w_value, w_output,
        w_gate, w_up, w_down, attn_gain, mlp_gain, query_gain, key_gain,
    ):
        layers = w_query.shape[0]
        half = inputs.shape[1]
        width = half * n_row
        tok_c = inputs.shape[0]
        tok = tok_c // n_row
        n_seq = n_col // 2
        r = lax.axis_index("row")
        c = lax.axis_index("col")
        core = c % 2
        seq_id = c // 2
        row = jnp.reshape(r, (1,)).astype(jnp.int32)
        qw = w_query.shape[2] // n_row
        kw = w_key.shape[2] // n_row
        ow = w_output.shape[1] // n_row
        ff = w_gate.shape[2] // n_row

        ps = jnp.concatenate([positions, segments], axis=0)
        ps_other = other_row(ps)
        ps_all = jnp.stack([jnp.where(r == 0, ps, ps_other), jnp.where(r == 0, ps_other, ps)])

        def cut(w, axis, size, start):
            return lax.dynamic_slice_in_dim(w, start * size, size, axis)

        away = 1 - r
        rcv = []
        for l in range(layers):
            rq = other_row(
                jnp.concatenate(
                    [
                        cut(w_query[l], 1, qw, away),
                        cut(w_key[l], 1, kw, away),
                        cut(w_value[l], 1, kw, away),
                    ],
                    axis=1,
                )
            )
            ro = other_row(cut(w_output[l], 0, ow, away))
            rgu = other_row(
                jnp.concatenate([cut(w_gate[l], 1, ff, away), cut(w_up[l], 1, ff, away)], axis=1)
            )
            rd = other_row(cut(w_down[l], 0, ff, away))
            rcv.append((rq, ro, rgu, rd))

        raw0 = gather_same(inputs).reshape(n_seq, n_row, tok_c, half)
        raw1 = other_core(raw0)
        cot_all = lax.all_gather(cotangent, plane, axis=0, tiled=False).reshape(
            n_seq, 2, n_row, tok_c, half
        )

        order = jnp.concatenate(
            [jnp.arange(tok_c) + core * tok_c, jnp.arange(tok_c) + (1 - core) * tok_c]
        )
        turned = jnp.where(core == 0, ps_all, jnp.roll(ps_all, tok_c, axis=2))
        freq = THETA ** (-2.0 * jnp.arange(HD // 2, dtype=F32) / HD)
        angles = turned[:, 0, :].astype(F32)[:, :, None] * freq[None, None, :]
        cos = jnp.cos(angles)
        sin = jnp.sin(angles)
        cos2 = jnp.concatenate([cos, cos], axis=-1)
        sin2 = jnp.concatenate([-sin, sin], axis=-1)
        seg = turned[:, 1, :]
        mask = (
            (seg[:, :, None] == seg[:, None, :]) & (order[None, None, :] <= order[None, :, None])
        ).astype(F32)

        gq = query_gain[:, None, :]
        gk = key_gain[:, None, :]
        ga = attn_gain[:, None, :]
        gm = mlp_gain[:, None, :]

        full = (n_seq, tok_c, width)
        nt = n_seq * SEQ
        wq_spec = lambda l: pl.BlockSpec((1, half, qw), lambda i, s: (l, 0, s[0]))
        wk_spec = lambda l: pl.BlockSpec((1, half, kw), lambda i, s: (l, 0, s[0]))
        wo_spec = lambda l: pl.BlockSpec((1, ow, half), lambda i, s: (l, s[0], 0))
        wg_spec = lambda l: pl.BlockSpec((1, half, ff), lambda i, s: (l, 0, s[0]))
        wd_spec = lambda l: pl.BlockSpec((1, ff, half), lambda i, s: (l, s[0], 0))
        q3 = qw + 2 * kw
        tables = [per_seq((n_seq, SEQ, HD)), per_seq((n_seq, SEQ, HD)), per_seq((n_seq, SEQ, SEQ))]

        def qkv_specs(l):
            return [
                wq_spec(l), wk_spec(l), wk_spec(l), whole((half, q3)),
                wo_spec(l), whole((ow, half)), whole((1, HD)), whole((1, HD)),
            ] + tables

        def qkv_args(l):
            return [
                w_query, w_key, w_value, rcv[l][0], w_output, rcv[l][1], gq[l], gk[l],
                cos2, sin2, mask,
            ]

        def mlp_specs(l):
            return [wg_spec(l), wg_spec(l), whole((half, 2 * ff)), wd_spec(l), whole((ff, half))]

        def mlp_args(l):
            return [w_gate, w_up, rcv[l][2], w_down, rcv[l][3]]

        def attn_fwd(l, n0, n1):
            return call(
                attn_fwd_kernel, (n_seq,),
                [per_seq(full), per_seq(full)] + qkv_specs(l),
                [per_seq(full), per_seq(full), per_seq((n_seq, SEQ, qw + kw)),
                 per_seq((n_seq, SEQ, kw)), per_seq((n_seq, SEQ, qw))],
                [sds(full, BF16), sds(full, BF16), sds((n_seq, SEQ, qw + kw), F32),
                 sds((n_seq, SEQ, kw), BF16), sds((n_seq, SEQ, qw), BF16)],
                2 * nt * width * (q3 + qw), 6e6, row, [n0, n1] + qkv_args(l),
            )

        def mlp_fwd(l, n0, n1):
            return call(
                mlp_fwd_kernel, (n_seq,),
                [per_seq(full), per_seq(full)] + mlp_specs(l),
                [per_seq(full), per_seq(full), per_seq((n_seq, SEQ, 2 * ff)),
                 per_seq((n_seq, SEQ, ff))],
                [sds(full, BF16), sds(full, BF16), sds((n_seq, SEQ, 2 * ff), F32),
                 sds((n_seq, SEQ, ff), BF16)],
                6 * nt * width * ff, 8e6, row, [n0, n1] + mlp_args(l),
            )

        def mlp_bwd(l, d0, d1, gu):
            return call(
                mlp_bwd_kernel, (n_seq,),
                [per_seq(full), per_seq(full), per_seq((n_seq, SEQ, 2 * ff))] + mlp_specs(l),
                [per_seq(full), per_seq(full), per_seq((n_seq, SEQ, 2 * ff))],
                [sds(full, BF16), sds(full, BF16), sds((n_seq, SEQ, 2 * ff), BF16)],
                6 * nt * width * ff, 8e6, row, [d0, d1, gu] + mlp_args(l),
            )

        def attn_bwd(l, d0, d1, qk, v, attn):
            return call(
                attn_bwd_kernel, (n_seq,),
                [per_seq(full), per_seq(full), per_seq((n_seq, SEQ, qw + kw)),
                 per_seq((n_seq, SEQ, kw)), per_seq((n_seq, SEQ, qw))] + qkv_specs(l),
                [per_seq(full), per_seq(full), per_seq((n_seq, SEQ, q3)),
                 per_seq((n_seq, 1, 2 * HD))],
                [sds(full, BF16), sds(full, BF16), sds((n_seq, SEQ, q3), BF16),
                 sds((n_seq, 1, 2 * HD), F32)],
                2 * nt * width * (q3 + qw), 8e6, row, [d0, d1, qk, v, attn] + qkv_args(l),
            )

        def wgrad(kernel, n0, n1, d0, d1, dy, own, got, rows, cols):
            args = [n0, n1, d0, d1, dy, own, got]
            return call(
                kernel, (1,), [whole(a.shape) for a in args],
                whole((n_dp, rows, cols)), sds((n_dp, rows, cols), BF16),
                2 * nt * n_dp * rows * cols, 8e6, row, args,
            )

        def norm_fwd(x, t, gain):
            return call(
                norm_fwd_kernel, (1,), [whole(x.shape), whole(t.shape), whole(gain.shape)],
                [whole(x.shape), whole(x.shape)], [sds(x.shape, F32), sds(x.shape, BF16)],
                1e5, 1e6, row, [x, t, gain],
            )

        def norm_bwd(t, resid, d_res, gain):
            return call(
                norm_bwd_kernel, (1,),
                [whole(t.shape), whole(resid.shape), whole(d_res.shape), whole(gain.shape)],
                [whole(resid.shape), whole(resid.shape), whole(gain.shape)],
                [sds(resid.shape, F32), sds(resid.shape, BF16), sds(gain.shape, F32)],
                1e5, 1e6, row, [t, resid, d_res, gain],
            )

        def own_tokens(blocks):
            mine = lax.dynamic_slice_in_dim(blocks, r * tok, tok, 1)
            return jnp.concatenate([mine[i] for i in range(n_row)], axis=-1).astype(F32)

        x = own_tokens(lax.dynamic_index_in_dim(raw0, seq_id, 0, keepdims=False))
        raw_block = (n_seq, n_row, tok_c, half)
        normed = call(
            norm_first_kernel, (n_seq,), [per_seq(raw_block), per_seq(raw_block), whole((1, width))],
            [per_seq(full), per_seq(full)], [sds(full, BF16), sds(full, BF16)],
            1e6, 4e6, row, [raw0, raw1, ga[0]],
        )

        saved = []
        for l in range(layers):
            n1_own, n1_oth = normed
            p0, p1, qk, v, attn = attn_fwd(l, n1_own, n1_oth)
            middle, n2 = norm_fwd(x, scatter(p0, p1), gm[l])
            n2_own, n2_oth = gather(n2)
            p0, p1, gu, hidden = mlp_fwd(l, n2_own, n2_oth)
            moved = scatter(p0, p1)
            saved.append((x, n1_own, n1_oth, qk, v, attn, middle, n2_own, n2_oth, gu, hidden))
            if l + 1 < layers:
                x, nxt = norm_fwd(x=middle, t=moved, gain=ga[l + 1])
                normed = gather(nxt)
            else:
                x = call(
                    add_kernel, (1,), [whole(middle.shape), whole(moved.shape)],
                    whole(middle.shape), sds(middle.shape, F32), 1e5, 1e6, row, [middle, moved],
                )

        def to_block(v):
            v = v.astype(F32)
            halves = [v[:, i * half : (i + 1) * half] for i in range(n_row)]
            mine = jnp.where(r == 0, halves[0], halves[1])
            got = other_row(jnp.where(r == 0, halves[1], halves[0]))
            return jnp.where(
                r == 0, jnp.concatenate([mine, got], 0), jnp.concatenate([got, mine], 0)
            )

        outputs = to_block(x)

        def pick_half(k):
            blk = lax.dynamic_index_in_dim(cot_all, k, 1, keepdims=False)
            return blk.transpose(0, 2, 1, 3).reshape(full)

        d0, d1 = pick_half(core), pick_half(1 - core)
        d_own = own_tokens(
            lax.dynamic_index_in_dim(
                lax.dynamic_index_in_dim(cot_all, seq_id, 0, keepdims=False), core, 0, keepdims=False
            )
        )
        kb = half // n_dp
        mlp_red = [None] * layers
        attn_red = [None] * layers
        g_attn = [None] * layers
        g_mlp = [None] * layers
        g_head = [None] * layers
        for l in reversed(range(layers)):
            xin, n1_own, n1_oth, qk, v, attn, middle, n2_own, n2_oth, gu, hidden = saved[l]
            p0, p1, dgu = mlp_bwd(l, d0, d1, gu)
            h_got = other_row(hidden)
            a_got = other_row(attn)
            wg_part = wgrad(
                mlp_wgrad_kernel, n2_own, n2_oth, d0, d1, dgu, hidden, h_got, 3 * kb, 2 * ff
            )
            mlp_red[l] = lax.psum_scatter(wg_part, "dp", scatter_dimension=0, tiled=False)
            d_mid, d_mid_round, g_mlp[l] = norm_bwd(scatter(p0, p1), middle, d_own, gm[l])
            d0, d1 = gather(d_mid_round)
            p0, p1, dqkv, g_head[l] = attn_bwd(l, d0, d1, qk, v, attn)
            wg_part = wgrad(attn_wgrad_kernel, n1_own, n1_oth, d0, d1, dqkv, attn, a_got, 3 * kb, q3)
            attn_red[l] = lax.psum_scatter(wg_part, "dp", scatter_dimension=0, tiled=False)
            d_own, d_round, g_attn[l] = norm_bwd(scatter(p0, p1), xin, d_mid, ga[l])
            if l > 0:
                d0, d1 = gather(d_round)
        d_inputs = to_block(d_own)

        gains = jnp.concatenate(
            [g.reshape(-1) for g in g_attn]
            + [g.reshape(-1) for g in g_mlp]
            + [jnp.sum(g, axis=0).reshape(-1) for g in g_head]
        )
        gains = lax.psum(gains.reshape(-1, HD), ("dp", "row", "col")).reshape(-1)
        lw = layers * width
        ga_out = gains[:lw].reshape(layers, width)
        gm_out = gains[lw : 2 * lw].reshape(layers, width)
        gh = gains[2 * lw :].reshape(layers, 2, HD)

        def join(own, got):
            return jnp.where(
                r == 0, jnp.concatenate([own, got], -1), jnp.concatenate([got, own], -1)
            ).astype(F32)

        grads = [[] for _ in range(7)]
        for l in range(layers):
            z = attn_red[l]
            got = other_row(z[kb : 2 * kb])
            mine = z[:kb]
            for k, (lo, hi) in enumerate(((0, qw), (qw, qw + kw), (qw + kw, q3))):
                grads[k].append(join(mine[:, lo:hi], got[:, lo:hi]))
            grads[3].append(z[2 * kb :].astype(F32))
            z = mlp_red[l]
            got = other_row(z[kb : 2 * kb])
            mine = z[:kb]
            for k, (lo, hi) in enumerate(((0, ff), (ff, 2 * ff))):
                grads[4 + k].append(join(mine[:, lo:hi], got[:, lo:hi]))
            low = z[2 * kb :]
            rest = 2 * ff - half
            parts = half // rest
            lowrows = kb // parts
            tail = jnp.concatenate(
                [low[m * lowrows : (m + 1) * lowrows, half:] for m in range(parts)], axis=1
            )
            grads[6].append(jnp.concatenate([low[:, :half], tail], axis=0).astype(F32))
        stacked = [jnp.stack(g) for g in grads]
        return (
            outputs, d_inputs, *stacked, ga_out, gm_out, gh[:, 0], gh[:, 1],
        )

    return body


def solution(mesh):
    body = make_body(mesh.shape["dp"], mesh.shape["row"], mesh.shape["col"])
    act = P(("dp", "col"), "row")
    seq = P(("dp", "row"), None)
    w_in = P(None, "row", "col")
    w_out = P(None, "col", "row")
    g_in = P(None, ("row", "dp"), "col")
    g_out = P(None, ("col", "dp"), "row")
    return jax.shard_map(
        body,
        mesh=mesh,
        in_specs=(
            act, seq, seq, act, w_in, w_in, w_in, w_out, w_in, w_in, w_out, P(), P(), P(), P(),
        ),
        out_specs=(
            act, act, g_in, g_in, g_in, g_out, g_in, g_in, g_out, P(), P(), P(), P(),
        ),
        check_vma=False,
    )
```

```python
import functools
import math

import jax
import jax.numpy as jnp
from jax import lax
from jax.experimental import pallas as pl
from jax.experimental.pallas import tpu as pltpu
from jax.sharding import PartitionSpec as P

HD = 128
SEQ = 256
EPS = 1e-06
THETA = 1000000.0
F32 = jnp.float32
BF16 = jnp.bfloat16


def dot_nn(a, b):
    return jnp.dot(a, b, preferred_element_type=F32)


def dot_nt(a, b):
    return lax.dot_general(a, b, (((1,), (1,)), ((), ())), preferred_element_type=F32)


def dot_tn(a, b):
    return lax.dot_general(a, b, (((0,), (0,)), ((), ())), preferred_element_type=F32)


def whole(shape):
    rank = len(shape)
    return pl.BlockSpec(tuple(shape), lambda *_: (0,) * rank)


def per_seq(shape):
    rest = len(shape) - 1
    return pl.BlockSpec((1,) + tuple(shape[1:]), lambda i, *_: (i,) + (0,) * rest)


def sds(shape, dtype):
    return jax.ShapeDtypeStruct(tuple(shape), dtype)


def call(kernel, grid, in_specs, out_specs, out_shape, flops, nbytes, row, args, scratch=()):
    return pl.pallas_call(
        kernel,
        grid_spec=pltpu.PrefetchScalarGridSpec(
            num_scalar_prefetch=1,
            grid=grid,
            in_specs=in_specs,
            out_specs=out_specs,
            scratch_shapes=list(scratch),
        ),
        out_shape=out_shape,
        cost_estimate=pl.CostEstimate(
            flops=int(flops), bytes_accessed=int(nbytes), transcendentals=0
        ),
    )(row, *args)


def both_halves(ref0, ref1, cols):
    return jnp.concatenate([ref0[0, :, cols], ref1[0, :, cols]], axis=0)


def rope_forward(v, cos2, sin2):
    return v * cos2 + pltpu.roll(v, v.shape[-1] // 2, 1) * sin2


def rope_backward(v, cos2, sin2):
    return v * cos2 - pltpu.roll(v, v.shape[-1] // 2, 1) * sin2


def head_inv(v):
    return lax.rsqrt(jnp.mean(v * v, axis=-1, keepdims=True) + EPS)


def feature_cols(row_ref, width):
    r = row_ref[0]
    own = pl.ds(pl.multiple_of(r * width, width), width)
    other = pl.ds(pl.multiple_of((1 - r) * width, width), width)
    return own, other


def got_attn(pk, qr, orows, at):
    n = pk.shape[0]
    w = 4 * HD
    rq = jnp.concatenate([pk[d, at : at + qr, :w] for d in range(n)], axis=0)
    ro = jnp.concatenate([pk[d, at + qr : at + qr + orows, :w] for d in range(n)], axis=0)
    return rq, ro


def got_mlp(pk, gr, dr, extra):
    n = pk.shape[0]
    half = 2 * pk.shape[2] // 3
    rgu = jnp.concatenate([pk[d, :gr, :] for d in range(n)], axis=0)
    rows = extra + dr
    low = rows // 3
    top = rows - low
    parts = []
    for d in range(n):
        if top > extra:
            parts.append(pk[d, gr + extra : gr + top, :half])
        parts.append(
            jnp.concatenate(
                [pk[d, gr : gr + low, half:], pk[d, gr + low : gr + 2 * low, half:]], axis=1
            )
        )
    return rgu, jnp.concatenate(parts, axis=0)


def norm_first_kernel(row_ref, a0, a1, gain, n0, n1):
    for src, dst in ((a0, n0), (a1, n1)):
        v = jnp.concatenate([src[0, 0], src[0, 1]], axis=-1).astype(F32)
        inv = lax.rsqrt(jnp.mean(v * v, axis=-1, keepdims=True) + EPS)
        dst[0] = (v * inv * gain[...]).astype(BF16)


def attn_fwd_kernel(
    pack, row_ref, n0, n1, wq, wk, wv, wo, pk, gq, gk, cos2, sin2, mask, p0, p1, qk_out, v_out, attn_out
):
    half = wq.shape[1]
    own, other = feature_cols(row_ref, half)
    qw = wq.shape[2]
    rq, ro = got_attn(pk, *pack)
    xo = both_halves(n0, n1, own)
    xt = both_halves(n0, n1, other)
    w_own = jnp.concatenate([wq[0], wk[0], wv[0]], axis=1)
    qkv = dot_nn(xo, w_own) + dot_nn(xt, rq)
    qk_out[0] = qkv[:, : qw + HD]
    v = qkv[:, qw + HD :].astype(BF16)
    v_out[0] = v
    c2 = cos2[0]
    s2 = sin2[0]
    k = qkv[:, qw : qw + HD]
    rot_k = rope_forward(k * head_inv(k) * gk[...], c2, s2).astype(BF16)
    allowed = mask[0] > 0
    parts = []
    for h in range(qw // HD):
        q = qkv[:, h * HD : (h + 1) * HD]
        rot_q = rope_forward(q * head_inv(q) * gq[...], c2, s2).astype(BF16)
        scores = dot_nt(rot_q, rot_k) * (1.0 / math.sqrt(HD))
        e = jnp.where(allowed, jnp.exp(scores), 0.0)
        total = jnp.sum(e, axis=-1, keepdims=True)
        probs = (e / total).astype(BF16)
        parts.append(dot_nn(probs, v).astype(BF16))
    attn = jnp.concatenate(parts, axis=1)
    attn_out[0] = attn
    hb = n0.shape[1]
    out_own = dot_nn(attn, wo[0]).astype(BF16)
    p0[0, :, own] = out_own[:hb]
    p1[0, :, own] = out_own[hb:]
    out_other = dot_nn(attn, ro).astype(BF16)
    p0[0, :, other] = out_other[:hb]
    p1[0, :, other] = out_other[hb:]


def mlp_fwd_kernel(pack, row_ref, n0, n1, wg, wu, wd, pk, p0, p1, gu_out, h_out):
    half = wg.shape[1]
    ff = wg.shape[2]
    own, other = feature_cols(row_ref, half)
    rgu, rd = got_mlp(pk, *pack)
    xo = both_halves(n0, n1, own)
    xt = both_halves(n0, n1, other)
    w_own = jnp.concatenate([wg[0], wu[0]], axis=1)
    gu = dot_nn(xo, w_own) + dot_nn(xt, rgu)
    gu_out[0] = gu
    gate = gu[:, :ff]
    hidden = (gate * jax.nn.sigmoid(gate) * gu[:, ff:]).astype(BF16)
    h_out[0] = hidden
    hb = n0.shape[1]
    out_own = dot_nn(hidden, wd[0]).astype(BF16)
    p0[0, :, own] = out_own[:hb]
    p1[0, :, own] = out_own[hb:]
    out_other = dot_nn(hidden, rd).astype(BF16)
    p0[0, :, other] = out_other[:hb]
    p1[0, :, other] = out_other[hb:]


def mlp_bwd_kernel(pack, row_ref, d0, d1, gu_in, wg, wu, wd, pk, p0, p1, dgu_out):
    half = wg.shape[1]
    ff = wg.shape[2]
    own, other = feature_cols(row_ref, half)
    rgu, rd = got_mlp(pk, *pack)
    do = both_halves(d0, d1, own)
    dt = both_halves(d0, d1, other)
    d_hidden = dot_nt(do, wd[0]) + dot_nt(dt, rd)
    gate = gu_in[0, :, :ff]
    up = gu_in[0, :, ff:]
    sig = jax.nn.sigmoid(gate)
    d_gate = (d_hidden * up * sig * (1.0 + gate * (1.0 - sig))).astype(BF16)
    d_up = (d_hidden * gate * sig).astype(BF16)
    dgu = jnp.concatenate([d_gate, d_up], axis=1)
    dgu_out[0] = dgu
    hb = d0.shape[1]
    w_own = jnp.concatenate([wg[0], wu[0]], axis=1)
    out_own = dot_nt(dgu, w_own).astype(BF16)
    p0[0, :, own] = out_own[:hb]
    p1[0, :, own] = out_own[hb:]
    out_other = dot_nt(dgu, rgu).astype(BF16)
    p0[0, :, other] = out_other[:hb]
    p1[0, :, other] = out_other[hb:]


def attn_bwd_kernel(
    pack, row_ref, d0, d1, qk_in, v_in, attn_in, wq, wk, wv, wo, pk, gq, gk, cos2, sin2, mask,
    p0, p1, dqkv_out, gain_out,
):
    half = wq.shape[1]
    qw = wq.shape[2]
    scale = 1.0 / math.sqrt(HD)
    own, other = feature_cols(row_ref, half)
    rq, ro = got_attn(pk, *pack)
    do = both_halves(d0, d1, own)
    dt = both_halves(d0, d1, other)
    d_attn = (dot_nt(do, wo[0]) + dot_nt(dt, ro)).astype(BF16)
    c2 = cos2[0]
    s2 = sin2[0]
    v = v_in[0]
    k = qk_in[0, :, qw : qw + HD]
    inv_k = head_inv(k)
    rot_k = rope_forward(k * inv_k * gk[...], c2, s2).astype(BF16)
    allowed = mask[0] > 0
    d_v = None
    d_rk = None
    gain_q = None
    outs = []
    for h in range(qw // HD):
        cols = slice(h * HD, (h + 1) * HD)
        q = qk_in[0, :, cols]
        inv_q = head_inv(q)
        rot_q = rope_forward(q * inv_q * gq[...], c2, s2).astype(BF16)
        scores = dot_nt(rot_q, rot_k) * scale
        e = jnp.where(allowed, jnp.exp(scores), 0.0)
        p_full = e / jnp.sum(e, axis=-1, keepdims=True)
        da = d_attn[:, cols]
        delta = jnp.sum(
            da.astype(F32) * attn_in[0, :, cols].astype(F32), axis=-1, keepdims=True
        )
        d_probs = dot_nt(da, v)
        d_scores = (p_full * (d_probs - delta)).astype(BF16)
        dv_h = dot_tn(p_full.astype(BF16), da)
        drk_h = dot_tn(d_scores, rot_q) * scale
        d_v = dv_h if d_v is None else d_v + dv_h
        d_rk = drk_h if d_rk is None else d_rk + drk_h
        d_nq = rope_backward(dot_nn(d_scores, rot_k) * scale, c2, s2)
        gsum = jnp.sum(d_nq * q * inv_q, axis=0, keepdims=True)
        gain_q = gsum if gain_q is None else gain_q + gsum
        n = d_nq * gq[...]
        proj = jnp.mean(n * q, axis=-1, keepdims=True)
        outs.append((inv_q * n - q * (inv_q * inv_q * inv_q * proj)).astype(BF16))
    d_nk = rope_backward(d_rk, c2, s2)
    gain_k = jnp.sum(d_nk * k * inv_k, axis=0, keepdims=True)
    n = d_nk * gk[...]
    proj = jnp.mean(n * k, axis=-1, keepdims=True)
    outs.append((inv_k * n - k * (inv_k * inv_k * inv_k * proj)).astype(BF16))
    outs.append(d_v.astype(BF16))
    gain_out[0] = jnp.concatenate([gain_q, gain_k], axis=1)
    dqkv = jnp.concatenate(outs, axis=1)
    dqkv_out[0] = dqkv
    hb = d0.shape[1]
    w_own = jnp.concatenate([wq[0], wk[0], wv[0]], axis=1)
    out_own = dot_nt(dqkv, w_own).astype(BF16)
    p0[0, :, own] = out_own[:hb]
    p1[0, :, own] = out_own[hb:]
    out_other = dot_nt(dqkv, rq).astype(BF16)
    p0[0, :, other] = out_other[:hb]
    p1[0, :, other] = out_other[hb:]


def token_rows(ref0, ref1, cols):
    pieces = []
    for s in range(ref0.shape[0]):
        pieces.append(ref0[s, :, cols])
        pieces.append(ref1[s, :, cols])
    return jnp.concatenate(pieces, axis=0)


def flat_rows(ref):
    return jnp.concatenate([ref[s] for s in range(ref.shape[0])], axis=0)


def in_grads(row_ref, n0, n1, dy, out):
    n_dp = out.shape[0]
    half = n0.shape[2] // 2
    kb = half // n_dp
    for slot, cols in enumerate(feature_cols(row_ref, half)):
        g = dot_tn(token_rows(n0, n1, cols), dy).astype(BF16)
        for d in range(n_dp):
            out[d, slot * kb : (slot + 1) * kb, :] = g[d * kb : (d + 1) * kb]
    return 2 * kb


def out_grads(row_ref, d0, d1, own_ref, got_ref, out, at):
    per = out.shape[0] // 2
    r = row_ref[0]
    dcols = token_rows(d0, d1, feature_cols(row_ref, d0.shape[2] // 2)[0])
    for who, href in ((r, own_ref), (1 - r, got_ref)):
        g = dot_tn(flat_rows(href), dcols).astype(BF16)
        ub = g.shape[0] // per
        for j in range(per):
            out[who * per + j, at : at + ub, :] = g[j * ub : (j + 1) * ub]
    return at + ub


def wgrad_up_kernel(row_ref, n0, n1, dgu, out):
    in_grads(row_ref, n0, n1, flat_rows(dgu), out)


def wgrad_rest_kernel(row_ref, n0, n1, dqkv, m0, m1, a_own, a_rcv, d0, d1, h_own, h_rcv, out):
    at = in_grads(row_ref, n0, n1, flat_rows(dqkv), out)
    at = out_grads(row_ref, m0, m1, a_own, a_rcv, out, at)
    out_grads(row_ref, d0, d1, h_own, h_rcv, out, at)


def norm_fwd_kernel(row_ref, x, t, gain, y_out, n_out):
    y = x[...]
    for i in range(t.shape[0]):
        y = y + t[i].astype(F32)
    y_out[...] = y
    inv = lax.rsqrt(jnp.mean(y * y, axis=-1, keepdims=True) + EPS)
    n_out[...] = (y * inv * gain[...]).astype(BF16)


def add_kernel(row_ref, x, t, y_out):
    y = x[...]
    for i in range(t.shape[0]):
        y = y + t[i].astype(F32)
    y_out[...] = y


def norm_bwd_kernel(row_ref, t, resid, d_res, gain, d_out, d_round, gain_out):
    dn = t[0].astype(F32)
    for i in range(1, t.shape[0]):
        dn = dn + t[i].astype(F32)
    x = resid[...]
    inv = lax.rsqrt(jnp.mean(x * x, axis=-1, keepdims=True) + EPS)
    gain_out[...] = jnp.sum(dn * x * inv, axis=0, keepdims=True)
    m = dn * gain[...]
    proj = jnp.mean(m * x, axis=-1, keepdims=True)
    d = d_res[...] + inv * m - x * (inv * inv * inv * proj)
    d_out[...] = d
    d_round[...] = d.astype(BF16)


def make_body(n_dp, n_row, n_col):
    pair = [(c, c ^ 1) for c in range(n_col)]
    swap = [(i, 1 - i) for i in range(n_row)]
    groups = [
        [c * n_row + i for c in range(k, n_col, 2) for i in range(n_row)] for k in range(2)
    ]
    plane = ("col", "row")

    def gather_same(v):
        return lax.all_gather(v, plane, axis=0, tiled=False, axis_index_groups=groups)

    def other_core(v):
        return lax.ppermute(v, "col", pair)

    def other_row(v):
        return lax.ppermute(v, "row", swap)

    def gather(v):
        own = gather_same(v).reshape(n_col // 2, n_row * v.shape[0], v.shape[1])
        return own, other_core(own)

    def scatter(p0, p1, first=None):
        got = other_core(p1)
        both = (p0.astype(F32) + got.astype(F32)).astype(BF16)
        blocks = (n_col // 2) * n_row
        both = both.reshape(blocks * (both.shape[0] * both.shape[1] // blocks), both.shape[2])
        if first is not None:
            both, first = lax.optimization_barrier((both, first))
        moved = lax.all_to_all(both, plane, 0, 0, tiled=True, axis_index_groups=groups)
        moved = moved.reshape(blocks, -1, both.shape[1])
        return moved if first is None else (moved, first)

    def body(
        inputs, positions, segments, cotangent, w_query, w_key, w_value, w_output,
        w_gate, w_up, w_down, attn_gain, mlp_gain, query_gain, key_gain,
    ):
        layers = w_query.shape[0]
        half = inputs.shape[1]
        width = half * n_row
        tok_c = inputs.shape[0]
        tok = tok_c // n_row
        n_seq = n_col // 2
        r = lax.axis_index("row")
        c = lax.axis_index("col")
        core = c % 2
        seq_id = c // 2
        row = jnp.reshape(r, (1,)).astype(jnp.int32)
        qw = w_query.shape[2] // n_row
        kw = w_key.shape[2] // n_row
        ow = w_output.shape[1] // n_row
        ff = w_gate.shape[2] // n_row

        ps = jnp.concatenate([positions, segments], axis=0)
        ps_other = other_row(ps)
        ps_all = jnp.stack([jnp.where(r == 0, ps, ps_other), jnp.where(r == 0, ps_other, ps)])

        def cut(w, axis, size, start):
            return lax.dynamic_slice_in_dim(w, start * size, size, axis)

        away = 1 - r
        dpi = lax.axis_index("dp")

        def piece(v):
            rows = v.shape[0] // n_dp
            return lax.dynamic_slice_in_dim(v, dpi * rows, rows, 0)

        def send_qkv(l):
            return jnp.concatenate(
                [
                    cut(w_query[l], 1, qw, away),
                    cut(w_key[l], 1, kw, away),
                    cut(w_value[l], 1, kw, away),
                ],
                axis=1,
            )

        def send_o(l):
            return cut(w_output[l], 0, ow, away)

        def send_mlp(l, lead):
            gu = jnp.concatenate(
                [piece(cut(w_gate[l], 1, ff, away)), piece(cut(w_up[l], 1, ff, away))], axis=1
            )
            rest = jnp.concatenate(lead + [piece(cut(w_down[l], 0, ff, away))], axis=0)
            low = rest.shape[0] // 3
            top = rest.shape[0] - low
            w = half // 2
            side = jnp.concatenate([rest[top:, :w], rest[top:, w:]], axis=0)
            return jnp.concatenate([gu, jnp.concatenate([rest[:top], side], axis=1)], axis=0)

        with jax.named_scope("w_first"):
            pk_first = other_row(jnp.concatenate([send_qkv(0), send_o(0)], axis=0))[None]
        pk_attn, pk_mlp, attn_pack, mlp_pack = [pk_first], [], [(half, ow, 0)], []
        for l in range(layers):
            lead = [] if l == 0 else [piece(send_qkv(l)), piece(send_o(l))]
            got = other_row(send_mlp(l, lead))
            if l > 0:
                got, _ = lax.optimization_barrier((got, pk_mlp[-1]))
            pk = lax.all_gather(got, "dp", axis=0, tiled=False)
            pk_mlp.append(pk)
            mlp_pack.append(
                (half // n_dp, ff // n_dp, sum(v.shape[0] for v in lead))
            )
            if l > 0:
                pk_attn.append(pk)
                attn_pack.append((half // n_dp, ow // n_dp, half // n_dp))

        raw0 = gather_same(inputs).reshape(n_seq, n_row, tok_c, half)
        raw1 = other_core(raw0)
        cot_in, _ = lax.optimization_barrier((cotangent, pk_mlp[-1]))
        cot_all = lax.all_gather(cot_in, plane, axis=0, tiled=False).reshape(
            n_seq, 2, n_row, tok_c, half
        )

        order = jnp.concatenate(
            [jnp.arange(tok_c) + core * tok_c, jnp.arange(tok_c) + (1 - core) * tok_c]
        )
        turned = jnp.where(core == 0, ps_all, jnp.roll(ps_all, tok_c, axis=2))
        freq = THETA ** (-2.0 * jnp.arange(HD // 2, dtype=F32) / HD)
        angles = turned[:, 0, :].astype(F32)[:, :, None] * freq[None, None, :]
        cos = jnp.cos(angles)
        sin = jnp.sin(angles)
        cos2 = jnp.concatenate([cos, cos], axis=-1)
        sin2 = jnp.concatenate([-sin, sin], axis=-1)
        seg = turned[:, 1, :]
        mask = (
            (seg[:, :, None] == seg[:, None, :]) & (order[None, None, :] <= order[None, :, None])
        ).astype(F32)

        gq = query_gain[:, None, :]
        gk = key_gain[:, None, :]
        ga = attn_gain[:, None, :]
        gm = mlp_gain[:, None, :]

        full = (n_seq, tok_c, width)
        nt = n_seq * SEQ
        wq_spec = lambda l: pl.BlockSpec((1, half, qw), lambda i, s: (l, 0, s[0]))
        wk_spec = lambda l: pl.BlockSpec((1, half, kw), lambda i, s: (l, 0, s[0]))
        wo_spec = lambda l: pl.BlockSpec((1, ow, half), lambda i, s: (l, s[0], 0))
        wg_spec = lambda l: pl.BlockSpec((1, half, ff), lambda i, s: (l, 0, s[0]))
        wd_spec = lambda l: pl.BlockSpec((1, ff, half), lambda i, s: (l, s[0], 0))
        q3 = qw + 2 * kw
        tables = [per_seq((n_seq, SEQ, HD)), per_seq((n_seq, SEQ, HD)), per_seq((n_seq, SEQ, SEQ))]

        def qkv_specs(l):
            return [
                wq_spec(l), wk_spec(l), wk_spec(l), wo_spec(l), whole(pk_attn[l].shape),
                whole((1, HD)), whole((1, HD)),
            ] + tables

        def qkv_args(l):
            return [
                w_query, w_key, w_value, w_output, pk_attn[l], gq[l], gk[l],
                cos2, sin2, mask,
            ]

        def mlp_specs(l):
            return [wg_spec(l), wg_spec(l), wd_spec(l), whole(pk_mlp[l].shape)]

        def mlp_args(l):
            return [w_gate, w_up, w_down, pk_mlp[l]]

        def attn_fwd(l, n0, n1):
            return call(
                functools.partial(attn_fwd_kernel, attn_pack[l]), (n_seq,),
                [per_seq(full), per_seq(full)] + qkv_specs(l),
                [per_seq(full), per_seq(full), per_seq((n_seq, SEQ, qw + kw)),
                 per_seq((n_seq, SEQ, kw)), per_seq((n_seq, SEQ, qw))],
                [sds(full, BF16), sds(full, BF16), sds((n_seq, SEQ, qw + kw), F32),
                 sds((n_seq, SEQ, kw), BF16), sds((n_seq, SEQ, qw), BF16)],
                2 * nt * width * (q3 + qw), 6e6, row, [n0, n1] + qkv_args(l),
            )

        def mlp_fwd(l, n0, n1):
            return call(
                functools.partial(mlp_fwd_kernel, mlp_pack[l]), (n_seq,),
                [per_seq(full), per_seq(full)] + mlp_specs(l),
                [per_seq(full), per_seq(full), per_seq((n_seq, SEQ, 2 * ff)),
                 per_seq((n_seq, SEQ, ff))],
                [sds(full, BF16), sds(full, BF16), sds((n_seq, SEQ, 2 * ff), F32),
                 sds((n_seq, SEQ, ff), BF16)],
                6 * nt * width * ff, 8e6, row, [n0, n1] + mlp_args(l),
            )

        def mlp_bwd(l, d0, d1, gu):
            return call(
                functools.partial(mlp_bwd_kernel, mlp_pack[l]), (n_seq,),
                [per_seq(full), per_seq(full), per_seq((n_seq, SEQ, 2 * ff))] + mlp_specs(l),
                [per_seq(full), per_seq(full), per_seq((n_seq, SEQ, 2 * ff))],
                [sds(full, BF16), sds(full, BF16), sds((n_seq, SEQ, 2 * ff), BF16)],
                6 * nt * width * ff, 8e6, row, [d0, d1, gu] + mlp_args(l),
            )

        def attn_bwd(l, d0, d1, qk, v, attn):
            return call(
                functools.partial(attn_bwd_kernel, attn_pack[l]), (n_seq,),
                [per_seq(full), per_seq(full), per_seq((n_seq, SEQ, qw + kw)),
                 per_seq((n_seq, SEQ, kw)), per_seq((n_seq, SEQ, qw))] + qkv_specs(l),
                [per_seq(full), per_seq(full), per_seq((n_seq, SEQ, q3)),
                 per_seq((n_seq, 1, 2 * HD))],
                [sds(full, BF16), sds(full, BF16), sds((n_seq, SEQ, q3), BF16),
                 sds((n_seq, 1, 2 * HD), F32)],
                2 * nt * width * (q3 + qw), 8e6, row, [d0, d1, qk, v, attn] + qkv_args(l),
            )

        def wgrad(kernel, rows, cols, args):
            return call(
                kernel, (1,), [whole(a.shape) for a in args],
                whole((n_dp, rows, cols)), sds((n_dp, rows, cols), BF16),
                2 * nt * n_dp * rows * cols, 8e6, row, args,
            )

        def norm_fwd(x, t, gain):
            return call(
                norm_fwd_kernel, (1,), [whole(x.shape), whole(t.shape), whole(gain.shape)],
                [whole(x.shape), whole(x.shape)], [sds(x.shape, F32), sds(x.shape, BF16)],
                1e5, 1e6, row, [x, t, gain],
            )

        def norm_bwd(t, resid, d_res, gain):
            return call(
                norm_bwd_kernel, (1,),
                [whole(t.shape), whole(resid.shape), whole(d_res.shape), whole(gain.shape)],
                [whole(resid.shape), whole(resid.shape), whole(gain.shape)],
                [sds(resid.shape, F32), sds(resid.shape, BF16), sds(gain.shape, F32)],
                1e5, 1e6, row, [t, resid, d_res, gain],
            )

        def own_tokens(blocks):
            mine = lax.dynamic_slice_in_dim(blocks, r * tok, tok, 1)
            return jnp.concatenate([mine[i] for i in range(n_row)], axis=-1).astype(F32)

        x = own_tokens(lax.dynamic_index_in_dim(raw0, seq_id, 0, keepdims=False))
        raw_block = (n_seq, n_row, tok_c, half)
        normed = call(
            norm_first_kernel, (n_seq,), [per_seq(raw_block), per_seq(raw_block), whole((1, width))],
            [per_seq(full), per_seq(full)], [sds(full, BF16), sds(full, BF16)],
            1e6, 4e6, row, [raw0, raw1, ga[0]],
        )

        saved = []
        for l in range(layers):
            n1_own, n1_oth = normed
            p0, p1, qk, v, attn = attn_fwd(l, n1_own, n1_oth)
            middle, n2 = norm_fwd(x, scatter(p0, p1), gm[l])
            n2_own, n2_oth = gather(n2)
            p0, p1, gu, hidden = mlp_fwd(l, n2_own, n2_oth)
            moved = scatter(p0, p1)
            saved.append((x, n1_own, n1_oth, qk, v, attn, middle, n2_own, n2_oth, gu, hidden))
            if l + 1 < layers:
                x, nxt = norm_fwd(x=middle, t=moved, gain=ga[l + 1])
                normed = gather(nxt)
            else:
                x = call(
                    add_kernel, (1,), [whole(middle.shape), whole(moved.shape)],
                    whole(middle.shape), sds(middle.shape, F32), 1e5, 1e6, row, [middle, moved],
                )

        def to_block(v):
            v = v.astype(F32)
            halves = [v[:, i * half : (i + 1) * half] for i in range(n_row)]
            mine = jnp.where(r == 0, halves[0], halves[1])
            got = other_row(jnp.where(r == 0, halves[1], halves[0]))
            return jnp.where(
                r == 0, jnp.concatenate([mine, got], 0), jnp.concatenate([got, mine], 0)
            )

        outputs = to_block(x)

        def pick_half(k):
            blk = lax.dynamic_index_in_dim(cot_all, k, 1, keepdims=False)
            return blk.transpose(0, 2, 1, 3).reshape(full)

        d0, d1 = pick_half(core), pick_half(1 - core)
        d_own = own_tokens(
            lax.dynamic_index_in_dim(
                lax.dynamic_index_in_dim(cot_all, seq_id, 0, keepdims=False), core, 0, keepdims=False
            )
        )
        kb = half // n_dp
        up_red = [None] * layers
        rest_red = [None] * layers
        g_attn = [None] * layers
        g_mlp = [None] * layers
        g_head = [None] * layers
        for l in reversed(range(layers)):
            xin, n1_own, n1_oth, qk, v, attn, middle, n2_own, n2_oth, gu, hidden = saved[l]
            o0, o1 = d0, d1
            p0, p1, dgu = mlp_bwd(l, d0, d1, gu)
            h_got = other_row(hidden)
            a_got = other_row(attn)
            part = wgrad(wgrad_up_kernel, 2 * kb, 2 * ff, [n2_own, n2_oth, dgu])
            moved, part = scatter(p0, p1, part)
            up_red[l] = lax.psum_scatter(part, "dp", scatter_dimension=0, tiled=False)
            d_mid, d_mid_round, g_mlp[l] = norm_bwd(moved, middle, d_own, gm[l])
            d0, d1 = gather(d_mid_round)
            p0, p1, dqkv, g_head[l] = attn_bwd(l, d0, d1, qk, v, attn)
            part = wgrad(
                wgrad_rest_kernel, 2 * kb + (2 * ow + 2 * ff) // n_dp, q3,
                [n1_own, n1_oth, dqkv, d0, d1, attn, a_got, o0, o1, hidden, h_got],
            )
            moved, part = scatter(p0, p1, part)
            rest_red[l] = lax.psum_scatter(part, "dp", scatter_dimension=0, tiled=False)
            d_own, d_round, g_attn[l] = norm_bwd(moved, xin, d_mid, ga[l])
            if l > 0:
                d0, d1 = gather(d_round)
        d_inputs = to_block(d_own)

        gains = jnp.concatenate(
            [g.reshape(-1) for g in g_attn]
            + [g.reshape(-1) for g in g_mlp]
            + [jnp.sum(g, axis=0).reshape(-1) for g in g_head]
        )
        gains = lax.psum(gains.reshape(-1, HD), ("row", "col"))
        gains = lax.psum(lax.optimization_barrier(gains), "dp").reshape(-1)
        lw = layers * width
        ga_out = gains[:lw].reshape(layers, width)
        gm_out = gains[lw : 2 * lw].reshape(layers, width)
        gh = gains[2 * lw :].reshape(layers, 2, HD)

        def join(own, got):
            return jnp.where(
                r == 0, jnp.concatenate([own, got], -1), jnp.concatenate([got, own], -1)
            ).astype(F32)

        grads = [[] for _ in range(7)]
        for l in range(layers):
            z = rest_red[l]
            got = other_row(z[kb : 2 * kb])
            mine = z[:kb]
            for k, (lo, hi) in enumerate(((0, qw), (qw, qw + kw), (qw + kw, q3))):
                grads[k].append(join(mine[:, lo:hi], got[:, lo:hi]))
            at = 2 * kb + 2 * ow // n_dp
            grads[3].append(z[2 * kb : at].astype(F32))
            grads[6].append(z[at:].astype(F32))
            z = up_red[l]
            got = other_row(z[kb : 2 * kb])
            mine = z[:kb]
            for k, (lo, hi) in enumerate(((0, ff), (ff, 2 * ff))):
                grads[4 + k].append(join(mine[:, lo:hi], got[:, lo:hi]))
        stacked = [jnp.stack(g) for g in grads]
        return (
            outputs, d_inputs, *stacked, ga_out, gm_out, gh[:, 0], gh[:, 1],
        )

    return body


def solution(mesh):
    body = make_body(mesh.shape["dp"], mesh.shape["row"], mesh.shape["col"])
    act = P(("dp", "col"), "row")
    seq = P(("dp", "row"), None)
    w_in = P(None, "row", "col")
    w_out = P(None, "col", "row")
    g_in = P(None, ("row", "dp"), "col")
    g_out = P(None, ("col", "dp"), "row")
    return jax.shard_map(
        body,
        mesh=mesh,
        in_specs=(
            act, seq, seq, act, w_in, w_in, w_in, w_out, w_in, w_in, w_out, P(), P(), P(), P(),
        ),
        out_specs=(
            act, act, g_in, g_in, g_in, g_out, g_in, g_in, g_out, P(), P(), P(), P(),
        ),
        check_vma=False,
    )
```

```python
import functools
import math

import jax
import jax.numpy as jnp
from jax import lax
from jax.experimental import pallas as pl
from jax.experimental.pallas import tpu as pltpu
from jax.sharding import PartitionSpec as P


HD = 128
SEQ = 256
EPS = 1e-06
THETA = 1000000.0
F32 = jnp.float32
BF16 = jnp.bfloat16
DP = "dp"
ROW = "row"
COL = "col"


def dot_nn(a, b):
    return jnp.dot(a, b, preferred_element_type=F32)


def dot_nt(a, b):
    return lax.dot_general(a, b, (((1,), (1,)), ((), ())), preferred_element_type=F32)


def dot_tn(a, b):
    return lax.dot_general(a, b, (((0,), (0,)), ((), ())), preferred_element_type=F32)


def whole(shape):
    rank = len(shape)
    return pl.BlockSpec(tuple(shape), lambda *_: (0,) * rank)


def per_seq(shape):
    rest = len(shape) - 1
    return pl.BlockSpec((1,) + tuple(shape[1:]), lambda i, *_: (i,) + (0,) * rest)


def sds(shape, dtype):
    return jax.ShapeDtypeStruct(tuple(shape), dtype)


def call(kernel, grid, in_specs, out_specs, out_shape, flops, nbytes, row, args, alias=None, vmem=None):
    return pl.pallas_call(
        kernel,
        grid_spec=pltpu.PrefetchScalarGridSpec(
            num_scalar_prefetch=2,
            grid=grid,
            in_specs=in_specs,
            out_specs=out_specs,
        ),
        out_shape=out_shape,
        input_output_aliases=alias or {},
        compiler_params=pltpu.CompilerParams(vmem_limit_bytes=vmem),
        cost_estimate=pl.CostEstimate(
            flops=int(flops), bytes_accessed=int(nbytes), transcendentals=0
        ),
    )(*row, *args)


def grad_halves(row_ref, ref0, ref1):
    r = row_ref[0]
    if len(ref0.shape) == 3:
        return [both_halves(ref0, ref1, cols) for cols in feature_cols(row_ref, ref0.shape[2] // 2)]
    return [jnp.concatenate([ref0[0, 0, i], ref1[0, 0, i]], axis=0) for i in (r, 1 - r)]


def both_halves(ref0, ref1, cols):
    return jnp.concatenate([ref0[0, :, cols], ref1[0, :, cols]], axis=0)


def rope_forward(v, cos2, sin2):
    return v * cos2 + pltpu.roll(v, v.shape[-1] // 2, 1) * sin2


def rope_backward(v, cos2, sin2):
    return v * cos2 - pltpu.roll(v, v.shape[-1] // 2, 1) * sin2


def head_inv(v):
    return lax.rsqrt(jnp.mean(v * v, axis=-1, keepdims=True) + EPS)


def feature_cols(row_ref, width):
    r = row_ref[0]
    own = pl.ds(pl.multiple_of(r * width, width), width)
    other = pl.ds(pl.multiple_of((1 - r) * width, width), width)
    return own, other


def got_attn(pk, qr, orows, at, w):
    n = pk.shape[0]
    rq = jnp.concatenate([pk[d, at : at + qr, :w] for d in range(n)], axis=0)
    ro = jnp.concatenate([pk[d, at + qr : at + qr + orows, :w] for d in range(n)], axis=0)
    return rq, ro


def got_mlp(pk, gr, dr, extra):
    n = pk.shape[0]
    half = 2 * pk.shape[2] // 3
    rgu = jnp.concatenate([pk[d, :gr, :] for d in range(n)], axis=0)
    rows = extra + dr
    low = rows // 3
    top = rows - low
    parts = []
    for d in range(n):
        if top > extra:
            parts.append(pk[d, gr + extra : gr + top, :half])
        parts.append(
            jnp.concatenate(
                [pk[d, gr : gr + low, half:], pk[d, gr + low : gr + 2 * low, half:]], axis=1
            )
        )
    return rgu, jnp.concatenate(parts, axis=0)


def norm_first_kernel(row_ref, side_ref, a0, a1, gain, n0, n1):
    for src, dst in ((a0, n0), (a1, n1)):
        v = jnp.concatenate([src[0, 0, 0], src[0, 0, 1]], axis=-1).astype(F32)
        inv = lax.rsqrt(jnp.mean(v * v, axis=-1, keepdims=True) + EPS)
        dst[0] = (v * inv * gain[...]).astype(BF16)


def attn_fwd_kernel(
    pack, row_ref, side_ref, n0, n1, wq, wk, wv, wo, pk, gq, gk, cos2, sin2, mask, p0, p1, qk_out, v_out, attn_out
):
    half = wq.shape[1]
    own, other = feature_cols(row_ref, half)
    qw = wq.shape[2]
    rq, ro = got_attn(pk, *pack)
    xo = both_halves(n0, n1, own)
    xt = both_halves(n0, n1, other)
    w_own = jnp.concatenate([wq[0], wk[0], wv[0]], axis=1)
    qkv = dot_nn(xo, w_own) + dot_nn(xt, rq)
    qk_out[0] = qkv[:, : qw + HD]
    v = qkv[:, qw + HD :].astype(BF16)
    v_out[0] = v
    c2 = cos2[0]
    s2 = sin2[0]
    k = qkv[:, qw : qw + HD]
    rot_k = rope_forward(k * head_inv(k) * gk[...], c2, s2).astype(BF16)
    allowed = mask[0] > 0
    parts = []
    for h in range(qw // HD):
        q = qkv[:, h * HD : (h + 1) * HD]
        rot_q = rope_forward(q * head_inv(q) * gq[...], c2, s2).astype(BF16)
        scores = dot_nt(rot_q, rot_k) * (1.0 / math.sqrt(HD))
        e = jnp.where(allowed, jnp.exp(scores), 0.0)
        total = jnp.sum(e, axis=-1, keepdims=True)
        probs = (e / total).astype(BF16)
        parts.append(dot_nn(probs, v).astype(BF16))
    attn = jnp.concatenate(parts, axis=1)
    attn_out[0] = attn
    hb = n0.shape[1]
    out_own = dot_nn(attn, wo[0]).astype(BF16)
    p0[0, :, own] = out_own[:hb]
    p1[0, :, own] = out_own[hb:]
    out_other = dot_nn(attn, ro).astype(BF16)
    p0[0, :, other] = out_other[:hb]
    p1[0, :, other] = out_other[hb:]


def mlp_fwd_kernel(pack, row_ref, side_ref, n0, n1, wg, wu, wd, pk, p0, p1, gu_out, h_out):
    half = wg.shape[1]
    ff = wg.shape[2]
    own, other = feature_cols(row_ref, half)
    rgu, rd = got_mlp(pk, *pack)
    xo = both_halves(n0, n1, own)
    xt = both_halves(n0, n1, other)
    w_own = jnp.concatenate([wg[0], wu[0]], axis=1)
    gu = dot_nn(xo, w_own) + dot_nn(xt, rgu)
    gu_out[0] = gu
    gate = gu[:, :ff]
    hidden = (gate * jax.nn.sigmoid(gate) * gu[:, ff:]).astype(BF16)
    h_out[0] = hidden
    hb = n0.shape[1]
    out_own = dot_nn(hidden, wd[0]).astype(BF16)
    p0[0, :, own] = out_own[:hb]
    p1[0, :, own] = out_own[hb:]
    out_other = dot_nn(hidden, rd).astype(BF16)
    p0[0, :, other] = out_other[:hb]
    p1[0, :, other] = out_other[hb:]


def mlp_bwd_kernel(pack, row_ref, side_ref, d0, d1, gu_in, wg, wu, wd, pk, p0, p1, dgu_out):
    half = wg.shape[1]
    ff = wg.shape[2]
    own, other = feature_cols(row_ref, half)
    rgu, rd = got_mlp(pk, *pack)
    do, dt = grad_halves(row_ref, d0, d1)
    d_hidden = dot_nt(do, wd[0]) + dot_nt(dt, rd)
    gate = gu_in[0, :, :ff]
    up = gu_in[0, :, ff:]
    sig = jax.nn.sigmoid(gate)
    d_gate = (d_hidden * up * sig * (1.0 + gate * (1.0 - sig))).astype(BF16)
    d_up = (d_hidden * gate * sig).astype(BF16)
    dgu = jnp.concatenate([d_gate, d_up], axis=1)
    dgu_out[0] = dgu
    hb = p0.shape[1]
    w_own = jnp.concatenate([wg[0], wu[0]], axis=1)
    out_own = dot_nt(dgu, w_own).astype(BF16)
    p0[0, :, own] = out_own[:hb]
    p1[0, :, own] = out_own[hb:]
    out_other = dot_nt(dgu, rgu).astype(BF16)
    p0[0, :, other] = out_other[:hb]
    p1[0, :, other] = out_other[hb:]


def attn_bwd_kernel(
    pack, row_ref, side_ref, d0, d1, qk_in, v_in, attn_in, wq, wk, wv, wo, pk, gq, gk, cos2, sin2, mask,
    p0, p1, dqkv_out, gain_out,
):
    half = wq.shape[1]
    qw = wq.shape[2]
    scale = 1.0 / math.sqrt(HD)
    own, other = feature_cols(row_ref, half)
    rq, ro = got_attn(pk, *pack)
    do, dt = grad_halves(row_ref, d0, d1)
    d_attn = (dot_nt(do, wo[0]) + dot_nt(dt, ro)).astype(BF16)
    c2 = cos2[0]
    s2 = sin2[0]
    v = v_in[0]
    k = qk_in[0, :, qw : qw + HD]
    inv_k = head_inv(k)
    rot_k = rope_forward(k * inv_k * gk[...], c2, s2).astype(BF16)
    allowed = mask[0] > 0
    d_v = None
    d_rk = None
    gain_q = None
    outs = []
    for h in range(qw // HD):
        cols = slice(h * HD, (h + 1) * HD)
        q = qk_in[0, :, cols]
        inv_q = head_inv(q)
        rot_q = rope_forward(q * inv_q * gq[...], c2, s2).astype(BF16)
        scores = dot_nt(rot_q, rot_k) * scale
        e = jnp.where(allowed, jnp.exp(scores), 0.0)
        p_full = e / jnp.sum(e, axis=-1, keepdims=True)
        da = d_attn[:, cols]
        delta = jnp.sum(
            da.astype(F32) * attn_in[0, :, cols].astype(F32), axis=-1, keepdims=True
        )
        d_probs = dot_nt(da, v)
        d_scores = (p_full * (d_probs - delta)).astype(BF16)
        dv_h = dot_tn(p_full.astype(BF16), da)
        drk_h = dot_tn(d_scores, rot_q) * scale
        d_v = dv_h if d_v is None else d_v + dv_h
        d_rk = drk_h if d_rk is None else d_rk + drk_h
        d_nq = rope_backward(dot_nn(d_scores, rot_k) * scale, c2, s2)
        gsum = jnp.sum(d_nq * q * inv_q, axis=0, keepdims=True)
        gain_q = gsum if gain_q is None else gain_q + gsum
        n = d_nq * gq[...]
        proj = jnp.mean(n * q, axis=-1, keepdims=True)
        outs.append((inv_q * n - q * (inv_q * inv_q * inv_q * proj)).astype(BF16))
    d_nk = rope_backward(d_rk, c2, s2)
    gain_k = jnp.sum(d_nk * k * inv_k, axis=0, keepdims=True)
    n = d_nk * gk[...]
    proj = jnp.mean(n * k, axis=-1, keepdims=True)
    outs.append((inv_k * n - k * (inv_k * inv_k * inv_k * proj)).astype(BF16))
    outs.append(d_v.astype(BF16))
    gain_out[0] = jnp.concatenate([gain_q, gain_k], axis=1)
    dqkv = jnp.concatenate(outs, axis=1)
    dqkv_out[0] = dqkv
    hb = p0.shape[1]
    w_own = jnp.concatenate([wq[0], wk[0], wv[0]], axis=1)
    out_own = dot_nt(dqkv, w_own).astype(BF16)
    p0[0, :, own] = out_own[:hb]
    p1[0, :, own] = out_own[hb:]
    out_other = dot_nt(dqkv, rq).astype(BF16)
    p0[0, :, other] = out_other[:hb]
    p1[0, :, other] = out_other[hb:]


def token_rows(ref0, ref1, cols):
    pieces = []
    for s in range(ref0.shape[0]):
        pieces.append(ref0[s, :, cols])
        pieces.append(ref1[s, :, cols])
    return jnp.concatenate(pieces, axis=0)


def flat_rows(ref):
    return jnp.concatenate([ref[s] for s in range(ref.shape[0])], axis=0)


def in_grads(row_ref, n0, n1, dy, out):
    n_dp = out.shape[0]
    half = n0.shape[2] // 2
    kb = half // n_dp
    for slot, cols in enumerate(feature_cols(row_ref, half)):
        g = dot_tn(token_rows(n0, n1, cols), dy).astype(BF16)
        for d in range(n_dp):
            out[d, slot * kb : (slot + 1) * kb, :] = g[d * kb : (d + 1) * kb]
    return 2 * kb


def out_grads(row_ref, d0, d1, own_ref, got_ref, out, at):
    per = out.shape[0] // 2
    r = row_ref[0]
    dcols = token_rows(d0, d1, feature_cols(row_ref, d0.shape[2] // 2)[0])
    for who, href in ((r, own_ref), (1 - r, got_ref)):
        g = dot_tn(flat_rows(href), dcols).astype(BF16)
        ub = g.shape[0] // per
        for j in range(per):
            out[who * per + j, at : at + ub, :] = g[j * ub : (j + 1) * ub]
    return at + ub


def wgrad_up_kernel(row_ref, side_ref, n0, n1, dgu, out):
    in_grads(row_ref, n0, n1, flat_rows(dgu), out)


def wgrad_down_kernel(row_ref, side_ref, d0, d1, h_own, h_rcv, held, out):
    kb = out.shape[1]
    half = kb * out.shape[0]
    rest = out.shape[2] - half
    per = out.shape[0] // 2
    r = row_ref[0]
    if len(d0.shape) == 3:
        dcols = token_rows(d0, d1, feature_cols(row_ref, half)[0])
    else:
        dcols = jnp.concatenate(
            [ref[s, 0, r] for s in range(d0.shape[0]) for ref in (d0, d1)], axis=0
        )
    for who, href in ((r, h_own), (1 - r, h_rcv)):
        g = dot_tn(flat_rows(href), dcols).astype(BF16)
        ub = g.shape[0] // per
        low = ub - kb
        for j in range(per):
            blk = g[j * ub : (j + 1) * ub]
            d = who * per + j
            out[d, :, :half] = blk[:kb]
            for m in range(half // rest):
                out[d, m * low : (m + 1) * low, half:] = blk[kb:, m * rest : (m + 1) * rest]


def wgrad_attn_kernel(row_ref, side_ref, n0, n1, dqkv, m0, m1, a_own, a_rcv, out):
    at = in_grads(row_ref, n0, n1, flat_rows(dqkv), out)
    out_grads(row_ref, m0, m1, a_own, a_rcv, out, at)


def finish_mlp_kernel(row_ref, side_ref, *refs):
    gate_out, up_out, down_out = refs[-3:]
    layers = gate_out.shape[0]
    kb = gate_out.shape[1]
    ff = gate_out.shape[2] // 2
    half = down_out.shape[2]
    low = down_out.shape[1] - kb
    own, other = feature_cols(row_ref, ff)
    for l in range(layers):
        z = refs[2 * l]
        got = refs[2 * l + 1]
        for ref, lo in ((gate_out, 0), (up_out, ff)):
            ref[l, :, own] = z[:kb, lo : lo + ff].astype(F32)
            ref[l, :, other] = got[:, lo : lo + ff].astype(F32)
        rest = z.shape[1] - half
        down_out[l, :kb, :] = z[2 * kb : 3 * kb, :half].astype(F32)
        for m in range(half // rest):
            down_out[l, kb:, m * rest : (m + 1) * rest] = z[
                2 * kb + m * low : 2 * kb + (m + 1) * low, half:
            ].astype(F32)


def finish_attn_kernel(row_ref, side_ref, *refs):
    q_out, k_out, v_out, o_out = refs[-4:]
    kb = q_out.shape[1]
    for l in range(q_out.shape[0]):
        z = refs[2 * l]
        got = refs[2 * l + 1]
        lo = 0
        for ref in (q_out, k_out, v_out):
            w = ref.shape[2] // 2
            own, other = feature_cols(row_ref, w)
            ref[l, :, own] = z[:kb, lo : lo + w].astype(F32)
            ref[l, :, other] = got[:, lo : lo + w].astype(F32)
            lo += w
        o_out[l] = z[2 * kb :, :].astype(F32)


def norm_fwd_kernel(row_ref, side_ref, x, t, gain, y_out, n_out):
    y = x[...]
    for i in range(t.shape[0]):
        y = y + t[i].astype(F32)
    y_out[...] = y
    inv = lax.rsqrt(jnp.mean(y * y, axis=-1, keepdims=True) + EPS)
    n_out[...] = (y * inv * gain[...]).astype(BF16)


def add_kernel(row_ref, side_ref, x, t, y_out):
    y = x[...]
    for i in range(t.shape[0]):
        y = y + t[i].astype(F32)
    y_out[...] = y


def norm_bwd_kernel(row_ref, side_ref, t, resid, d_res, gain, d_out, d_round, gain_out):
    dn = t[0].astype(F32)
    for i in range(1, t.shape[0]):
        dn = dn + t[i].astype(F32)
    x = resid[...]
    inv = lax.rsqrt(jnp.mean(x * x, axis=-1, keepdims=True) + EPS)
    gain_out[...] = jnp.sum(dn * x * inv, axis=0, keepdims=True)
    m = dn * gain[...]
    proj = jnp.mean(m * x, axis=-1, keepdims=True)
    d = d_res[...] + inv * m - x * (inv * inv * inv * proj)
    d_out[...] = d
    d_round[...] = d.astype(BF16)


def make_body(n_dp, n_row, n_col):
    pair = [(c, c ^ 1) for c in range(n_col)]
    swap = [(i, 1 - i) for i in range(n_row)]
    groups = [
        [c * n_row + i for c in range(k, n_col, 2) for i in range(n_row)] for k in range(2)
    ]
    plane = (COL, ROW)

    def gather_same(v):
        return lax.all_gather(v, plane, axis=0, tiled=False, axis_index_groups=groups)

    def other_core(v):
        return lax.ppermute(v, COL, pair)

    def other_row(v):
        return lax.ppermute(v, ROW, swap)

    def gather(v):
        own = gather_same(v).reshape(n_col // 2, n_row * v.shape[0], v.shape[1])
        return own, other_core(own)

    def scatter(p0, p1, late=None):
        blocks = (n_col // 2) * n_row
        width = p0.shape[2]
        sums = []
        for q0, q1 in ((p0, p1),) if late is None else ((p0, p1), late):
            got = other_core(q1)
            both = (q0.astype(F32) + got.astype(F32)).astype(BF16)
            sums.append(both.reshape(blocks, -1, width))
        both = sums[0] if late is None else jnp.concatenate(sums, axis=1)
        both = both.reshape(-1, width)
        moved = lax.all_to_all(both, plane, 0, 0, tiled=True, axis_index_groups=groups)
        return moved.reshape(blocks, -1, both.shape[1])

    def body(
        inputs, positions, segments, cotangent, w_query, w_key, w_value, w_output,
        w_gate, w_up, w_down, attn_gain, mlp_gain, query_gain, key_gain,
    ):
        layers = w_query.shape[0]
        half = inputs.shape[1]
        width = half * n_row
        tok_c = inputs.shape[0]
        tok = tok_c // n_row
        n_seq = n_col // 2
        r = lax.axis_index(ROW)
        c = lax.axis_index(COL)
        core = c % 2
        seq_id = c // 2
        row = (jnp.reshape(r, (1,)).astype(jnp.int32), jnp.reshape(core, (1,)).astype(jnp.int32))
        qw = w_query.shape[2] // n_row
        kw = w_key.shape[2] // n_row
        ow = w_output.shape[1] // n_row
        ff = w_gate.shape[2] // n_row

        ps = jnp.concatenate([positions, segments], axis=0)
        ps_other = other_row(ps)
        ps_all = jnp.stack([jnp.where(r == 0, ps, ps_other), jnp.where(r == 0, ps_other, ps)])

        def cut(w, axis, size, start):
            return lax.dynamic_slice_in_dim(w, start * size, size, axis)

        away = 1 - r
        dpi = lax.axis_index(DP)

        def piece(v):
            rows = v.shape[0] // n_dp
            return lax.dynamic_slice_in_dim(v, dpi * rows, rows, 0)

        def send_qkv(l):
            return jnp.concatenate(
                [
                    cut(w_query[l], 1, qw, away),
                    cut(w_key[l], 1, kw, away),
                    cut(w_value[l], 1, kw, away),
                ],
                axis=1,
            )

        def send_o(l):
            return cut(w_output[l], 0, ow, away)

        def send_mlp(l, lead):
            gu = jnp.concatenate(
                [piece(cut(w_gate[l], 1, ff, away)), piece(cut(w_up[l], 1, ff, away))], axis=1
            )
            rest = jnp.concatenate(lead + [piece(cut(w_down[l], 0, ff, away))], axis=0)
            low = rest.shape[0] // 3
            top = rest.shape[0] - low
            w = half // 2
            side = jnp.concatenate([rest[top:, :w], rest[top:, w:]], axis=0)
            return jnp.concatenate([gu, jnp.concatenate([rest[:top], side], axis=1)], axis=0)

        pk_first = other_row(jnp.concatenate([send_qkv(0), send_o(0)], axis=0))[None]
        raw = lax.all_gather(inputs, plane, axis=0, tiled=False).reshape(
            n_seq, 2, n_row, tok_c, half
        )
        pk_attn, pk_mlp, attn_pack, mlp_pack = [pk_first], [], [(half, ow, 0, half)], []
        for l in range(layers):
            lead = [] if l == 0 else [piece(send_qkv(l)), piece(send_o(l))]
            got = other_row(send_mlp(l, lead))
            pk = lax.all_gather(got, DP, axis=0, tiled=False)
            pk_mlp.append(pk)
            mlp_pack.append(
                (half // n_dp, ff // n_dp, sum(v.shape[0] for v in lead))
            )
            if l > 0:
                pk_attn.append(pk)
                attn_pack.append((half // n_dp, ow // n_dp, half // n_dp, half))

        cot_all = lax.all_gather(cotangent, plane, axis=0, tiled=False).reshape(
            n_seq, 2, n_row, tok_c, half
        )

        order = jnp.concatenate(
            [jnp.arange(tok_c) + core * tok_c, jnp.arange(tok_c) + (1 - core) * tok_c]
        )
        turned = jnp.where(core == 0, ps_all, jnp.roll(ps_all, tok_c, axis=2))
        freq = THETA ** (-2.0 * jnp.arange(HD // 2, dtype=F32) / HD)
        angles = turned[:, 0, :].astype(F32)[:, :, None] * freq[None, None, :]
        cos = jnp.cos(angles)
        sin = jnp.sin(angles)
        cos2 = jnp.concatenate([cos, cos], axis=-1)
        sin2 = jnp.concatenate([-sin, sin], axis=-1)
        seg = turned[:, 1, :]
        mask = (
            (seg[:, :, None] == seg[:, None, :]) & (order[None, None, :] <= order[None, :, None])
        ).astype(F32)

        gq = query_gain[:, None, :]
        gk = key_gain[:, None, :]
        ga = attn_gain[:, None, :]
        gm = mlp_gain[:, None, :]

        full = (n_seq, tok_c, width)
        nt = n_seq * SEQ
        wq_spec = lambda l: pl.BlockSpec((1, half, qw), lambda i, s, t: (l, 0, s[0]))
        wk_spec = lambda l: pl.BlockSpec((1, half, kw), lambda i, s, t: (l, 0, s[0]))
        wo_spec = lambda l: pl.BlockSpec((1, ow, half), lambda i, s, t: (l, s[0], 0))
        wg_spec = lambda l: pl.BlockSpec((1, half, ff), lambda i, s, t: (l, 0, s[0]))
        wd_spec = lambda l: pl.BlockSpec((1, ff, half), lambda i, s, t: (l, s[0], 0))
        q3 = qw + 2 * kw
        tables = [per_seq((n_seq, SEQ, HD)), per_seq((n_seq, SEQ, HD)), per_seq((n_seq, SEQ, SEQ))]

        def qkv_specs(l):
            return [
                wq_spec(l), wk_spec(l), wk_spec(l), wo_spec(l), whole(pk_attn[l].shape),
                whole((1, HD)), whole((1, HD)),
            ] + tables

        def qkv_args(l):
            return [
                w_query, w_key, w_value, w_output, pk_attn[l], gq[l], gk[l],
                cos2, sin2, mask,
            ]

        def mlp_specs(l):
            return [wg_spec(l), wg_spec(l), wd_spec(l), whole(pk_mlp[l].shape)]

        def mlp_args(l):
            return [w_gate, w_up, w_down, pk_mlp[l]]

        def attn_fwd(l, n0, n1):
            return call(
                functools.partial(attn_fwd_kernel, attn_pack[l]), (n_seq,),
                [per_seq(full), per_seq(full)] + qkv_specs(l),
                [per_seq(full), per_seq(full), per_seq((n_seq, SEQ, qw + kw)),
                 per_seq((n_seq, SEQ, kw)), per_seq((n_seq, SEQ, qw))],
                [sds(full, BF16), sds(full, BF16), sds((n_seq, SEQ, qw + kw), F32),
                 sds((n_seq, SEQ, kw), BF16), sds((n_seq, SEQ, qw), BF16)],
                2 * nt * width * (q3 + qw), 6e6, row, [n0, n1] + qkv_args(l),
            )

        def mlp_fwd(l, n0, n1):
            return call(
                functools.partial(mlp_fwd_kernel, mlp_pack[l]), (n_seq,),
                [per_seq(full), per_seq(full)] + mlp_specs(l),
                [per_seq(full), per_seq(full), per_seq((n_seq, SEQ, 2 * ff)),
                 per_seq((n_seq, SEQ, ff))],
                [sds(full, BF16), sds(full, BF16), sds((n_seq, SEQ, 2 * ff), F32),
                 sds((n_seq, SEQ, ff), BF16)],
                6 * nt * width * ff, 8e6, row, [n0, n1] + mlp_args(l),
            )

        def mlp_bwd(l, d0, d1, gu):
            return call(
                functools.partial(mlp_bwd_kernel, mlp_pack[l]), (n_seq,),
                grad_specs(l)[0] + [per_seq((n_seq, SEQ, 2 * ff))] + mlp_specs(l),
                [per_seq(full), per_seq(full), per_seq((n_seq, SEQ, 2 * ff))],
                [sds(full, BF16), sds(full, BF16), sds((n_seq, SEQ, 2 * ff), BF16)],
                6 * nt * width * ff, 8e6, row, [d0, d1, gu] + mlp_args(l),
            )

        def attn_bwd(l, d0, d1, qk, v, attn):
            return call(
                functools.partial(attn_bwd_kernel, attn_pack[l]), (n_seq,),
                [per_seq(full), per_seq(full), per_seq((n_seq, SEQ, qw + kw)),
                 per_seq((n_seq, SEQ, kw)), per_seq((n_seq, SEQ, qw))] + qkv_specs(l),
                [per_seq(full), per_seq(full), per_seq((n_seq, SEQ, q3)),
                 per_seq((n_seq, 1, 2 * HD))],
                [sds(full, BF16), sds(full, BF16), sds((n_seq, SEQ, q3), BF16),
                 sds((n_seq, 1, 2 * HD), F32)],
                2 * nt * width * (q3 + qw), 8e6, row, [d0, d1, qk, v, attn] + qkv_args(l),
            )

        def wgrad(kernel, rows, cols, args):
            return call(
                kernel, (1,), [whole(a.shape) for a in args],
                whole((n_dp, rows, cols)), sds((n_dp, rows, cols), BF16),
                2 * nt * n_dp * rows * cols, 8e6, row, args,
            )

        def norm_fwd(x, t, gain):
            return call(
                norm_fwd_kernel, (1,), [whole(x.shape), whole(t.shape), whole(gain.shape)],
                [whole(x.shape), whole(x.shape)], [sds(x.shape, F32), sds(x.shape, BF16)],
                1e5, 1e6, row, [x, t, gain],
            )

        def norm_bwd(t, resid, d_res, gain):
            return call(
                norm_bwd_kernel, (1,),
                [part_of(0), whole(resid.shape), whole(d_res.shape), whole(gain.shape)],
                [whole(resid.shape), whole(resid.shape), whole(gain.shape)],
                [sds(resid.shape, F32), sds(resid.shape, BF16), sds(gain.shape, F32)],
                1e5, 1e6, row, [t, resid, d_res, gain],
            )

        def own_tokens(blocks):
            mine = lax.dynamic_slice_in_dim(blocks, r * tok, tok, 1)
            return jnp.concatenate([mine[i] for i in range(n_row)], axis=-1).astype(F32)

        def own_block(blocks):
            mine = lax.dynamic_index_in_dim(blocks, seq_id, 0, keepdims=False)
            return own_tokens(lax.dynamic_index_in_dim(mine, core, 0, keepdims=False))

        x = own_block(raw)
        raw_shape = (1, 1, n_row, tok_c, half)
        normed = call(
            norm_first_kernel, (n_seq,),
            [
                pl.BlockSpec(raw_shape, lambda i, s, t: (i, t[0], 0, 0, 0)),
                pl.BlockSpec(raw_shape, lambda i, s, t: (i, 1 - t[0], 0, 0, 0)),
                whole((1, width)),
            ],
            [per_seq(full), per_seq(full)], [sds(full, BF16), sds(full, BF16)],
            1e6, 4e6, row, [raw, raw, ga[0]],
        )

        saved = []
        for l in range(layers):
            n1_own, n1_oth = normed
            p0, p1, qk, v, attn = attn_fwd(l, n1_own, n1_oth)
            middle, n2 = norm_fwd(x, scatter(p0, p1), gm[l])
            n2_own, n2_oth = gather(n2)
            p0, p1, gu, hidden = mlp_fwd(l, n2_own, n2_oth)
            saved.append((x, n1_own, n1_oth, qk, v, attn, middle, n2_own, n2_oth, gu, hidden))
            if l + 1 < layers:
                moved = scatter(p0, p1)
                x, nxt = norm_fwd(middle, moved, ga[l + 1])
                normed = gather(nxt)
            else:
                last_p = (p0, p1)

        def to_block(v):
            v = v.astype(F32)
            halves = [v[:, i * half : (i + 1) * half] for i in range(n_row)]
            mine = jnp.where(r == 0, halves[0], halves[1])
            got = other_row(jnp.where(r == 0, halves[1], halves[0]))
            return jnp.where(
                r == 0, jnp.concatenate([mine, got], 0), jnp.concatenate([got, mine], 0)
            )

        def part_of(j):
            return pl.BlockSpec((n_seq * n_row, tok, width), lambda *_: (0, j, 0))

        d0 = d1 = cot_all

        def grad_specs(l):
            if l + 1 < layers:
                return [per_seq(full), per_seq(full)], [whole(full), whole(full)]
            one, every = (1, 1, n_row, tok_c, half), (n_seq, 1, n_row, tok_c, half)
            return (
                [
                    pl.BlockSpec(one, lambda i, s, t: (i, t[0], 0, 0, 0)),
                    pl.BlockSpec(one, lambda i, s, t: (i, 1 - t[0], 0, 0, 0)),
                ],
                [
                    pl.BlockSpec(every, lambda i, s, t: (0, t[0], 0, 0, 0)),
                    pl.BlockSpec(every, lambda i, s, t: (0, 1 - t[0], 0, 0, 0)),
                ],
            )

        d_own = own_block(cot_all)
        kb = half // n_dp
        mlp_red = [None] * layers
        attn_red = [None] * layers
        g_attn = [None] * layers
        g_mlp = [None] * layers
        g_head = [None] * layers
        for l in reversed(range(layers)):
            xin, n1_own, n1_oth, qk, v, attn, middle, n2_own, n2_oth, gu, hidden = saved[l]
            o0, o1 = d0, d1
            p0, p1, dgu = mlp_bwd(l, d0, d1, gu)
            h_got = other_row(hidden)
            a_got = other_row(attn)
            args = [n2_own, n2_oth, dgu]
            part_shape = (n_dp, 3 * kb, 2 * ff)
            part = call(
                wgrad_up_kernel, (1,), [whole(a.shape) for a in args],
                pl.BlockSpec((n_dp, 2 * kb, 2 * ff), lambda i, s, t: (0, 0, 0)),
                sds(part_shape, BF16), 8 * nt * half * ff, 4e6, row, args,
            )
            args = [o0, o1, hidden, h_got]
            part = call(
                wgrad_down_kernel, (1,),
                grad_specs(l)[1] + [whole(hidden.shape)] * 2 + [pl.BlockSpec(memory_space=pl.ANY)],
                pl.BlockSpec((n_dp, kb, 2 * ff), lambda i, s, t: (0, 2, 0)),
                sds(part_shape, BF16), 4 * nt * half * ff, 4e6, row, args + [part],
                alias={len(args) + 2: 0},
            )
            if l + 1 == layers:
                moved_both = scatter(p0, p1, last_p)
                x = call(
                    add_kernel, (1,), [whole(middle.shape), part_of(1)],
                    whole(middle.shape), sds(middle.shape, F32), 1e5, 1e6, row,
                    [middle, moved_both],
                )
                outputs = to_block(x)
                moved = moved_both
            else:
                moved = scatter(p0, p1)
            mlp_red[l] = lax.psum_scatter(part, DP, scatter_dimension=0, tiled=False)
            d_mid, d_mid_round, g_mlp[l] = norm_bwd(moved, middle, d_own, gm[l])
            d0, d1 = gather(d_mid_round)
            p0, p1, dqkv, g_head[l] = attn_bwd(l, d0, d1, qk, v, attn)
            part = wgrad(
                wgrad_attn_kernel, 3 * kb, q3,
                [n1_own, n1_oth, dqkv, d0, d1, attn, a_got],
            )
            moved = scatter(p0, p1)
            attn_red[l] = lax.psum_scatter(part, DP, scatter_dimension=0, tiled=False)
            d_own, d_round, g_attn[l] = norm_bwd(moved, xin, d_mid, ga[l])
            if l > 0:
                d0, d1 = gather(d_round)
        d_inputs = to_block(d_own)

        gains = jnp.concatenate(
            [g.reshape(-1) for g in g_attn]
            + [g.reshape(-1) for g in g_mlp]
            + [jnp.sum(g, axis=0).reshape(-1) for g in g_head]
        )
        gains = gains.reshape(-1, HD)
        for axis, size in ((COL, n_col), (ROW, n_row), (DP, n_dp)):
            step = 1
            while step < size:
                peers = [(i, i ^ step) for i in range(size)]
                gains = gains + lax.ppermute(gains, axis, peers)
                step *= 2
        gains = gains.reshape(-1)
        lw = layers * width
        ga_out = gains[:lw].reshape(layers, width)
        gm_out = gains[lw : 2 * lw].reshape(layers, width)
        gh = gains[2 * lw :].reshape(layers, 2, HD)

        def finish(kernel, reds, shapes):
            args = []
            for z in reds:
                args += [z, other_row(z[kb : 2 * kb])]
            return call(
                kernel, (1,), [whole(a.shape) for a in args],
                [whole(o) for o in shapes], [sds(o, F32) for o in shapes], 1e5, 8e6, row, args,
            )

        g_gate, g_up, g_down = finish(
            finish_mlp_kernel, mlp_red,
            [(layers, kb, 2 * ff), (layers, kb, 2 * ff), (layers, 2 * ff // n_dp, half)],
        )
        g_q, g_k, g_v, g_o = finish(
            finish_attn_kernel, attn_red,
            [(layers, kb, 2 * qw), (layers, kb, 2 * kw), (layers, kb, 2 * kw),
             (layers, 2 * ow // n_dp, half)],
        )
        stacked = (g_q, g_k, g_v, g_o, g_gate, g_up, g_down)
        return (
            outputs, d_inputs, *stacked, ga_out, gm_out, gh[:, 0], gh[:, 1],
        )

    return body


def solution(mesh):
    body = make_body(mesh.shape[DP], mesh.shape[ROW], mesh.shape[COL])
    act = P((DP, COL), ROW)
    seq = P((DP, ROW), None)
    w_in = P(None, ROW, COL)
    w_out = P(None, COL, ROW)
    g_in = P(None, (ROW, DP), COL)
    g_out = P(None, (COL, DP), ROW)

    return jax.shard_map(
        body,
        mesh=mesh,
        in_specs=(
            act, seq, seq, act, w_in, w_in, w_in, w_out, w_in, w_in, w_out, P(), P(), P(), P(),
        ),
        out_specs=(
            act, act, g_in, g_in, g_in, g_out, g_in, g_in, g_out, P(), P(), P(), P(),
        ),
        check_vma=False,
    )
```

```python
import functools
import math

import jax
import jax.numpy as jnp
from jax import lax
from jax.experimental import pallas as pl
from jax.experimental.pallas import tpu as pltpu
from jax.sharding import PartitionSpec as P


HD = 128
SEQ = 256
EPS = 1e-06
THETA = 1000000.0
F32 = jnp.float32
BF16 = jnp.bfloat16
DP = "dp"
ROW = "row"
COL = "col"


def dot_nn(a, b):
    return jnp.dot(a, b, preferred_element_type=F32)


def dot_nt(a, b):
    return lax.dot_general(a, b, (((1,), (1,)), ((), ())), preferred_element_type=F32)


def dot_tn(a, b):
    return lax.dot_general(a, b, (((0,), (0,)), ((), ())), preferred_element_type=F32)


def whole(shape):
    rank = len(shape)
    return pl.BlockSpec(tuple(shape), lambda *_: (0,) * rank)


def per_seq(shape):
    rest = len(shape) - 1
    return pl.BlockSpec((1,) + tuple(shape[1:]), lambda i, *_: (i,) + (0,) * rest)


def sds(shape, dtype):
    return jax.ShapeDtypeStruct(tuple(shape), dtype)


def call(kernel, grid, in_specs, out_specs, out_shape, flops, nbytes, row, args, alias=None, vmem=None):
    return pl.pallas_call(
        kernel,
        grid_spec=pltpu.PrefetchScalarGridSpec(
            num_scalar_prefetch=2,
            grid=grid,
            in_specs=in_specs,
            out_specs=out_specs,
        ),
        out_shape=out_shape,
        input_output_aliases=alias or {},
        compiler_params=pltpu.CompilerParams(vmem_limit_bytes=vmem),
        cost_estimate=pl.CostEstimate(
            flops=int(flops), bytes_accessed=int(nbytes), transcendentals=0
        ),
    )(*row, *args)


def grad_halves(row_ref, ref0, ref1):
    r = row_ref[0]
    if len(ref0.shape) == 3:
        return [both_halves(ref0, ref1, cols) for cols in feature_cols(row_ref, ref0.shape[2] // 2)]
    return [jnp.concatenate([ref0[0, 0, i], ref1[0, 0, i]], axis=0) for i in (r, 1 - r)]


def both_halves(ref0, ref1, cols):
    return jnp.concatenate([ref0[0, :, cols], ref1[0, :, cols]], axis=0)


def rope_forward(v, cos2, sin2):
    return v * cos2 + pltpu.roll(v, v.shape[-1] // 2, 1) * sin2


def rope_backward(v, cos2, sin2):
    return v * cos2 - pltpu.roll(v, v.shape[-1] // 2, 1) * sin2


def head_inv(v):
    return lax.rsqrt(jnp.mean(v * v, axis=-1, keepdims=True) + EPS)


def feature_cols(row_ref, width):
    r = row_ref[0]
    own = pl.ds(pl.multiple_of(r * width, width), width)
    other = pl.ds(pl.multiple_of((1 - r) * width, width), width)
    return own, other


def got_attn(pk, qr, orows, at, w):
    n = pk.shape[0]
    rq = jnp.concatenate([pk[d, at : at + qr, :w] for d in range(n)], axis=0)
    ro = jnp.concatenate([pk[d, at + qr : at + qr + orows, :w] for d in range(n)], axis=0)
    return rq, ro


def got_mlp(pk, gr, dr, extra):
    n = pk.shape[0]
    half = 2 * pk.shape[2] // 3
    rgu = jnp.concatenate([pk[d, :gr, :] for d in range(n)], axis=0)
    rows = extra + dr
    low = rows // 3
    top = rows - low
    parts = []
    for d in range(n):
        if top > extra:
            parts.append(pk[d, gr + extra : gr + top, :half])
        parts.append(
            jnp.concatenate(
                [pk[d, gr : gr + low, half:], pk[d, gr + low : gr + 2 * low, half:]], axis=1
            )
        )
    return rgu, jnp.concatenate(parts, axis=0)


def norm_first_kernel(row_ref, side_ref, a0, a1, gain, n0, n1):
    for src, dst in ((a0, n0), (a1, n1)):
        v = jnp.concatenate([src[0, 0, 0], src[0, 0, 1]], axis=-1).astype(F32)
        inv = lax.rsqrt(jnp.mean(v * v, axis=-1, keepdims=True) + EPS)
        dst[0] = (v * inv * gain[...]).astype(BF16)


def attn_fwd_kernel(
    pack, row_ref, side_ref, n0, n1, wq, wk, wv, wo, pk, gq, gk, cos2, sin2, mask, p0, p1, qk_out, v_out, attn_out
):
    half = wq.shape[1]
    own, other = feature_cols(row_ref, half)
    qw = wq.shape[2]
    rq, ro = got_attn(pk, *pack)
    xo = both_halves(n0, n1, own)
    xt = both_halves(n0, n1, other)
    w_own = jnp.concatenate([wq[0], wk[0], wv[0]], axis=1)
    qkv = dot_nn(xo, w_own) + dot_nn(xt, rq)
    qk_out[0] = qkv[:, : qw + HD]
    v = qkv[:, qw + HD :].astype(BF16)
    v_out[0] = v
    c2 = cos2[0]
    s2 = sin2[0]
    k = qkv[:, qw : qw + HD]
    rot_k = rope_forward(k * head_inv(k) * gk[...], c2, s2).astype(BF16)
    allowed = mask[0] > 0
    parts = []
    for h in range(qw // HD):
        q = qkv[:, h * HD : (h + 1) * HD]
        rot_q = rope_forward(q * head_inv(q) * gq[...], c2, s2).astype(BF16)
        scores = dot_nt(rot_q, rot_k) * (1.0 / math.sqrt(HD))
        e = jnp.where(allowed, jnp.exp(scores), 0.0)
        total = jnp.sum(e, axis=-1, keepdims=True)
        probs = (e / total).astype(BF16)
        parts.append(dot_nn(probs, v).astype(BF16))
    attn = jnp.concatenate(parts, axis=1)
    attn_out[0] = attn
    hb = n0.shape[1]
    out_own = dot_nn(attn, wo[0]).astype(BF16)
    p0[0, :, own] = out_own[:hb]
    p1[0, :, own] = out_own[hb:]
    out_other = dot_nn(attn, ro).astype(BF16)
    p0[0, :, other] = out_other[:hb]
    p1[0, :, other] = out_other[hb:]


def mlp_fwd_kernel(pack, row_ref, side_ref, n0, n1, wg, wu, wd, pk, p0, p1, gu_out, h_out):
    half = wg.shape[1]
    ff = wg.shape[2]
    own, other = feature_cols(row_ref, half)
    rgu, rd = got_mlp(pk, *pack)
    xo = both_halves(n0, n1, own)
    xt = both_halves(n0, n1, other)
    w_own = jnp.concatenate([wg[0], wu[0]], axis=1)
    gu = dot_nn(xo, w_own) + dot_nn(xt, rgu)
    gu_out[0] = gu
    gate = gu[:, :ff]
    hidden = (gate * jax.nn.sigmoid(gate) * gu[:, ff:]).astype(BF16)
    h_out[0] = hidden
    hb = n0.shape[1]
    out_own = dot_nn(hidden, wd[0]).astype(BF16)
    p0[0, :, own] = out_own[:hb]
    p1[0, :, own] = out_own[hb:]
    out_other = dot_nn(hidden, rd).astype(BF16)
    p0[0, :, other] = out_other[:hb]
    p1[0, :, other] = out_other[hb:]


def mlp_bwd_kernel(pack, row_ref, side_ref, d0, d1, gu_in, wg, wu, wd, pk, p0, p1, dgu_out):
    half = wg.shape[1]
    ff = wg.shape[2]
    own, other = feature_cols(row_ref, half)
    rgu, rd = got_mlp(pk, *pack)
    do, dt = grad_halves(row_ref, d0, d1)
    d_hidden = dot_nt(do, wd[0]) + dot_nt(dt, rd)
    gate = gu_in[0, :, :ff]
    up = gu_in[0, :, ff:]
    sig = jax.nn.sigmoid(gate)
    d_gate = (d_hidden * up * sig * (1.0 + gate * (1.0 - sig))).astype(BF16)
    d_up = (d_hidden * gate * sig).astype(BF16)
    dgu = jnp.concatenate([d_gate, d_up], axis=1)
    dgu_out[0] = dgu
    hb = p0.shape[1]
    w_own = jnp.concatenate([wg[0], wu[0]], axis=1)
    out_own = dot_nt(dgu, w_own).astype(BF16)
    p0[0, :, own] = out_own[:hb]
    p1[0, :, own] = out_own[hb:]
    out_other = dot_nt(dgu, rgu).astype(BF16)
    p0[0, :, other] = out_other[:hb]
    p1[0, :, other] = out_other[hb:]


def attn_bwd_kernel(
    pack, row_ref, side_ref, d0, d1, qk_in, v_in, attn_in, wq, wk, wv, wo, pk, gq, gk, cos2, sin2, mask,
    p0, p1, dqkv_out, gain_out,
):
    half = wq.shape[1]
    qw = wq.shape[2]
    scale = 1.0 / math.sqrt(HD)
    own, other = feature_cols(row_ref, half)
    rq, ro = got_attn(pk, *pack)
    do, dt = grad_halves(row_ref, d0, d1)
    d_attn = (dot_nt(do, wo[0]) + dot_nt(dt, ro)).astype(BF16)
    c2 = cos2[0]
    s2 = sin2[0]
    v = v_in[0]
    k = qk_in[0, :, qw : qw + HD]
    inv_k = head_inv(k)
    rot_k = rope_forward(k * inv_k * gk[...], c2, s2).astype(BF16)
    allowed = mask[0] > 0
    d_v = None
    d_rk = None
    gain_q = None
    outs = []
    for h in range(qw // HD):
        cols = slice(h * HD, (h + 1) * HD)
        q = qk_in[0, :, cols]
        inv_q = head_inv(q)
        rot_q = rope_forward(q * inv_q * gq[...], c2, s2).astype(BF16)
        scores = dot_nt(rot_q, rot_k) * scale
        e = jnp.where(allowed, jnp.exp(scores), 0.0)
        p_full = e / jnp.sum(e, axis=-1, keepdims=True)
        da = d_attn[:, cols]
        delta = jnp.sum(
            da.astype(F32) * attn_in[0, :, cols].astype(F32), axis=-1, keepdims=True
        )
        d_probs = dot_nt(da, v)
        d_scores = (p_full * (d_probs - delta)).astype(BF16)
        dv_h = dot_tn(p_full.astype(BF16), da)
        drk_h = dot_tn(d_scores, rot_q) * scale
        d_v = dv_h if d_v is None else d_v + dv_h
        d_rk = drk_h if d_rk is None else d_rk + drk_h
        d_nq = rope_backward(dot_nn(d_scores, rot_k) * scale, c2, s2)
        gsum = jnp.sum(d_nq * q * inv_q, axis=0, keepdims=True)
        gain_q = gsum if gain_q is None else gain_q + gsum
        n = d_nq * gq[...]
        proj = jnp.mean(n * q, axis=-1, keepdims=True)
        outs.append((inv_q * n - q * (inv_q * inv_q * inv_q * proj)).astype(BF16))
    d_nk = rope_backward(d_rk, c2, s2)
    gain_k = jnp.sum(d_nk * k * inv_k, axis=0, keepdims=True)
    n = d_nk * gk[...]
    proj = jnp.mean(n * k, axis=-1, keepdims=True)
    outs.append((inv_k * n - k * (inv_k * inv_k * inv_k * proj)).astype(BF16))
    outs.append(d_v.astype(BF16))
    gain_out[0] = jnp.concatenate([gain_q, gain_k], axis=1)
    dqkv = jnp.concatenate(outs, axis=1)
    dqkv_out[0] = dqkv
    hb = p0.shape[1]
    w_own = jnp.concatenate([wq[0], wk[0], wv[0]], axis=1)
    out_own = dot_nt(dqkv, w_own).astype(BF16)
    p0[0, :, own] = out_own[:hb]
    p1[0, :, own] = out_own[hb:]
    out_other = dot_nt(dqkv, rq).astype(BF16)
    p0[0, :, other] = out_other[:hb]
    p1[0, :, other] = out_other[hb:]


def token_rows(ref0, ref1, cols):
    pieces = []
    for s in range(ref0.shape[0]):
        pieces.append(ref0[s, :, cols])
        pieces.append(ref1[s, :, cols])
    return jnp.concatenate(pieces, axis=0)


def flat_rows(ref):
    return jnp.concatenate([ref[s] for s in range(ref.shape[0])], axis=0)


def in_grads(row_ref, n0, n1, dy, out):
    n_dp = out.shape[0]
    half = n0.shape[2] // 2
    kb = half // n_dp
    for slot, cols in enumerate(feature_cols(row_ref, half)):
        g = dot_tn(token_rows(n0, n1, cols), dy).astype(BF16)
        for d in range(n_dp):
            out[d, slot * kb : (slot + 1) * kb, :] = g[d * kb : (d + 1) * kb]
    return 2 * kb


def out_grads(row_ref, d0, d1, own_ref, got_ref, out, at):
    per = out.shape[0] // 2
    r = row_ref[0]
    dcols = token_rows(d0, d1, feature_cols(row_ref, d0.shape[2] // 2)[0])
    for who, href in ((r, own_ref), (1 - r, got_ref)):
        g = dot_tn(flat_rows(href), dcols).astype(BF16)
        ub = g.shape[0] // per
        for j in range(per):
            out[who * per + j, at : at + ub, :] = g[j * ub : (j + 1) * ub]
    return at + ub


def wgrad_up_kernel(row_ref, side_ref, n0, n1, dgu, out):
    in_grads(row_ref, n0, n1, flat_rows(dgu), out)


def wgrad_down_kernel(row_ref, side_ref, d0, d1, h_own, h_rcv, held, out):
    kb = out.shape[1]
    half = kb * out.shape[0]
    rest = out.shape[2] - half
    per = out.shape[0] // 2
    r = row_ref[0]
    if len(d0.shape) == 3:
        dcols = token_rows(d0, d1, feature_cols(row_ref, half)[0])
    else:
        dcols = jnp.concatenate(
            [ref[s, 0, r] for s in range(d0.shape[0]) for ref in (d0, d1)], axis=0
        )
    for who, href in ((r, h_own), (1 - r, h_rcv)):
        g = dot_tn(flat_rows(href), dcols).astype(BF16)
        ub = g.shape[0] // per
        low = ub - kb
        for j in range(per):
            blk = g[j * ub : (j + 1) * ub]
            d = who * per + j
            out[d, :, :half] = blk[:kb]
            for m in range(half // rest):
                out[d, m * low : (m + 1) * low, half:] = blk[kb:, m * rest : (m + 1) * rest]


def wgrad_attn_kernel(row_ref, side_ref, n0, n1, dqkv, m0, m1, a_own, a_rcv, out):
    at = in_grads(row_ref, n0, n1, flat_rows(dqkv), out)
    out_grads(row_ref, m0, m1, a_own, a_rcv, out, at)


def finish_mlp_kernel(row_ref, side_ref, *refs):
    gate_out, up_out, down_out = refs[-3:]
    layers = gate_out.shape[0]
    kb = gate_out.shape[1]
    ff = gate_out.shape[2] // 2
    half = down_out.shape[2]
    low = down_out.shape[1] - kb
    own, other = feature_cols(row_ref, ff)
    for l in range(layers):
        z = refs[2 * l]
        got = refs[2 * l + 1]
        for ref, lo in ((gate_out, 0), (up_out, ff)):
            ref[l, :, own] = z[:kb, lo : lo + ff].astype(F32)
            ref[l, :, other] = got[:, lo : lo + ff].astype(F32)
        rest = z.shape[1] - half
        down_out[l, :kb, :] = z[2 * kb : 3 * kb, :half].astype(F32)
        for m in range(half // rest):
            down_out[l, kb:, m * rest : (m + 1) * rest] = z[
                2 * kb + m * low : 2 * kb + (m + 1) * low, half:
            ].astype(F32)


def finish_attn_kernel(row_ref, side_ref, *refs):
    q_out, k_out, v_out, o_out = refs[-4:]
    kb = q_out.shape[1]
    for l in range(q_out.shape[0]):
        z = refs[2 * l]
        got = refs[2 * l + 1]
        lo = 0
        for ref in (q_out, k_out, v_out):
            w = ref.shape[2] // 2
            own, other = feature_cols(row_ref, w)
            ref[l, :, own] = z[:kb, lo : lo + w].astype(F32)
            ref[l, :, other] = got[:, lo : lo + w].astype(F32)
            lo += w
        o_out[l] = z[2 * kb :, :].astype(F32)


def norm_fwd_kernel(row_ref, side_ref, x, t, gain, y_out, n_out):
    y = x[...]
    for i in range(t.shape[0]):
        y = y + t[i].astype(F32)
    y_out[...] = y
    inv = lax.rsqrt(jnp.mean(y * y, axis=-1, keepdims=True) + EPS)
    n_out[...] = (y * inv * gain[...]).astype(BF16)


def add_kernel(row_ref, side_ref, x, t, y_out):
    y = x[...]
    for i in range(t.shape[0]):
        y = y + t[i].astype(F32)
    y_out[...] = y


def norm_bwd_kernel(row_ref, side_ref, t, resid, d_res, gain, d_out, d_round, gain_out):
    dn = t[0].astype(F32)
    for i in range(1, t.shape[0]):
        dn = dn + t[i].astype(F32)
    x = resid[...]
    inv = lax.rsqrt(jnp.mean(x * x, axis=-1, keepdims=True) + EPS)
    gain_out[...] = jnp.sum(dn * x * inv, axis=0, keepdims=True)
    m = dn * gain[...]
    proj = jnp.mean(m * x, axis=-1, keepdims=True)
    d = d_res[...] + inv * m - x * (inv * inv * inv * proj)
    d_out[...] = d
    d_round[...] = d.astype(BF16)


def make_body(n_dp, n_row, n_col):
    pair = [(c, c ^ 1) for c in range(n_col)]
    swap = [(i, 1 - i) for i in range(n_row)]
    groups = [
        [c * n_row + i for c in range(k, n_col, 2) for i in range(n_row)] for k in range(2)
    ]
    plane = (COL, ROW)

    def gather_same(v):
        return lax.all_gather(v, plane, axis=0, tiled=False, axis_index_groups=groups)

    def other_core(v):
        return lax.ppermute(v, COL, pair)

    def other_row(v):
        return lax.ppermute(v, ROW, swap)

    def gather(v):
        own = gather_same(v).reshape(n_col // 2, n_row * v.shape[0], v.shape[1])
        return own, other_core(own)

    def scatter(p0, p1, late=None):
        blocks = (n_col // 2) * n_row
        width = p0.shape[2]
        sums = []
        for q0, q1 in ((p0, p1),) if late is None else ((p0, p1), late):
            got = other_core(q1)
            both = (q0.astype(F32) + got.astype(F32)).astype(BF16)
            sums.append(both.reshape(blocks, -1, width))
        both = sums[0] if late is None else jnp.concatenate(sums, axis=1)
        both = both.reshape(-1, width)
        moved = lax.all_to_all(both, plane, 0, 0, tiled=True, axis_index_groups=groups)
        return moved.reshape(blocks, -1, both.shape[1])

    def body(
        inputs, positions, segments, cotangent, w_query, w_key, w_value, w_output,
        w_gate, w_up, w_down, attn_gain, mlp_gain, query_gain, key_gain,
    ):
        layers = w_query.shape[0]
        half = inputs.shape[1]
        width = half * n_row
        tok_c = inputs.shape[0]
        tok = tok_c // n_row
        n_seq = n_col // 2
        r = lax.axis_index(ROW)
        c = lax.axis_index(COL)
        core = c % 2
        seq_id = c // 2
        row = (jnp.reshape(r, (1,)).astype(jnp.int32), jnp.reshape(core, (1,)).astype(jnp.int32))
        qw = w_query.shape[2] // n_row
        kw = w_key.shape[2] // n_row
        ow = w_output.shape[1] // n_row
        ff = w_gate.shape[2] // n_row

        ps = jnp.concatenate([positions, segments], axis=0)
        ps_other = other_row(ps)
        ps_all = jnp.stack([jnp.where(r == 0, ps, ps_other), jnp.where(r == 0, ps_other, ps)])

        def cut(w, axis, size, start):
            return lax.dynamic_slice_in_dim(w, start * size, size, axis)

        away = 1 - r
        dpi = lax.axis_index(DP)

        def piece(v):
            rows = v.shape[0] // n_dp
            return lax.dynamic_slice_in_dim(v, dpi * rows, rows, 0)

        def send_qkv(l):
            return jnp.concatenate(
                [
                    cut(w_query[l], 1, qw, away),
                    cut(w_key[l], 1, kw, away),
                    cut(w_value[l], 1, kw, away),
                ],
                axis=1,
            )

        def send_o(l):
            return cut(w_output[l], 0, ow, away)

        def send_mlp(l, lead):
            gu = jnp.concatenate(
                [piece(cut(w_gate[l], 1, ff, away)), piece(cut(w_up[l], 1, ff, away))], axis=1
            )
            rest = jnp.concatenate(lead + [piece(cut(w_down[l], 0, ff, away))], axis=0)
            low = rest.shape[0] // 3
            top = rest.shape[0] - low
            w = half // 2
            side = jnp.concatenate([rest[top:, :w], rest[top:, w:]], axis=0)
            return jnp.concatenate([gu, jnp.concatenate([rest[:top], side], axis=1)], axis=0)

        raw = lax.all_gather(inputs, plane, axis=0, tiled=False).reshape(
            n_seq, 2, n_row, tok_c, half
        )
        pk_attn, pk_mlp = [], []
        attn_pack = (half, ow, 0, half)
        mlp_pack = (half // n_dp, ff // n_dp, 0)
        for l in range(layers):
            pk_attn.append(other_row(jnp.concatenate([send_qkv(l), send_o(l)], axis=0))[None])
            got = other_row(send_mlp(l, []))
            pk_mlp.append(lax.all_gather(got, DP, axis=0, tiled=False))

        cot_all = lax.all_gather(cotangent, plane, axis=0, tiled=False).reshape(
            n_seq, 2, n_row, tok_c, half
        )

        order = jnp.concatenate(
            [jnp.arange(tok_c) + core * tok_c, jnp.arange(tok_c) + (1 - core) * tok_c]
        )
        turned = jnp.where(core == 0, ps_all, jnp.roll(ps_all, tok_c, axis=2))
        freq = THETA ** (-2.0 * jnp.arange(HD // 2, dtype=F32) / HD)
        angles = turned[:, 0, :].astype(F32)[:, :, None] * freq[None, None, :]
        cos = jnp.cos(angles)
        sin = jnp.sin(angles)
        cos2 = jnp.concatenate([cos, cos], axis=-1)
        sin2 = jnp.concatenate([-sin, sin], axis=-1)
        seg = turned[:, 1, :]
        mask = (
            (seg[:, :, None] == seg[:, None, :]) & (order[None, None, :] <= order[None, :, None])
        ).astype(F32)

        gq = query_gain[:, None, :]
        gk = key_gain[:, None, :]
        ga = attn_gain[:, None, :]
        gm = mlp_gain[:, None, :]

        full = (n_seq, tok_c, width)
        nt = n_seq * SEQ
        wq_spec = lambda l: pl.BlockSpec((1, half, qw), lambda i, s, t: (l, 0, s[0]))
        wk_spec = lambda l: pl.BlockSpec((1, half, kw), lambda i, s, t: (l, 0, s[0]))
        wo_spec = lambda l: pl.BlockSpec((1, ow, half), lambda i, s, t: (l, s[0], 0))
        wg_spec = lambda l: pl.BlockSpec((1, half, ff), lambda i, s, t: (l, 0, s[0]))
        wd_spec = lambda l: pl.BlockSpec((1, ff, half), lambda i, s, t: (l, s[0], 0))
        q3 = qw + 2 * kw
        tables = [per_seq((n_seq, SEQ, HD)), per_seq((n_seq, SEQ, HD)), per_seq((n_seq, SEQ, SEQ))]

        def qkv_specs(l):
            return [
                wq_spec(l), wk_spec(l), wk_spec(l), wo_spec(l), whole(pk_attn[l].shape),
                whole((1, HD)), whole((1, HD)),
            ] + tables

        def qkv_args(l):
            return [
                w_query, w_key, w_value, w_output, pk_attn[l], gq[l], gk[l],
                cos2, sin2, mask,
            ]

        def mlp_specs(l):
            return [wg_spec(l), wg_spec(l), wd_spec(l), whole(pk_mlp[l].shape)]

        def mlp_args(l):
            return [w_gate, w_up, w_down, pk_mlp[l]]

        def attn_fwd(l, n0, n1):
            return call(
                functools.partial(attn_fwd_kernel, attn_pack), (n_seq,),
                [per_seq(full), per_seq(full)] + qkv_specs(l),
                [per_seq(full), per_seq(full), per_seq((n_seq, SEQ, qw + kw)),
                 per_seq((n_seq, SEQ, kw)), per_seq((n_seq, SEQ, qw))],
                [sds(full, BF16), sds(full, BF16), sds((n_seq, SEQ, qw + kw), F32),
                 sds((n_seq, SEQ, kw), BF16), sds((n_seq, SEQ, qw), BF16)],
                2 * nt * width * (q3 + qw), 6e6, row, [n0, n1] + qkv_args(l),
            )

        def mlp_fwd(l, n0, n1):
            return call(
                functools.partial(mlp_fwd_kernel, mlp_pack), (n_seq,),
                [per_seq(full), per_seq(full)] + mlp_specs(l),
                [per_seq(full), per_seq(full), per_seq((n_seq, SEQ, 2 * ff)),
                 per_seq((n_seq, SEQ, ff))],
                [sds(full, BF16), sds(full, BF16), sds((n_seq, SEQ, 2 * ff), F32),
                 sds((n_seq, SEQ, ff), BF16)],
                6 * nt * width * ff, 8e6, row, [n0, n1] + mlp_args(l),
            )

        def mlp_bwd(l, d0, d1, gu):
            return call(
                functools.partial(mlp_bwd_kernel, mlp_pack), (n_seq,),
                grad_specs(l)[0] + [per_seq((n_seq, SEQ, 2 * ff))] + mlp_specs(l),
                [per_seq(full), per_seq(full), per_seq((n_seq, SEQ, 2 * ff))],
                [sds(full, BF16), sds(full, BF16), sds((n_seq, SEQ, 2 * ff), BF16)],
                6 * nt * width * ff, 8e6, row, [d0, d1, gu] + mlp_args(l),
            )

        def attn_bwd(l, d0, d1, qk, v, attn):
            return call(
                functools.partial(attn_bwd_kernel, attn_pack), (n_seq,),
                [per_seq(full), per_seq(full), per_seq((n_seq, SEQ, qw + kw)),
                 per_seq((n_seq, SEQ, kw)), per_seq((n_seq, SEQ, qw))] + qkv_specs(l),
                [per_seq(full), per_seq(full), per_seq((n_seq, SEQ, q3)),
                 per_seq((n_seq, 1, 2 * HD))],
                [sds(full, BF16), sds(full, BF16), sds((n_seq, SEQ, q3), BF16),
                 sds((n_seq, 1, 2 * HD), F32)],
                2 * nt * width * (q3 + qw), 8e6, row, [d0, d1, qk, v, attn] + qkv_args(l),
            )

        def wgrad(kernel, rows, cols, args):
            return call(
                kernel, (1,), [whole(a.shape) for a in args],
                whole((n_dp, rows, cols)), sds((n_dp, rows, cols), BF16),
                2 * nt * n_dp * rows * cols, 8e6, row, args,
            )

        def norm_fwd(x, t, gain):
            return call(
                norm_fwd_kernel, (1,), [whole(x.shape), whole(t.shape), whole(gain.shape)],
                [whole(x.shape), whole(x.shape)], [sds(x.shape, F32), sds(x.shape, BF16)],
                1e5, 1e6, row, [x, t, gain],
            )

        def norm_bwd(t, resid, d_res, gain):
            return call(
                norm_bwd_kernel, (1,),
                [part_of(0), whole(resid.shape), whole(d_res.shape), whole(gain.shape)],
                [whole(resid.shape), whole(resid.shape), whole(gain.shape)],
                [sds(resid.shape, F32), sds(resid.shape, BF16), sds(gain.shape, F32)],
                1e5, 1e6, row, [t, resid, d_res, gain],
            )

        def own_tokens(blocks):
            mine = lax.dynamic_slice_in_dim(blocks, r * tok, tok, 1)
            return jnp.concatenate([mine[i] for i in range(n_row)], axis=-1).astype(F32)

        def own_block(blocks):
            mine = lax.dynamic_index_in_dim(blocks, seq_id, 0, keepdims=False)
            return own_tokens(lax.dynamic_index_in_dim(mine, core, 0, keepdims=False))

        x = own_block(raw)
        raw_shape = (1, 1, n_row, tok_c, half)
        normed = call(
            norm_first_kernel, (n_seq,),
            [
                pl.BlockSpec(raw_shape, lambda i, s, t: (i, t[0], 0, 0, 0)),
                pl.BlockSpec(raw_shape, lambda i, s, t: (i, 1 - t[0], 0, 0, 0)),
                whole((1, width)),
            ],
            [per_seq(full), per_seq(full)], [sds(full, BF16), sds(full, BF16)],
            1e6, 4e6, row, [raw, raw, ga[0]],
        )

        saved = []
        for l in range(layers):
            n1_own, n1_oth = normed
            p0, p1, qk, v, attn = attn_fwd(l, n1_own, n1_oth)
            middle, n2 = norm_fwd(x, scatter(p0, p1), gm[l])
            n2_own, n2_oth = gather(n2)
            p0, p1, gu, hidden = mlp_fwd(l, n2_own, n2_oth)
            saved.append((x, n1_own, n1_oth, qk, v, attn, middle, n2_own, n2_oth, gu, hidden))
            if l + 1 < layers:
                moved = scatter(p0, p1)
                x, nxt = norm_fwd(middle, moved, ga[l + 1])
                normed = gather(nxt)
            else:
                last_p = (p0, p1)

        def to_block(v):
            v = v.astype(F32)
            halves = [v[:, i * half : (i + 1) * half] for i in range(n_row)]
            mine = jnp.where(r == 0, halves[0], halves[1])
            got = other_row(jnp.where(r == 0, halves[1], halves[0]))
            return jnp.where(
                r == 0, jnp.concatenate([mine, got], 0), jnp.concatenate([got, mine], 0)
            )

        def part_of(j):
            return pl.BlockSpec((n_seq * n_row, tok, width), lambda *_: (0, j, 0))

        d0 = d1 = cot_all

        def grad_specs(l):
            if l + 1 < layers:
                return [per_seq(full), per_seq(full)], [whole(full), whole(full)]
            one, every = (1, 1, n_row, tok_c, half), (n_seq, 1, n_row, tok_c, half)
            return (
                [
                    pl.BlockSpec(one, lambda i, s, t: (i, t[0], 0, 0, 0)),
                    pl.BlockSpec(one, lambda i, s, t: (i, 1 - t[0], 0, 0, 0)),
                ],
                [
                    pl.BlockSpec(every, lambda i, s, t: (0, t[0], 0, 0, 0)),
                    pl.BlockSpec(every, lambda i, s, t: (0, 1 - t[0], 0, 0, 0)),
                ],
            )

        d_own = own_block(cot_all)
        kb = half // n_dp
        mlp_red = [None] * layers
        attn_red = [None] * layers
        g_attn = [None] * layers
        g_mlp = [None] * layers
        g_head = [None] * layers
        for l in reversed(range(layers)):
            xin, n1_own, n1_oth, qk, v, attn, middle, n2_own, n2_oth, gu, hidden = saved[l]
            o0, o1 = d0, d1
            p0, p1, dgu = mlp_bwd(l, d0, d1, gu)
            h_got = other_row(hidden)
            a_got = other_row(attn)
            args = [n2_own, n2_oth, dgu]
            part_shape = (n_dp, 3 * kb, 2 * ff)
            part = call(
                wgrad_up_kernel, (1,), [whole(a.shape) for a in args],
                pl.BlockSpec((n_dp, 2 * kb, 2 * ff), lambda i, s, t: (0, 0, 0)),
                sds(part_shape, BF16), 8 * nt * half * ff, 4e6, row, args,
            )
            args = [o0, o1, hidden, h_got]
            part = call(
                wgrad_down_kernel, (1,),
                grad_specs(l)[1] + [whole(hidden.shape)] * 2 + [pl.BlockSpec(memory_space=pl.ANY)],
                pl.BlockSpec((n_dp, kb, 2 * ff), lambda i, s, t: (0, 2, 0)),
                sds(part_shape, BF16), 4 * nt * half * ff, 4e6, row, args + [part],
                alias={len(args) + 2: 0},
            )
            if l + 1 == layers:
                moved_both = scatter(p0, p1, last_p)
                x = call(
                    add_kernel, (1,), [whole(middle.shape), part_of(1)],
                    whole(middle.shape), sds(middle.shape, F32), 1e5, 1e6, row,
                    [middle, moved_both],
                )
                outputs = to_block(x)
                moved = moved_both
            else:
                moved = scatter(p0, p1)
            mlp_red[l] = lax.psum_scatter(part, DP, scatter_dimension=0, tiled=False)
            d_mid, d_mid_round, g_mlp[l] = norm_bwd(moved, middle, d_own, gm[l])
            d0, d1 = gather(d_mid_round)
            p0, p1, dqkv, g_head[l] = attn_bwd(l, d0, d1, qk, v, attn)
            part = wgrad(
                wgrad_attn_kernel, 3 * kb, q3,
                [n1_own, n1_oth, dqkv, d0, d1, attn, a_got],
            )
            moved = scatter(p0, p1)
            attn_red[l] = lax.psum_scatter(part, DP, scatter_dimension=0, tiled=False)
            d_own, d_round, g_attn[l] = norm_bwd(moved, xin, d_mid, ga[l])
            if l > 0:
                d0, d1 = gather(d_round)
        d_inputs = to_block(d_own)

        gains = jnp.concatenate(
            [g.reshape(-1) for g in g_attn]
            + [g.reshape(-1) for g in g_mlp]
            + [jnp.sum(g, axis=0).reshape(-1) for g in g_head]
        )
        gains = gains.reshape(-1, HD)
        for axis, size in ((COL, n_col), (ROW, n_row), (DP, n_dp)):
            step = 1
            while step < size:
                peers = [(i, i ^ step) for i in range(size)]
                gains = gains + lax.ppermute(gains, axis, peers)
                step *= 2
        gains = gains.reshape(-1)
        lw = layers * width
        ga_out = gains[:lw].reshape(layers, width)
        gm_out = gains[lw : 2 * lw].reshape(layers, width)
        gh = gains[2 * lw :].reshape(layers, 2, HD)

        def finish(kernel, reds, shapes):
            args = []
            for z in reds:
                args += [z, other_row(z[kb : 2 * kb])]
            return call(
                kernel, (1,), [whole(a.shape) for a in args],
                [whole(o) for o in shapes], [sds(o, F32) for o in shapes], 1e5, 8e6, row, args,
            )

        g_gate, g_up, g_down = finish(
            finish_mlp_kernel, mlp_red,
            [(layers, kb, 2 * ff), (layers, kb, 2 * ff), (layers, 2 * ff // n_dp, half)],
        )
        g_q, g_k, g_v, g_o = finish(
            finish_attn_kernel, attn_red,
            [(layers, kb, 2 * qw), (layers, kb, 2 * kw), (layers, kb, 2 * kw),
             (layers, 2 * ow // n_dp, half)],
        )
        stacked = (g_q, g_k, g_v, g_o, g_gate, g_up, g_down)
        return (
            outputs, d_inputs, *stacked, ga_out, gm_out, gh[:, 0], gh[:, 1],
        )

    return body


def solution(mesh):
    body = make_body(mesh.shape[DP], mesh.shape[ROW], mesh.shape[COL])
    act = P((DP, COL), ROW)
    seq = P((DP, ROW), None)
    w_in = P(None, ROW, COL)
    w_out = P(None, COL, ROW)
    g_in = P(None, (ROW, DP), COL)
    g_out = P(None, (COL, DP), ROW)

    return jax.shard_map(
        body,
        mesh=mesh,
        in_specs=(
            act, seq, seq, act, w_in, w_in, w_in, w_out, w_in, w_in, w_out, P(), P(), P(), P(),
        ),
        out_specs=(
            act, act, g_in, g_in, g_in, g_out, g_in, g_in, g_out, P(), P(), P(), P(),
        ),
        check_vma=False,
    )
```

```python
import functools
import math

import jax
import jax.numpy as jnp
from jax import lax
from jax.experimental import pallas as pl
from jax.experimental.pallas import tpu as pltpu
from jax.sharding import PartitionSpec as P


HD = 128
SEQ = 256
EPS = 1e-06
THETA = 1000000.0
F32 = jnp.float32
BF16 = jnp.bfloat16
DP = "dp"
ROW = "row"
COL = "col"


def dot_nn(a, b):
    return jnp.dot(a, b, preferred_element_type=F32)


def dot_nt(a, b):
    return lax.dot_general(a, b, (((1,), (1,)), ((), ())), preferred_element_type=F32)


def dot_tn(a, b):
    return lax.dot_general(a, b, (((0,), (0,)), ((), ())), preferred_element_type=F32)


def whole(shape):
    rank = len(shape)
    return pl.BlockSpec(tuple(shape), lambda *_: (0,) * rank)


def per_seq(shape):
    rest = len(shape) - 1
    return pl.BlockSpec((1,) + tuple(shape[1:]), lambda i, *_: (i,) + (0,) * rest)


def sds(shape, dtype):
    return jax.ShapeDtypeStruct(tuple(shape), dtype)


def call(kernel, grid, in_specs, out_specs, out_shape, flops, nbytes, row, args, alias=None):
    return pl.pallas_call(
        kernel,
        grid_spec=pltpu.PrefetchScalarGridSpec(
            num_scalar_prefetch=2,
            grid=grid,
            in_specs=in_specs,
            out_specs=out_specs,
        ),
        out_shape=out_shape,
        input_output_aliases=alias or {},
        cost_estimate=pl.CostEstimate(
            flops=int(flops), bytes_accessed=int(nbytes), transcendentals=0
        ),
    )(*row, *args)


def grad_halves(row_ref, ref0, ref1):
    r = row_ref[0]
    if len(ref0.shape) == 3:
        return [both_halves(ref0, ref1, cols) for cols in feature_cols(row_ref, ref0.shape[2] // 2)]
    return [jnp.concatenate([ref0[0, 0, i], ref1[0, 0, i]], axis=0) for i in (r, 1 - r)]


def both_halves(ref0, ref1, cols):
    return jnp.concatenate([ref0[0, :, cols], ref1[0, :, cols]], axis=0)


def rope_forward(v, cos2, sin2):
    return v * cos2 + pltpu.roll(v, v.shape[-1] // 2, 1) * sin2


def rope_backward(v, cos2, sin2):
    return v * cos2 - pltpu.roll(v, v.shape[-1] // 2, 1) * sin2


def head_inv(v):
    return lax.rsqrt(jnp.mean(v * v, axis=-1, keepdims=True) + EPS)


def feature_cols(row_ref, width):
    r = row_ref[0]
    own = pl.ds(pl.multiple_of(r * width, width), width)
    other = pl.ds(pl.multiple_of((1 - r) * width, width), width)
    return own, other


def got_attn(pk, qr, orows, at, w):
    n = pk.shape[0]
    rq = jnp.concatenate([pk[d, at : at + qr, :w] for d in range(n)], axis=0)
    ro = jnp.concatenate([pk[d, at + qr : at + qr + orows, :w] for d in range(n)], axis=0)
    return rq, ro


def got_mlp(pk, gr, dr, extra):
    n = pk.shape[0]
    half = 2 * pk.shape[2] // 3
    rgu = jnp.concatenate([pk[d, :gr, :] for d in range(n)], axis=0)
    rows = extra + dr
    low = rows // 3
    top = rows - low
    parts = []
    for d in range(n):
        if top > extra:
            parts.append(pk[d, gr + extra : gr + top, :half])
        parts.append(
            jnp.concatenate(
                [pk[d, gr : gr + low, half:], pk[d, gr + low : gr + 2 * low, half:]], axis=1
            )
        )
    return rgu, jnp.concatenate(parts, axis=0)


def norm_first_kernel(row_ref, side_ref, a0, a1, gain, n0, n1):
    for src, dst in ((a0, n0), (a1, n1)):
        v = jnp.concatenate([src[0, 0, 0], src[0, 0, 1]], axis=-1).astype(F32)
        inv = lax.rsqrt(jnp.mean(v * v, axis=-1, keepdims=True) + EPS)
        dst[0] = (v * inv * gain[...]).astype(BF16)


def attn_fwd_kernel(
    pack, row_ref, side_ref, n0, n1, wq, wk, wv, wo, pk, gq, gk, cos2, sin2, mask, p0, p1, qk_out, v_out, attn_out
):
    half = wq.shape[1]
    own, other = feature_cols(row_ref, half)
    qw = wq.shape[2]
    rq, ro = got_attn(pk, *pack)
    xo = both_halves(n0, n1, own)
    xt = both_halves(n0, n1, other)
    w_own = jnp.concatenate([wq[0], wk[0], wv[0]], axis=1)
    qkv = dot_nn(xo, w_own) + dot_nn(xt, rq)
    qk_out[0] = qkv[:, : qw + HD]
    v = qkv[:, qw + HD :].astype(BF16)
    v_out[0] = v
    c2 = cos2[0]
    s2 = sin2[0]
    k = qkv[:, qw : qw + HD]
    rot_k = rope_forward(k * head_inv(k) * gk[...], c2, s2).astype(BF16)
    allowed = mask[0] > 0
    parts = []
    for h in range(qw // HD):
        q = qkv[:, h * HD : (h + 1) * HD]
        rot_q = rope_forward(q * head_inv(q) * gq[...], c2, s2).astype(BF16)
        scores = dot_nt(rot_q, rot_k) * (1.0 / math.sqrt(HD))
        e = jnp.where(allowed, jnp.exp(scores), 0.0)
        total = jnp.sum(e, axis=-1, keepdims=True)
        probs = (e / total).astype(BF16)
        parts.append(dot_nn(probs, v).astype(BF16))
    attn = jnp.concatenate(parts, axis=1)
    attn_out[0] = attn
    hb = n0.shape[1]
    out_own = dot_nn(attn, wo[0]).astype(BF16)
    p0[0, :, own] = out_own[:hb]
    p1[0, :, own] = out_own[hb:]
    out_other = dot_nn(attn, ro).astype(BF16)
    p0[0, :, other] = out_other[:hb]
    p1[0, :, other] = out_other[hb:]


def mlp_fwd_kernel(pack, row_ref, side_ref, n0, n1, wg, wu, wd, pk, p0, p1, gu_out, h_out):
    half = wg.shape[1]
    ff = wg.shape[2]
    own, other = feature_cols(row_ref, half)
    rgu, rd = got_mlp(pk, *pack)
    xo = both_halves(n0, n1, own)
    xt = both_halves(n0, n1, other)
    w_own = jnp.concatenate([wg[0], wu[0]], axis=1)
    gu = dot_nn(xo, w_own) + dot_nn(xt, rgu)
    gu_out[0] = gu
    gate = gu[:, :ff]
    hidden = (gate * jax.nn.sigmoid(gate) * gu[:, ff:]).astype(BF16)
    h_out[0] = hidden
    hb = n0.shape[1]
    out_own = dot_nn(hidden, wd[0]).astype(BF16)
    p0[0, :, own] = out_own[:hb]
    p1[0, :, own] = out_own[hb:]
    out_other = dot_nn(hidden, rd).astype(BF16)
    p0[0, :, other] = out_other[:hb]
    p1[0, :, other] = out_other[hb:]


def mlp_bwd_kernel(pack, row_ref, side_ref, d0, d1, gu_in, wg, wu, wd, pk, p0, p1, dgu_out):
    half = wg.shape[1]
    ff = wg.shape[2]
    own, other = feature_cols(row_ref, half)
    rgu, rd = got_mlp(pk, *pack)
    do, dt = grad_halves(row_ref, d0, d1)
    d_hidden = dot_nt(do, wd[0]) + dot_nt(dt, rd)
    gate = gu_in[0, :, :ff]
    up = gu_in[0, :, ff:]
    sig = jax.nn.sigmoid(gate)
    d_gate = (d_hidden * up * sig * (1.0 + gate * (1.0 - sig))).astype(BF16)
    d_up = (d_hidden * gate * sig).astype(BF16)
    dgu = jnp.concatenate([d_gate, d_up], axis=1)
    dgu_out[0] = dgu
    hb = p0.shape[1]
    w_own = jnp.concatenate([wg[0], wu[0]], axis=1)
    out_own = dot_nt(dgu, w_own).astype(BF16)
    p0[0, :, own] = out_own[:hb]
    p1[0, :, own] = out_own[hb:]
    out_other = dot_nt(dgu, rgu).astype(BF16)
    p0[0, :, other] = out_other[:hb]
    p1[0, :, other] = out_other[hb:]


def attn_bwd_kernel(
    pack, row_ref, side_ref, d0, d1, qk_in, v_in, attn_in, wq, wk, wv, wo, pk, gq, gk, cos2, sin2, mask,
    *refs,
):
    if len(refs) > 4:
        n0, n1, p0, p1, dqkv_out, gain_out, ngain_out = refs
    else:
        p0, p1, dqkv_out, gain_out = refs
    half = wq.shape[1]
    qw = wq.shape[2]
    scale = 1.0 / math.sqrt(HD)
    own, other = feature_cols(row_ref, half)
    rq, ro = got_attn(pk, *pack)
    do, dt = grad_halves(row_ref, d0, d1)
    d_attn = (dot_nt(do, wo[0]) + dot_nt(dt, ro)).astype(BF16)
    c2 = cos2[0]
    s2 = sin2[0]
    v = v_in[0]
    k = qk_in[0, :, qw : qw + HD]
    inv_k = head_inv(k)
    rot_k = rope_forward(k * inv_k * gk[...], c2, s2).astype(BF16)
    allowed = mask[0] > 0
    d_v = None
    d_rk = None
    gain_q = None
    outs = []
    for h in range(qw // HD):
        cols = slice(h * HD, (h + 1) * HD)
        q = qk_in[0, :, cols]
        inv_q = head_inv(q)
        rot_q = rope_forward(q * inv_q * gq[...], c2, s2).astype(BF16)
        scores = dot_nt(rot_q, rot_k) * scale
        e = jnp.where(allowed, jnp.exp(scores), 0.0)
        p_full = e / jnp.sum(e, axis=-1, keepdims=True)
        da = d_attn[:, cols]
        delta = jnp.sum(
            da.astype(F32) * attn_in[0, :, cols].astype(F32), axis=-1, keepdims=True
        )
        d_probs = dot_nt(da, v)
        d_scores = (p_full * (d_probs - delta)).astype(BF16)
        dv_h = dot_tn(p_full.astype(BF16), da)
        drk_h = dot_tn(d_scores, rot_q) * scale
        d_v = dv_h if d_v is None else d_v + dv_h
        d_rk = drk_h if d_rk is None else d_rk + drk_h
        d_nq = rope_backward(dot_nn(d_scores, rot_k) * scale, c2, s2)
        gsum = jnp.sum(d_nq * q * inv_q, axis=0, keepdims=True)
        gain_q = gsum if gain_q is None else gain_q + gsum
        n = d_nq * gq[...]
        proj = jnp.mean(n * q, axis=-1, keepdims=True)
        outs.append((inv_q * n - q * (inv_q * inv_q * inv_q * proj)).astype(BF16))
    d_nk = rope_backward(d_rk, c2, s2)
    gain_k = jnp.sum(d_nk * k * inv_k, axis=0, keepdims=True)
    n = d_nk * gk[...]
    proj = jnp.mean(n * k, axis=-1, keepdims=True)
    outs.append((inv_k * n - k * (inv_k * inv_k * inv_k * proj)).astype(BF16))
    outs.append(d_v.astype(BF16))
    gain_out[0] = jnp.concatenate([gain_q, gain_k], axis=1)
    dqkv = jnp.concatenate(outs, axis=1)
    dqkv_out[0] = dqkv
    hb = p0.shape[1]
    w_own = jnp.concatenate([wq[0], wk[0], wv[0]], axis=1)
    out_own = dot_nt(dqkv, w_own)
    if len(refs) > 4:
        x = both_halves(n0, n1, own).astype(F32)
        ngain_out[0, :, own] = jnp.sum(out_own * x, axis=0, keepdims=True)
    out_own = out_own.astype(BF16)
    p0[0, :, own] = out_own[:hb]
    p1[0, :, own] = out_own[hb:]
    out_other = dot_nt(dqkv, rq)
    if len(refs) > 4:
        x = both_halves(n0, n1, other).astype(F32)
        ngain_out[0, :, other] = jnp.sum(out_other * x, axis=0, keepdims=True)
    out_other = out_other.astype(BF16)
    p0[0, :, other] = out_other[:hb]
    p1[0, :, other] = out_other[hb:]


def token_rows(ref0, ref1, cols):
    pieces = []
    for s in range(ref0.shape[0]):
        pieces.append(ref0[s, :, cols])
        pieces.append(ref1[s, :, cols])
    return jnp.concatenate(pieces, axis=0)


def flat_rows(ref):
    return jnp.concatenate([ref[s] for s in range(ref.shape[0])], axis=0)


def in_grads(row_ref, n0, n1, dy, out):
    n_dp = out.shape[0]
    half = n0.shape[2] // 2
    kb = half // n_dp
    for slot, cols in enumerate(feature_cols(row_ref, half)):
        g = dot_tn(token_rows(n0, n1, cols), dy).astype(BF16)
        for d in range(n_dp):
            out[d, slot * kb : (slot + 1) * kb, :] = g[d * kb : (d + 1) * kb]
    return 2 * kb


def out_grads(row_ref, d0, d1, own_ref, got_ref, out, at):
    per = out.shape[0] // 2
    r = row_ref[0]
    dcols = token_rows(d0, d1, feature_cols(row_ref, d0.shape[2] // 2)[0])
    for who, href in ((r, own_ref), (1 - r, got_ref)):
        g = dot_tn(flat_rows(href), dcols).astype(BF16)
        ub = g.shape[0] // per
        for j in range(per):
            out[who * per + j, at : at + ub, :] = g[j * ub : (j + 1) * ub]
    return at + ub


def wgrad_up_kernel(row_ref, side_ref, n0, n1, dgu, out):
    in_grads(row_ref, n0, n1, flat_rows(dgu), out)


def wgrad_down_kernel(row_ref, side_ref, d0, d1, h_own, h_rcv, held, out):
    kb = out.shape[1]
    half = kb * out.shape[0]
    rest = out.shape[2] - half
    per = out.shape[0] // 2
    r = row_ref[0]
    if len(d0.shape) == 3:
        dcols = token_rows(d0, d1, feature_cols(row_ref, half)[0])
    else:
        dcols = jnp.concatenate(
            [ref[s, 0, r] for s in range(d0.shape[0]) for ref in (d0, d1)], axis=0
        )
    for who, href in ((r, h_own), (1 - r, h_rcv)):
        g = dot_tn(flat_rows(href), dcols).astype(BF16)
        ub = g.shape[0] // per
        low = ub - kb
        for j in range(per):
            blk = g[j * ub : (j + 1) * ub]
            d = who * per + j
            out[d, :, :half] = blk[:kb]
            for m in range(half // rest):
                out[d, m * low : (m + 1) * low, half:] = blk[kb:, m * rest : (m + 1) * rest]


def wgrad_attn_kernel(row_ref, side_ref, n0, n1, dqkv, m0, m1, a_own, a_rcv, out):
    at = in_grads(row_ref, n0, n1, flat_rows(dqkv), out)
    out_grads(row_ref, m0, m1, a_own, a_rcv, out, at)


def finish_mlp_kernel(row_ref, side_ref, *refs):
    gate_out, up_out, down_out = refs[-3:]
    layers = gate_out.shape[0]
    kb = gate_out.shape[1]
    ff = gate_out.shape[2] // 2
    half = down_out.shape[2]
    low = down_out.shape[1] - kb
    own, other = feature_cols(row_ref, ff)
    for l in range(layers):
        z = refs[2 * l]
        got = refs[2 * l + 1]
        for ref, lo in ((gate_out, 0), (up_out, ff)):
            ref[l, :, own] = z[:kb, lo : lo + ff].astype(F32)
            ref[l, :, other] = got[:, lo : lo + ff].astype(F32)
        rest = z.shape[1] - half
        down_out[l, :kb, :] = z[2 * kb : 3 * kb, :half].astype(F32)
        for m in range(half // rest):
            down_out[l, kb:, m * rest : (m + 1) * rest] = z[
                2 * kb + m * low : 2 * kb + (m + 1) * low, half:
            ].astype(F32)


def finish_attn_kernel(row_ref, side_ref, *refs):
    q_out, k_out, v_out, o_out = refs[-4:]
    kb = q_out.shape[1]
    for l in range(q_out.shape[0]):
        z = refs[2 * l]
        got = refs[2 * l + 1]
        lo = 0
        for ref in (q_out, k_out, v_out):
            w = ref.shape[2] // 2
            own, other = feature_cols(row_ref, w)
            ref[l, :, own] = z[:kb, lo : lo + w].astype(F32)
            ref[l, :, other] = got[:, lo : lo + w].astype(F32)
            lo += w
        o_out[l] = z[2 * kb :, :].astype(F32)


def norm_fwd_kernel(row_ref, side_ref, x, t, gain, y_out, n_out):
    y = x[...]
    for i in range(t.shape[0]):
        y = y + t[i].astype(F32)
    y_out[...] = y
    inv = lax.rsqrt(jnp.mean(y * y, axis=-1, keepdims=True) + EPS)
    n_out[...] = (y * inv * gain[...]).astype(BF16)


def add_kernel(row_ref, side_ref, x, t, y_out):
    y = x[...]
    for i in range(t.shape[0]):
        y = y + t[i].astype(F32)
    y_out[...] = y


def norm_bwd_kernel(row_ref, side_ref, t, resid, d_res, gain, d_out, d_round, gain_out):
    dn = t[0].astype(F32)
    for i in range(1, t.shape[0]):
        dn = dn + t[i].astype(F32)
    x = resid[...]
    inv = lax.rsqrt(jnp.mean(x * x, axis=-1, keepdims=True) + EPS)
    gain_out[...] = jnp.sum(dn * x * inv, axis=0, keepdims=True)
    m = dn * gain[...]
    proj = jnp.mean(m * x, axis=-1, keepdims=True)
    d = d_res[...] + inv * m - x * (inv * inv * inv * proj)
    d_out[...] = d
    d_round[...] = d.astype(BF16)


def make_body(n_dp, n_row, n_col):
    pair = [(c, c ^ 1) for c in range(n_col)]
    swap = [(i, 1 - i) for i in range(n_row)]
    groups = [
        [c * n_row + i for c in range(k, n_col, 2) for i in range(n_row)] for k in range(2)
    ]
    plane = (COL, ROW)

    def gather_same(v):
        return lax.all_gather(v, plane, axis=0, tiled=False, axis_index_groups=groups)

    def other_core(v):
        return lax.ppermute(v, COL, pair)

    def other_row(v):
        return lax.ppermute(v, ROW, swap)

    def gather(v):
        own = gather_same(v).reshape(n_col // 2, n_row * v.shape[0], v.shape[1])
        return own, other_core(own)

    def scatter(p0, p1, late=None):
        blocks = (n_col // 2) * n_row
        width = p0.shape[2]
        sums = []
        for q0, q1 in ((p0, p1),) if late is None else ((p0, p1), late):
            got = other_core(q1)
            both = (q0.astype(F32) + got.astype(F32)).astype(BF16)
            sums.append(both.reshape(blocks, -1, width))
        both = sums[0] if late is None else jnp.concatenate(sums, axis=1)
        both = both.reshape(-1, width)
        moved = lax.all_to_all(both, plane, 0, 0, tiled=True, axis_index_groups=groups)
        return moved.reshape(blocks, -1, both.shape[1])

    def body(
        inputs, positions, segments, cotangent, w_query, w_key, w_value, w_output,
        w_gate, w_up, w_down, attn_gain, mlp_gain, query_gain, key_gain,
    ):
        layers = w_query.shape[0]
        half = inputs.shape[1]
        width = half * n_row
        tok_c = inputs.shape[0]
        tok = tok_c // n_row
        n_seq = n_col // 2
        r = lax.axis_index(ROW)
        c = lax.axis_index(COL)
        core = c % 2
        seq_id = c // 2
        row = (jnp.reshape(r, (1,)).astype(jnp.int32), jnp.reshape(core, (1,)).astype(jnp.int32))
        qw = w_query.shape[2] // n_row
        kw = w_key.shape[2] // n_row
        ow = w_output.shape[1] // n_row
        ff = w_gate.shape[2] // n_row

        ps = jnp.concatenate([positions, segments], axis=0)
        ps_other = other_row(ps)
        ps_all = jnp.stack([jnp.where(r == 0, ps, ps_other), jnp.where(r == 0, ps_other, ps)])

        def cut(w, axis, size, start):
            return lax.dynamic_slice_in_dim(w, start * size, size, axis)

        away = 1 - r
        dpi = lax.axis_index(DP)

        def piece(v):
            rows = v.shape[0] // n_dp
            return lax.dynamic_slice_in_dim(v, dpi * rows, rows, 0)

        def send_qkv(l):
            return jnp.concatenate(
                [
                    cut(w_query[l], 1, qw, away),
                    cut(w_key[l], 1, kw, away),
                    cut(w_value[l], 1, kw, away),
                ],
                axis=1,
            )

        def send_o(l):
            return cut(w_output[l], 0, ow, away)

        def send_mlp(l, lead):
            gu = jnp.concatenate(
                [piece(cut(w_gate[l], 1, ff, away)), piece(cut(w_up[l], 1, ff, away))], axis=1
            )
            rest = jnp.concatenate(lead + [piece(cut(w_down[l], 0, ff, away))], axis=0)
            low = rest.shape[0] // 3
            top = rest.shape[0] - low
            w = half // 2
            side = jnp.concatenate([rest[top:, :w], rest[top:, w:]], axis=0)
            return jnp.concatenate([gu, jnp.concatenate([rest[:top], side], axis=1)], axis=0)

        raw = lax.all_gather(inputs, plane, axis=0, tiled=False).reshape(
            n_seq, 2, n_row, tok_c, half
        )
        pk_attn, pk_mlp = [], []
        attn_pack = (half, ow, 0, half)
        mlp_pack = (half // n_dp, ff // n_dp, 0)
        for l in range(layers):
            pk_attn.append(other_row(jnp.concatenate([send_qkv(l), send_o(l)], axis=0))[None])
            got = other_row(send_mlp(l, []))
            pk_mlp.append(lax.all_gather(got, DP, axis=0, tiled=False))

        cot_all = lax.all_gather(cotangent, plane, axis=0, tiled=False).reshape(
            n_seq, 2, n_row, tok_c, half
        )

        order = jnp.concatenate(
            [jnp.arange(tok_c) + core * tok_c, jnp.arange(tok_c) + (1 - core) * tok_c]
        )
        turned = jnp.where(core == 0, ps_all, jnp.roll(ps_all, tok_c, axis=2))
        freq = THETA ** (-2.0 * jnp.arange(HD // 2, dtype=F32) / HD)
        angles = turned[:, 0, :].astype(F32)[:, :, None] * freq[None, None, :]
        cos = jnp.cos(angles)
        sin = jnp.sin(angles)
        cos2 = jnp.concatenate([cos, cos], axis=-1)
        sin2 = jnp.concatenate([-sin, sin], axis=-1)
        seg = turned[:, 1, :]
        mask = (
            (seg[:, :, None] == seg[:, None, :]) & (order[None, None, :] <= order[None, :, None])
        ).astype(F32)

        gq = query_gain[:, None, :]
        gk = key_gain[:, None, :]
        ga = attn_gain[:, None, :]
        gm = mlp_gain[:, None, :]

        full = (n_seq, tok_c, width)
        nt = n_seq * SEQ
        wq_spec = lambda l: pl.BlockSpec((1, half, qw), lambda i, s, t: (l, 0, s[0]))
        wk_spec = lambda l: pl.BlockSpec((1, half, kw), lambda i, s, t: (l, 0, s[0]))
        wo_spec = lambda l: pl.BlockSpec((1, ow, half), lambda i, s, t: (l, s[0], 0))
        wg_spec = lambda l: pl.BlockSpec((1, half, ff), lambda i, s, t: (l, 0, s[0]))
        wd_spec = lambda l: pl.BlockSpec((1, ff, half), lambda i, s, t: (l, s[0], 0))
        q3 = qw + 2 * kw
        tables = [per_seq((n_seq, SEQ, HD)), per_seq((n_seq, SEQ, HD)), per_seq((n_seq, SEQ, SEQ))]

        def qkv_specs(l):
            return [
                wq_spec(l), wk_spec(l), wk_spec(l), wo_spec(l), whole(pk_attn[l].shape),
                whole((1, HD)), whole((1, HD)),
            ] + tables

        def qkv_args(l):
            return [
                w_query, w_key, w_value, w_output, pk_attn[l], gq[l], gk[l],
                cos2, sin2, mask,
            ]

        def mlp_specs(l):
            return [wg_spec(l), wg_spec(l), wd_spec(l), whole(pk_mlp[l].shape)]

        def mlp_args(l):
            return [w_gate, w_up, w_down, pk_mlp[l]]

        def attn_fwd(l, n0, n1):
            return call(
                functools.partial(attn_fwd_kernel, attn_pack), (n_seq,),
                [per_seq(full), per_seq(full)] + qkv_specs(l),
                [per_seq(full), per_seq(full), per_seq((n_seq, SEQ, qw + kw)),
                 per_seq((n_seq, SEQ, kw)), per_seq((n_seq, SEQ, qw))],
                [sds(full, BF16), sds(full, BF16), sds((n_seq, SEQ, qw + kw), F32),
                 sds((n_seq, SEQ, kw), BF16), sds((n_seq, SEQ, qw), BF16)],
                2 * nt * width * (q3 + qw), 6e6, row, [n0, n1] + qkv_args(l),
            )

        def mlp_fwd(l, n0, n1):
            return call(
                functools.partial(mlp_fwd_kernel, mlp_pack), (n_seq,),
                [per_seq(full), per_seq(full)] + mlp_specs(l),
                [per_seq(full), per_seq(full), per_seq((n_seq, SEQ, 2 * ff)),
                 per_seq((n_seq, SEQ, ff))],
                [sds(full, BF16), sds(full, BF16), sds((n_seq, SEQ, 2 * ff), F32),
                 sds((n_seq, SEQ, ff), BF16)],
                6 * nt * width * ff, 8e6, row, [n0, n1] + mlp_args(l),
            )

        def mlp_bwd(l, d0, d1, gu):
            return call(
                functools.partial(mlp_bwd_kernel, mlp_pack), (n_seq,),
                grad_specs(l)[0] + [per_seq((n_seq, SEQ, 2 * ff))] + mlp_specs(l),
                [per_seq(full), per_seq(full), per_seq((n_seq, SEQ, 2 * ff))],
                [sds(full, BF16), sds(full, BF16), sds((n_seq, SEQ, 2 * ff), BF16)],
                6 * nt * width * ff, 8e6, row, [d0, d1, gu] + mlp_args(l),
            )

        def attn_bwd(l, d0, d1, qk, v, attn, normed=()):
            specs = [per_seq(full), per_seq(full), per_seq((n_seq, SEQ, q3)),
                     per_seq((n_seq, 1, 2 * HD))]
            shapes = [sds(full, BF16), sds(full, BF16), sds((n_seq, SEQ, q3), BF16),
                      sds((n_seq, 1, 2 * HD), F32)]
            if normed:
                specs.append(per_seq((n_seq, 1, width)))
                shapes.append(sds((n_seq, 1, width), F32))
            return call(
                functools.partial(attn_bwd_kernel, attn_pack), (n_seq,),
                [per_seq(full), per_seq(full), per_seq((n_seq, SEQ, qw + kw)),
                 per_seq((n_seq, SEQ, kw)), per_seq((n_seq, SEQ, qw))] + qkv_specs(l)
                + [per_seq(full) for _ in normed],
                specs, shapes, 2 * nt * width * (q3 + qw), 8e6, row,
                [d0, d1, qk, v, attn] + qkv_args(l) + list(normed),
            )

        def wgrad(kernel, rows, cols, args):
            return call(
                kernel, (1,), [whole(a.shape) for a in args],
                whole((n_dp, rows, cols)), sds((n_dp, rows, cols), BF16),
                2 * nt * n_dp * rows * cols, 8e6, row, args,
            )

        def norm_fwd(x, t, gain):
            return call(
                norm_fwd_kernel, (1,), [whole(x.shape), whole(t.shape), whole(gain.shape)],
                [whole(x.shape), whole(x.shape)], [sds(x.shape, F32), sds(x.shape, BF16)],
                1e5, 1e6, row, [x, t, gain],
            )

        def norm_bwd(t, resid, d_res, gain):
            return call(
                norm_bwd_kernel, (1,),
                [part_of(0), whole(resid.shape), whole(d_res.shape), whole(gain.shape)],
                [whole(resid.shape), whole(resid.shape), whole(gain.shape)],
                [sds(resid.shape, F32), sds(resid.shape, BF16), sds(gain.shape, F32)],
                1e5, 1e6, row, [t, resid, d_res, gain],
            )

        def own_tokens(blocks):
            mine = lax.dynamic_slice_in_dim(blocks, r * tok, tok, 1)
            return jnp.concatenate([mine[i] for i in range(n_row)], axis=-1).astype(F32)

        def own_block(blocks):
            mine = lax.dynamic_index_in_dim(blocks, seq_id, 0, keepdims=False)
            return own_tokens(lax.dynamic_index_in_dim(mine, core, 0, keepdims=False))

        x = own_block(raw)
        raw_shape = (1, 1, n_row, tok_c, half)
        normed = call(
            norm_first_kernel, (n_seq,),
            [
                pl.BlockSpec(raw_shape, lambda i, s, t: (i, t[0], 0, 0, 0)),
                pl.BlockSpec(raw_shape, lambda i, s, t: (i, 1 - t[0], 0, 0, 0)),
                whole((1, width)),
            ],
            [per_seq(full), per_seq(full)], [sds(full, BF16), sds(full, BF16)],
            1e6, 4e6, row, [raw, raw, ga[0]],
        )

        saved = []
        for l in range(layers):
            n1_own, n1_oth = normed
            p0, p1, qk, v, attn = attn_fwd(l, n1_own, n1_oth)
            middle, n2 = norm_fwd(x, scatter(p0, p1), gm[l])
            n2_own, n2_oth = gather(n2)
            p0, p1, gu, hidden = mlp_fwd(l, n2_own, n2_oth)
            saved.append((x, n1_own, n1_oth, qk, v, attn, middle, n2_own, n2_oth, gu, hidden))
            if l + 1 < layers:
                moved = scatter(p0, p1)
                x, nxt = norm_fwd(middle, moved, ga[l + 1])
                normed = gather(nxt)
            else:
                last_p = (p0, p1)
                last_mid = middle

        def to_block(v):
            v = v.astype(F32)
            halves = [v[:, i * half : (i + 1) * half] for i in range(n_row)]
            mine = jnp.where(r == 0, halves[0], halves[1])
            got = other_row(jnp.where(r == 0, halves[1], halves[0]))
            return jnp.where(
                r == 0, jnp.concatenate([mine, got], 0), jnp.concatenate([got, mine], 0)
            )

        def part_of(j):
            return pl.BlockSpec((n_seq * n_row, tok, width), lambda *_: (0, j, 0))

        d0 = d1 = cot_all

        def grad_specs(l):
            if l + 1 < layers:
                return [per_seq(full), per_seq(full)], [whole(full), whole(full)]
            one, every = (1, 1, n_row, tok_c, half), (n_seq, 1, n_row, tok_c, half)
            return (
                [
                    pl.BlockSpec(one, lambda i, s, t: (i, t[0], 0, 0, 0)),
                    pl.BlockSpec(one, lambda i, s, t: (i, 1 - t[0], 0, 0, 0)),
                ],
                [
                    pl.BlockSpec(every, lambda i, s, t: (0, t[0], 0, 0, 0)),
                    pl.BlockSpec(every, lambda i, s, t: (0, 1 - t[0], 0, 0, 0)),
                ],
            )

        d_own = own_block(cot_all)
        kb = half // n_dp
        mlp_red = [None] * layers
        attn_red = [None] * layers
        g_attn = [None] * layers
        g_mlp = [None] * layers
        g_head = [None] * layers
        for l in reversed(range(layers)):
            xin, n1_own, n1_oth, qk, v, attn, middle, n2_own, n2_oth, gu, hidden = saved[l]
            o0, o1 = d0, d1
            p0, p1, dgu = mlp_bwd(l, d0, d1, gu)
            h_got = other_row(hidden)
            a_got = other_row(attn)
            args = [n2_own, n2_oth, dgu]
            part_shape = (n_dp, 3 * kb, 2 * ff)
            part = call(
                wgrad_up_kernel, (1,), [whole(a.shape) for a in args],
                pl.BlockSpec((n_dp, 2 * kb, 2 * ff), lambda i, s, t: (0, 0, 0)),
                sds(part_shape, BF16), 8 * nt * half * ff, 4e6, row, args,
            )
            args = [o0, o1, hidden, h_got]
            part = call(
                wgrad_down_kernel, (1,),
                grad_specs(l)[1] + [whole(hidden.shape)] * 2 + [pl.BlockSpec(memory_space=pl.ANY)],
                pl.BlockSpec((n_dp, kb, 2 * ff), lambda i, s, t: (0, 2, 0)),
                sds(part_shape, BF16), 4 * nt * half * ff, 4e6, row, args + [part],
                alias={len(args) + 2: 0},
            )
            moved = scatter(p0, p1)
            mlp_red[l] = lax.psum_scatter(part, DP, scatter_dimension=0, tiled=False)
            d_mid, d_mid_round, g_mlp[l] = norm_bwd(moved, middle, d_own, gm[l])
            d0, d1 = gather(d_mid_round)
            got = attn_bwd(l, d0, d1, qk, v, attn, (n1_own, n1_oth) if l == 0 else ())
            p0, p1, dqkv, g_head[l] = got[:4]
            part = wgrad(
                wgrad_attn_kernel, 3 * kb, q3,
                [n1_own, n1_oth, dqkv, d0, d1, attn, a_got],
            )
            moved = scatter(p0, p1, last_p if l == 0 else None)
            attn_red[l] = lax.psum_scatter(part, DP, scatter_dimension=0, tiled=False)
            d_own, d_round, g_attn[l] = norm_bwd(moved, xin, d_mid, ga[l])
            if l == 0:
                g_attn[l] = jnp.sum(got[4], axis=0) / ga[l]
                x = call(
                    add_kernel, (1,), [whole(last_mid.shape), part_of(1)],
                    whole(last_mid.shape), sds(last_mid.shape, F32), 1e5, 1e6, row,
                    [last_mid, moved],
                )
                outputs = to_block(x)
            if l > 0:
                d0, d1 = gather(d_round)
        d_inputs = to_block(d_own)

        gains = jnp.concatenate(
            [g.reshape(-1) for g in g_attn]
            + [g.reshape(-1) for g in g_mlp]
            + [jnp.sum(g, axis=0).reshape(-1) for g in g_head]
        )
        gains = gains.reshape(-1, HD)
        for axis, size in ((COL, n_col), (ROW, n_row), (DP, n_dp)):
            step = 1
            while step < size:
                peers = [(i, i ^ step) for i in range(size)]
                gains = gains + lax.ppermute(gains, axis, peers)
                step *= 2
        gains = gains.reshape(-1)
        lw = layers * width
        ga_out = gains[:lw].reshape(layers, width)
        gm_out = gains[lw : 2 * lw].reshape(layers, width)
        gh = gains[2 * lw :].reshape(layers, 2, HD)

        def finish(kernel, reds, shapes):
            args = []
            for z in reds:
                args += [z, other_row(z[kb : 2 * kb])]
            return call(
                kernel, (1,), [whole(a.shape) for a in args],
                [whole(o) for o in shapes], [sds(o, F32) for o in shapes], 1e5, 8e6, row, args,
            )

        g_gate, g_up, g_down = finish(
            finish_mlp_kernel, mlp_red,
            [(layers, kb, 2 * ff), (layers, kb, 2 * ff), (layers, 2 * ff // n_dp, half)],
        )
        g_q, g_k, g_v, g_o = finish(
            finish_attn_kernel, attn_red,
            [(layers, kb, 2 * qw), (layers, kb, 2 * kw), (layers, kb, 2 * kw),
             (layers, 2 * ow // n_dp, half)],
        )
        stacked = (g_q, g_k, g_v, g_o, g_gate, g_up, g_down)
        return (
            outputs, d_inputs, *stacked, ga_out, gm_out, gh[:, 0], gh[:, 1],
        )

    return body


def solution(mesh):
    body = make_body(mesh.shape[DP], mesh.shape[ROW], mesh.shape[COL])
    act = P((DP, COL), ROW)
    seq = P((DP, ROW), None)
    w_in = P(None, ROW, COL)
    w_out = P(None, COL, ROW)
    g_in = P(None, (ROW, DP), COL)
    g_out = P(None, (COL, DP), ROW)

    return jax.shard_map(
        body,
        mesh=mesh,
        in_specs=(
            act, seq, seq, act, w_in, w_in, w_in, w_out, w_in, w_in, w_out, P(), P(), P(), P(),
        ),
        out_specs=(
            act, act, g_in, g_in, g_in, g_out, g_in, g_in, g_out, P(), P(), P(), P(),
        ),
        check_vma=False,
    )
```

```python
import functools
import math

import jax
import jax.numpy as jnp
from jax import lax
from jax.experimental import pallas as pl
from jax.experimental.pallas import tpu as pltpu
from jax.sharding import PartitionSpec as P


HD = 128
SEQ = 256
EPS = 1e-06
THETA = 1000000.0
F32 = jnp.float32
BF16 = jnp.bfloat16
DP = "dp"
ROW = "row"
COL = "col"


def dot_nn(a, b):
    return jnp.dot(a, b, preferred_element_type=F32)


def dot_nt(a, b):
    return lax.dot_general(a, b, (((1,), (1,)), ((), ())), preferred_element_type=F32)


def dot_tn(a, b):
    return lax.dot_general(a, b, (((0,), (0,)), ((), ())), preferred_element_type=F32)


def whole(shape):
    rank = len(shape)
    return pl.BlockSpec(tuple(shape), lambda *_: (0,) * rank)


def per_seq(shape):
    rest = len(shape) - 1
    return pl.BlockSpec((1,) + tuple(shape[1:]), lambda i, *_: (i,) + (0,) * rest)


def sds(shape, dtype):
    return jax.ShapeDtypeStruct(tuple(shape), dtype)


def call(kernel, grid, in_specs, out_specs, out_shape, flops, nbytes, row, args, alias=None):
    return pl.pallas_call(
        kernel,
        grid_spec=pltpu.PrefetchScalarGridSpec(
            num_scalar_prefetch=2,
            grid=grid,
            in_specs=in_specs,
            out_specs=out_specs,
        ),
        out_shape=out_shape,
        input_output_aliases=alias or {},
        cost_estimate=pl.CostEstimate(
            flops=int(flops), bytes_accessed=int(nbytes), transcendentals=0
        ),
    )(*row, *args)


def grad_halves(row_ref, ref0, ref1):
    r = row_ref[0]
    if len(ref0.shape) == 3:
        return [both_halves(ref0, ref1, cols) for cols in feature_cols(row_ref, ref0.shape[2] // 2)]
    return [jnp.concatenate([ref0[0, 0, i], ref1[0, 0, i]], axis=0) for i in (r, 1 - r)]


def small_call(kernel, out_shape, args):
    spec = pl.BlockSpec(memory_space=pltpu.VMEM)
    nbytes = sum(a.size * a.dtype.itemsize for a in args)
    return pl.pallas_call(
        kernel,
        in_specs=[spec] * len(args),
        out_specs=[spec] * len(out_shape),
        out_shape=out_shape,
        cost_estimate=pl.CostEstimate(
            flops=int(1e5), bytes_accessed=int(nbytes), transcendentals=0
        ),
    )(*args)


def both_halves(ref0, ref1, cols):
    return jnp.concatenate([ref0[0, :, cols], ref1[0, :, cols]], axis=0)


def rope_forward(v, cos2, sin2):
    return v * cos2 + pltpu.roll(v, v.shape[-1] // 2, 1) * sin2


def rope_backward(v, cos2, sin2):
    return v * cos2 - pltpu.roll(v, v.shape[-1] // 2, 1) * sin2


def head_inv(v):
    return lax.rsqrt(jnp.mean(v * v, axis=-1, keepdims=True) + EPS)


def feature_cols(row_ref, width):
    r = row_ref[0]
    own = pl.ds(pl.multiple_of(r * width, width), width)
    other = pl.ds(pl.multiple_of((1 - r) * width, width), width)
    return own, other


def got_attn(pk, qr, orows, at, w):
    n = pk.shape[0]
    rq = jnp.concatenate([pk[d, at : at + qr, :w] for d in range(n)], axis=0)
    ro = jnp.concatenate([pk[d, at + qr : at + qr + orows, :w] for d in range(n)], axis=0)
    return rq, ro


def got_mlp(pk, gr, dr, extra):
    n = pk.shape[0]
    half = 2 * pk.shape[2] // 3
    rgu = jnp.concatenate([pk[d, :gr, :] for d in range(n)], axis=0)
    rows = extra + dr
    low = rows // 3
    top = rows - low
    parts = []
    for d in range(n):
        if top > extra:
            parts.append(pk[d, gr + extra : gr + top, :half])
        parts.append(
            jnp.concatenate(
                [pk[d, gr : gr + low, half:], pk[d, gr + low : gr + 2 * low, half:]], axis=1
            )
        )
    return rgu, jnp.concatenate(parts, axis=0)


def norm_first_kernel(row_ref, side_ref, a0, a1, gain, n0, n1):
    for src, dst in ((a0, n0), (a1, n1)):
        v = jnp.concatenate([src[0, 0, 0], src[0, 0, 1]], axis=-1).astype(F32)
        inv = lax.rsqrt(jnp.mean(v * v, axis=-1, keepdims=True) + EPS)
        dst[0] = (v * inv * gain[...]).astype(BF16)


def attn_fwd_kernel(
    pack, row_ref, side_ref, n0, n1, wq, wk, wv, wo, pk, gq, gk, cos2, sin2, mask, p0, p1, qk_out, v_out, attn_out
):
    half = wq.shape[1]
    own, other = feature_cols(row_ref, half)
    qw = wq.shape[2]
    rq, ro = got_attn(pk, *pack)
    xo = both_halves(n0, n1, own)
    xt = both_halves(n0, n1, other)
    w_own = jnp.concatenate([wq[0], wk[0], wv[0]], axis=1)
    qkv = dot_nn(xo, w_own) + dot_nn(xt, rq)
    qk_out[0] = qkv[:, : qw + HD]
    v = qkv[:, qw + HD :].astype(BF16)
    v_out[0] = v
    c2 = cos2[0]
    s2 = sin2[0]
    k = qkv[:, qw : qw + HD]
    rot_k = rope_forward(k * head_inv(k) * gk[...], c2, s2).astype(BF16)
    allowed = mask[0] > 0
    parts = []
    for h in range(qw // HD):
        q = qkv[:, h * HD : (h + 1) * HD]
        rot_q = rope_forward(q * head_inv(q) * gq[...], c2, s2).astype(BF16)
        scores = dot_nt(rot_q, rot_k) * (1.0 / math.sqrt(HD))
        e = jnp.where(allowed, jnp.exp(scores), 0.0)
        total = jnp.sum(e, axis=-1, keepdims=True)
        probs = (e / total).astype(BF16)
        parts.append(dot_nn(probs, v).astype(BF16))
    attn = jnp.concatenate(parts, axis=1)
    attn_out[0] = attn
    hb = n0.shape[1]
    out_own = dot_nn(attn, wo[0]).astype(BF16)
    p0[0, :, own] = out_own[:hb]
    p1[0, :, own] = out_own[hb:]
    out_other = dot_nn(attn, ro).astype(BF16)
    p0[0, :, other] = out_other[:hb]
    p1[0, :, other] = out_other[hb:]


def mlp_fwd_kernel(pack, row_ref, side_ref, n0, n1, wg, wu, wd, pk, p0, p1, gu_out, h_out):
    half = wg.shape[1]
    ff = wg.shape[2]
    own, other = feature_cols(row_ref, half)
    rgu, rd = got_mlp(pk, *pack)
    xo = both_halves(n0, n1, own)
    xt = both_halves(n0, n1, other)
    w_own = jnp.concatenate([wg[0], wu[0]], axis=1)
    gu = dot_nn(xo, w_own) + dot_nn(xt, rgu)
    gu_out[0] = gu
    gate = gu[:, :ff]
    hidden = (gate * jax.nn.sigmoid(gate) * gu[:, ff:]).astype(BF16)
    h_out[0] = hidden
    hb = n0.shape[1]
    out_own = dot_nn(hidden, wd[0]).astype(BF16)
    p0[0, :, own] = out_own[:hb]
    p1[0, :, own] = out_own[hb:]
    out_other = dot_nn(hidden, rd).astype(BF16)
    p0[0, :, other] = out_other[:hb]
    p1[0, :, other] = out_other[hb:]


def mlp_bwd_kernel(pack, row_ref, side_ref, d0, d1, gu_in, wg, wu, wd, pk, p0, p1, dgu_out):
    half = wg.shape[1]
    ff = wg.shape[2]
    own, other = feature_cols(row_ref, half)
    rgu, rd = got_mlp(pk, *pack)
    do, dt = grad_halves(row_ref, d0, d1)
    d_hidden = dot_nt(do, wd[0]) + dot_nt(dt, rd)
    gate = gu_in[0, :, :ff]
    up = gu_in[0, :, ff:]
    sig = jax.nn.sigmoid(gate)
    d_gate = (d_hidden * up * sig * (1.0 + gate * (1.0 - sig))).astype(BF16)
    d_up = (d_hidden * gate * sig).astype(BF16)
    dgu = jnp.concatenate([d_gate, d_up], axis=1)
    dgu_out[0] = dgu
    hb = p0.shape[1]
    w_own = jnp.concatenate([wg[0], wu[0]], axis=1)
    out_own = dot_nt(dgu, w_own).astype(BF16)
    p0[0, :, own] = out_own[:hb]
    p1[0, :, own] = out_own[hb:]
    out_other = dot_nt(dgu, rgu).astype(BF16)
    p0[0, :, other] = out_other[:hb]
    p1[0, :, other] = out_other[hb:]


def attn_bwd_kernel(
    pack, row_ref, side_ref, d0, d1, qk_in, v_in, attn_in, wq, wk, wv, wo, pk, gq, gk, cos2, sin2, mask,
    *refs,
):
    if len(refs) > 4:
        n0, n1, p0, p1, dqkv_out, gain_out, ngain_out = refs
    else:
        p0, p1, dqkv_out, gain_out = refs
    half = wq.shape[1]
    qw = wq.shape[2]
    scale = 1.0 / math.sqrt(HD)
    own, other = feature_cols(row_ref, half)
    rq, ro = got_attn(pk, *pack)
    do, dt = grad_halves(row_ref, d0, d1)
    d_attn = (dot_nt(do, wo[0]) + dot_nt(dt, ro)).astype(BF16)
    c2 = cos2[0]
    s2 = sin2[0]
    v = v_in[0]
    k = qk_in[0, :, qw : qw + HD]
    inv_k = head_inv(k)
    rot_k = rope_forward(k * inv_k * gk[...], c2, s2).astype(BF16)
    allowed = mask[0] > 0
    d_v = None
    d_rk = None
    gain_q = None
    outs = []
    for h in range(qw // HD):
        cols = slice(h * HD, (h + 1) * HD)
        q = qk_in[0, :, cols]
        inv_q = head_inv(q)
        rot_q = rope_forward(q * inv_q * gq[...], c2, s2).astype(BF16)
        scores = dot_nt(rot_q, rot_k) * scale
        e = jnp.where(allowed, jnp.exp(scores), 0.0)
        p_full = e / jnp.sum(e, axis=-1, keepdims=True)
        da = d_attn[:, cols]
        delta = jnp.sum(
            da.astype(F32) * attn_in[0, :, cols].astype(F32), axis=-1, keepdims=True
        )
        d_probs = dot_nt(da, v)
        d_scores = (p_full * (d_probs - delta)).astype(BF16)
        dv_h = dot_tn(p_full.astype(BF16), da)
        drk_h = dot_tn(d_scores, rot_q) * scale
        d_v = dv_h if d_v is None else d_v + dv_h
        d_rk = drk_h if d_rk is None else d_rk + drk_h
        d_nq = rope_backward(dot_nn(d_scores, rot_k) * scale, c2, s2)
        gsum = jnp.sum(d_nq * q * inv_q, axis=0, keepdims=True)
        gain_q = gsum if gain_q is None else gain_q + gsum
        n = d_nq * gq[...]
        proj = jnp.mean(n * q, axis=-1, keepdims=True)
        outs.append((inv_q * n - q * (inv_q * inv_q * inv_q * proj)).astype(BF16))
    d_nk = rope_backward(d_rk, c2, s2)
    gain_k = jnp.sum(d_nk * k * inv_k, axis=0, keepdims=True)
    n = d_nk * gk[...]
    proj = jnp.mean(n * k, axis=-1, keepdims=True)
    outs.append((inv_k * n - k * (inv_k * inv_k * inv_k * proj)).astype(BF16))
    outs.append(d_v.astype(BF16))
    gain_out[0] = jnp.concatenate([gain_q, gain_k], axis=1)
    dqkv = jnp.concatenate(outs, axis=1)
    dqkv_out[0] = dqkv
    hb = p0.shape[1]
    w_own = jnp.concatenate([wq[0], wk[0], wv[0]], axis=1)
    out_own = dot_nt(dqkv, w_own)
    if len(refs) > 4:
        x = both_halves(n0, n1, own).astype(F32)
        ngain_out[0, :, own] = jnp.sum(out_own * x, axis=0, keepdims=True)
    out_own = out_own.astype(BF16)
    p0[0, :, own] = out_own[:hb]
    p1[0, :, own] = out_own[hb:]
    out_other = dot_nt(dqkv, rq)
    if len(refs) > 4:
        x = both_halves(n0, n1, other).astype(F32)
        ngain_out[0, :, other] = jnp.sum(out_other * x, axis=0, keepdims=True)
    out_other = out_other.astype(BF16)
    p0[0, :, other] = out_other[:hb]
    p1[0, :, other] = out_other[hb:]


def token_rows(ref0, ref1, cols):
    pieces = []
    for s in range(ref0.shape[0]):
        pieces.append(ref0[s, :, cols])
        pieces.append(ref1[s, :, cols])
    return jnp.concatenate(pieces, axis=0)


def flat_rows(ref):
    return jnp.concatenate([ref[s] for s in range(ref.shape[0])], axis=0)


def in_grads(row_ref, n0, n1, dy, out):
    n_dp = out.shape[0]
    half = n0.shape[2] // 2
    kb = half // n_dp
    for slot, cols in enumerate(feature_cols(row_ref, half)):
        g = dot_tn(token_rows(n0, n1, cols), dy).astype(BF16)
        for d in range(n_dp):
            out[d, slot * kb : (slot + 1) * kb, :] = g[d * kb : (d + 1) * kb]
    return 2 * kb


def out_grads(row_ref, d0, d1, own_ref, got_ref, out, at):
    per = out.shape[0] // 2
    r = row_ref[0]
    dcols = token_rows(d0, d1, feature_cols(row_ref, d0.shape[2] // 2)[0])
    for who, href in ((r, own_ref), (1 - r, got_ref)):
        g = dot_tn(flat_rows(href), dcols).astype(BF16)
        ub = g.shape[0] // per
        for j in range(per):
            out[who * per + j, at : at + ub, :] = g[j * ub : (j + 1) * ub]
    return at + ub


def wgrad_up_kernel(row_ref, side_ref, n0, n1, dgu, out):
    in_grads(row_ref, n0, n1, flat_rows(dgu), out)


def wgrad_down_kernel(row_ref, side_ref, d0, d1, h_own, h_rcv, held, out):
    kb = out.shape[1]
    half = kb * out.shape[0]
    rest = out.shape[2] - half
    per = out.shape[0] // 2
    r = row_ref[0]
    if len(d0.shape) == 3:
        dcols = token_rows(d0, d1, feature_cols(row_ref, half)[0])
    else:
        dcols = jnp.concatenate(
            [ref[s, 0, r] for s in range(d0.shape[0]) for ref in (d0, d1)], axis=0
        )
    for who, href in ((r, h_own), (1 - r, h_rcv)):
        g = dot_tn(flat_rows(href), dcols).astype(BF16)
        ub = g.shape[0] // per
        low = ub - kb
        for j in range(per):
            blk = g[j * ub : (j + 1) * ub]
            d = who * per + j
            out[d, :, :half] = blk[:kb]
            for m in range(half // rest):
                out[d, m * low : (m + 1) * low, half:] = blk[kb:, m * rest : (m + 1) * rest]


def wgrad_attn_kernel(row_ref, side_ref, n0, n1, dqkv, m0, m1, a_own, a_rcv, out):
    at = in_grads(row_ref, n0, n1, flat_rows(dqkv), out)
    out_grads(row_ref, m0, m1, a_own, a_rcv, out, at)


def finish_mlp_kernel(row_ref, side_ref, *refs):
    gate_out, up_out, down_out = refs[-3:]
    layers = gate_out.shape[0]
    kb = gate_out.shape[1]
    ff = gate_out.shape[2] // 2
    half = down_out.shape[2]
    low = down_out.shape[1] - kb
    own, other = feature_cols(row_ref, ff)
    for l in range(layers):
        z = refs[2 * l]
        got = refs[2 * l + 1]
        for ref, lo in ((gate_out, 0), (up_out, ff)):
            ref[l, :, own] = z[:kb, lo : lo + ff].astype(F32)
            ref[l, :, other] = got[:, lo : lo + ff].astype(F32)
        rest = z.shape[1] - half
        down_out[l, :kb, :] = z[2 * kb : 3 * kb, :half].astype(F32)
        for m in range(half // rest):
            down_out[l, kb:, m * rest : (m + 1) * rest] = z[
                2 * kb + m * low : 2 * kb + (m + 1) * low, half:
            ].astype(F32)


def finish_attn_kernel(row_ref, side_ref, *refs):
    q_out, k_out, v_out, o_out = refs[-4:]
    kb = q_out.shape[1]
    for l in range(q_out.shape[0]):
        z = refs[0] if l == 0 else refs[2 * l - 1]
        lo = 0
        for ref in (q_out, k_out, v_out):
            w = ref.shape[2] // 2
            own, other = feature_cols(row_ref, w)
            ref[l, :, own] = z[:kb, lo : lo + w].astype(F32)
            if l > 0:
                ref[l, :, other] = refs[2 * l][:, lo : lo + w].astype(F32)
            lo += w
        o_out[l] = z[2 * kb :, :].astype(F32)


def finish_last_kernel(row_ref, side_ref, got, q_in, k_in, v_in, q_out, k_out, v_out):
    lo = 0
    for ref in (q_out, k_out, v_out):
        w = ref.shape[2]
        ref[0] = got[:, lo : lo + w].astype(F32)
        lo += w


def summed(t, rows, at):
    total = t[0, at * rows : (at + 1) * rows].astype(F32)
    for i in range(1, t.shape[0]):
        total = total + t[i, at * rows : (at + 1) * rows].astype(F32)
    return total


def norm_fwd_kernel(x, t, gain, y_out, n_out):
    y = x[...] + summed(t, x.shape[0], 0)
    y_out[...] = y
    inv = lax.rsqrt(jnp.mean(y * y, axis=-1, keepdims=True) + EPS)
    n_out[...] = (y * inv * gain[...]).astype(BF16)


def add_kernel(x, t, y_out):
    y_out[...] = x[...] + summed(t, x.shape[0], 1)


def norm_bwd_kernel(t, resid, d_res, gain, d_out, d_round, gain_out):
    x = resid[...]
    dn = summed(t, x.shape[0], 0)
    inv = lax.rsqrt(jnp.mean(x * x, axis=-1, keepdims=True) + EPS)
    gain_out[...] = jnp.sum(dn * x * inv, axis=0, keepdims=True)
    m = dn * gain[...]
    proj = jnp.mean(m * x, axis=-1, keepdims=True)
    d = d_res[...] + inv * m - x * (inv * inv * inv * proj)
    d_out[...] = d
    d_round[...] = d.astype(BF16)


def make_body(n_dp, n_row, n_col):
    pair = [(c, c ^ 1) for c in range(n_col)]
    swap = [(i, 1 - i) for i in range(n_row)]
    groups = [
        [c * n_row + i for c in range(k, n_col, 2) for i in range(n_row)] for k in range(2)
    ]
    plane = (COL, ROW)

    def gather_same(v):
        return lax.all_gather(v, plane, axis=0, tiled=False, axis_index_groups=groups)

    def other_core(v):
        return lax.ppermute(v, COL, pair)

    def other_row(v):
        return lax.ppermute(v, ROW, swap)

    def gather(v):
        own = gather_same(v).reshape(n_col // 2, n_row * v.shape[0], v.shape[1])
        return own, other_core(own)

    def scatter(p0, p1, late=None):
        blocks = (n_col // 2) * n_row
        width = p0.shape[2]
        sums = []
        for q0, q1 in ((p0, p1),) if late is None else ((p0, p1), late):
            got = other_core(q1)
            both = (q0.astype(F32) + got.astype(F32)).astype(BF16)
            sums.append(both.reshape(blocks, -1, width))
        both = sums[0] if late is None else jnp.concatenate(sums, axis=1)
        both = both.reshape(-1, width)
        moved = lax.all_to_all(both, plane, 0, 0, tiled=True, axis_index_groups=groups)
        return moved.reshape(blocks, -1, both.shape[1])

    def body(
        inputs, positions, segments, cotangent, w_query, w_key, w_value, w_output,
        w_gate, w_up, w_down, attn_gain, mlp_gain, query_gain, key_gain,
    ):
        layers = w_query.shape[0]
        half = inputs.shape[1]
        width = half * n_row
        tok_c = inputs.shape[0]
        tok = tok_c // n_row
        n_seq = n_col // 2
        r = lax.axis_index(ROW)
        c = lax.axis_index(COL)
        core = c % 2
        seq_id = c // 2
        row = (jnp.reshape(r, (1,)).astype(jnp.int32), jnp.reshape(core, (1,)).astype(jnp.int32))
        qw = w_query.shape[2] // n_row
        kw = w_key.shape[2] // n_row
        ow = w_output.shape[1] // n_row
        ff = w_gate.shape[2] // n_row

        ps = jnp.concatenate([positions, segments], axis=0)
        ps_other = other_row(ps)
        ps_all = jnp.stack([jnp.where(r == 0, ps, ps_other), jnp.where(r == 0, ps_other, ps)])

        def cut(w, axis, size, start):
            return lax.dynamic_slice_in_dim(w, start * size, size, axis)

        away = 1 - r
        dpi = lax.axis_index(DP)

        def piece(v):
            rows = v.shape[0] // n_dp
            return lax.dynamic_slice_in_dim(v, dpi * rows, rows, 0)

        def send_qkv(l):
            return jnp.concatenate(
                [
                    cut(w_query[l], 1, qw, away),
                    cut(w_key[l], 1, kw, away),
                    cut(w_value[l], 1, kw, away),
                ],
                axis=1,
            )

        def send_o(l):
            return cut(w_output[l], 0, ow, away)

        def send_mlp(l, lead):
            gu = jnp.concatenate(
                [piece(cut(w_gate[l], 1, ff, away)), piece(cut(w_up[l], 1, ff, away))], axis=1
            )
            rest = jnp.concatenate(lead + [piece(cut(w_down[l], 0, ff, away))], axis=0)
            low = rest.shape[0] // 3
            top = rest.shape[0] - low
            w = half // 2
            side = jnp.concatenate([rest[top:, :w], rest[top:, w:]], axis=0)
            return jnp.concatenate([gu, jnp.concatenate([rest[:top], side], axis=1)], axis=0)

        give = [send_mlp(l, []) for l in range(layers)]
        raw = lax.all_gather(inputs, plane, axis=0, tiled=False).reshape(
            n_seq, 2, n_row, tok_c, half
        )
        raw, late = lax.optimization_barrier((raw, give[1:]))
        give = give[:1] + list(late)
        pk_attn, pk_mlp = [], []
        attn_pack = (half, ow, 0, half)
        mlp_pack = (half // n_dp, ff // n_dp, 0)
        for l in range(layers):
            pk_attn.append(other_row(jnp.concatenate([send_qkv(l), send_o(l)], axis=0))[None])
            got = other_row(give[l])
            pk_mlp.append(lax.all_gather(got, DP, axis=0, tiled=False))

        cot_all = lax.all_gather(cotangent, plane, axis=0, tiled=False).reshape(
            n_seq, 2, n_row, tok_c, half
        )

        order = jnp.concatenate(
            [jnp.arange(tok_c) + core * tok_c, jnp.arange(tok_c) + (1 - core) * tok_c]
        )
        turned = jnp.where(core == 0, ps_all, jnp.roll(ps_all, tok_c, axis=2))
        freq = THETA ** (-2.0 * jnp.arange(HD // 2, dtype=F32) / HD)
        angles = turned[:, 0, :].astype(F32)[:, :, None] * freq[None, None, :]
        cos = jnp.cos(angles)
        sin = jnp.sin(angles)
        cos2 = jnp.concatenate([cos, cos], axis=-1)
        sin2 = jnp.concatenate([-sin, sin], axis=-1)
        seg = turned[:, 1, :]
        mask = (
            (seg[:, :, None] == seg[:, None, :]) & (order[None, None, :] <= order[None, :, None])
        ).astype(F32)

        gq = query_gain[:, None, :]
        gk = key_gain[:, None, :]
        ga = attn_gain[:, None, :]
        gm = mlp_gain[:, None, :]

        full = (n_seq, tok_c, width)
        nt = n_seq * SEQ
        wq_spec = lambda l: pl.BlockSpec((1, half, qw), lambda i, s, t: (l, 0, s[0]))
        wk_spec = lambda l: pl.BlockSpec((1, half, kw), lambda i, s, t: (l, 0, s[0]))
        wo_spec = lambda l: pl.BlockSpec((1, ow, half), lambda i, s, t: (l, s[0], 0))
        wg_spec = lambda l: pl.BlockSpec((1, half, ff), lambda i, s, t: (l, 0, s[0]))
        wd_spec = lambda l: pl.BlockSpec((1, ff, half), lambda i, s, t: (l, s[0], 0))
        q3 = qw + 2 * kw
        tables = [per_seq((n_seq, SEQ, HD)), per_seq((n_seq, SEQ, HD)), per_seq((n_seq, SEQ, SEQ))]

        def qkv_specs(l):
            return [
                wq_spec(l), wk_spec(l), wk_spec(l), wo_spec(l), whole(pk_attn[l].shape),
                whole((1, HD)), whole((1, HD)),
            ] + tables

        def qkv_args(l):
            return [
                w_query, w_key, w_value, w_output, pk_attn[l], gq[l], gk[l],
                cos2, sin2, mask,
            ]

        def mlp_specs(l):
            return [wg_spec(l), wg_spec(l), wd_spec(l), whole(pk_mlp[l].shape)]

        def mlp_args(l):
            return [w_gate, w_up, w_down, pk_mlp[l]]

        def attn_fwd(l, n0, n1):
            return call(
                functools.partial(attn_fwd_kernel, attn_pack), (n_seq,),
                [per_seq(full), per_seq(full)] + qkv_specs(l),
                [per_seq(full), per_seq(full), per_seq((n_seq, SEQ, qw + kw)),
                 per_seq((n_seq, SEQ, kw)), per_seq((n_seq, SEQ, qw))],
                [sds(full, BF16), sds(full, BF16), sds((n_seq, SEQ, qw + kw), F32),
                 sds((n_seq, SEQ, kw), BF16), sds((n_seq, SEQ, qw), BF16)],
                2 * nt * width * (q3 + qw), 6e6, row, [n0, n1] + qkv_args(l),
            )

        def mlp_fwd(l, n0, n1):
            return call(
                functools.partial(mlp_fwd_kernel, mlp_pack), (n_seq,),
                [per_seq(full), per_seq(full)] + mlp_specs(l),
                [per_seq(full), per_seq(full), per_seq((n_seq, SEQ, 2 * ff)),
                 per_seq((n_seq, SEQ, ff))],
                [sds(full, BF16), sds(full, BF16), sds((n_seq, SEQ, 2 * ff), F32),
                 sds((n_seq, SEQ, ff), BF16)],
                6 * nt * width * ff, 8e6, row, [n0, n1] + mlp_args(l),
            )

        def mlp_bwd(l, d0, d1, gu):
            return call(
                functools.partial(mlp_bwd_kernel, mlp_pack), (n_seq,),
                grad_specs(l)[0] + [per_seq((n_seq, SEQ, 2 * ff))] + mlp_specs(l),
                [per_seq(full), per_seq(full), per_seq((n_seq, SEQ, 2 * ff))],
                [sds(full, BF16), sds(full, BF16), sds((n_seq, SEQ, 2 * ff), BF16)],
                6 * nt * width * ff, 8e6, row, [d0, d1, gu] + mlp_args(l),
            )

        def attn_bwd(l, d0, d1, qk, v, attn, normed=()):
            specs = [per_seq(full), per_seq(full), per_seq((n_seq, SEQ, q3)),
                     per_seq((n_seq, 1, 2 * HD))]
            shapes = [sds(full, BF16), sds(full, BF16), sds((n_seq, SEQ, q3), BF16),
                      sds((n_seq, 1, 2 * HD), F32)]
            if normed:
                specs.append(per_seq((n_seq, 1, width)))
                shapes.append(sds((n_seq, 1, width), F32))
            return call(
                functools.partial(attn_bwd_kernel, attn_pack), (n_seq,),
                [per_seq(full), per_seq(full), per_seq((n_seq, SEQ, qw + kw)),
                 per_seq((n_seq, SEQ, kw)), per_seq((n_seq, SEQ, qw))] + qkv_specs(l)
                + [per_seq(full) for _ in normed],
                specs, shapes, 2 * nt * width * (q3 + qw), 8e6, row,
                [d0, d1, qk, v, attn] + qkv_args(l) + list(normed),
            )

        def wgrad(kernel, rows, cols, args):
            return call(
                kernel, (1,), [whole(a.shape) for a in args],
                whole((n_dp, rows, cols)), sds((n_dp, rows, cols), BF16),
                2 * nt * n_dp * rows * cols, 8e6, row, args,
            )

        def norm_fwd(x, t, gain):
            shapes = [sds(x.shape, F32), sds(x.shape, BF16)]
            return small_call(norm_fwd_kernel, shapes, [x, t, gain])

        def norm_bwd(t, resid, d_res, gain):
            shapes = [sds(resid.shape, F32), sds(resid.shape, BF16), sds(gain.shape, F32)]
            return small_call(norm_bwd_kernel, shapes, [t, resid, d_res, gain])

        def own_tokens(blocks):
            mine = lax.dynamic_slice_in_dim(blocks, r * tok, tok, 1)
            return jnp.concatenate([mine[i] for i in range(n_row)], axis=-1).astype(F32)

        def own_block(blocks):
            mine = lax.dynamic_index_in_dim(blocks, seq_id, 0, keepdims=False)
            return own_tokens(lax.dynamic_index_in_dim(mine, core, 0, keepdims=False))

        x = own_block(raw)
        raw_shape = (1, 1, n_row, tok_c, half)
        normed = call(
            norm_first_kernel, (n_seq,),
            [
                pl.BlockSpec(raw_shape, lambda i, s, t: (i, t[0], 0, 0, 0)),
                pl.BlockSpec(raw_shape, lambda i, s, t: (i, 1 - t[0], 0, 0, 0)),
                whole((1, width)),
            ],
            [per_seq(full), per_seq(full)], [sds(full, BF16), sds(full, BF16)],
            1e6, 4e6, row, [raw, raw, ga[0]],
        )

        saved = []
        for l in range(layers):
            n1_own, n1_oth = normed
            p0, p1, qk, v, attn = attn_fwd(l, n1_own, n1_oth)
            middle, n2 = norm_fwd(x, scatter(p0, p1), gm[l])
            n2_own, n2_oth = gather(n2)
            p0, p1, gu, hidden = mlp_fwd(l, n2_own, n2_oth)
            saved.append((x, n1_own, n1_oth, qk, v, attn, middle, n2_own, n2_oth, gu, hidden))
            if l + 1 < layers:
                moved = scatter(p0, p1)
                x, nxt = norm_fwd(middle, moved, ga[l + 1])
                normed = gather(nxt)
            else:
                last_p = (p0, p1)
                last_mid = middle

        def to_block(v):
            v = v.astype(F32)
            halves = [v[:, i * half : (i + 1) * half] for i in range(n_row)]
            mine = jnp.where(r == 0, halves[0], halves[1])
            got = other_row(jnp.where(r == 0, halves[1], halves[0]))
            return jnp.where(
                r == 0, jnp.concatenate([mine, got], 0), jnp.concatenate([got, mine], 0)
            )

        d0 = d1 = cot_all

        def grad_specs(l):
            if l + 1 < layers:
                return [per_seq(full), per_seq(full)], [whole(full), whole(full)]
            one, every = (1, 1, n_row, tok_c, half), (n_seq, 1, n_row, tok_c, half)
            return (
                [
                    pl.BlockSpec(one, lambda i, s, t: (i, t[0], 0, 0, 0)),
                    pl.BlockSpec(one, lambda i, s, t: (i, 1 - t[0], 0, 0, 0)),
                ],
                [
                    pl.BlockSpec(every, lambda i, s, t: (0, t[0], 0, 0, 0)),
                    pl.BlockSpec(every, lambda i, s, t: (0, 1 - t[0], 0, 0, 0)),
                ],
            )

        d_own = own_block(cot_all)
        kb = half // n_dp
        mlp_red = [None] * layers
        attn_red = [None] * layers
        g_attn = [None] * layers
        g_mlp = [None] * layers
        g_head = [None] * layers
        for l in reversed(range(layers)):
            xin, n1_own, n1_oth, qk, v, attn, middle, n2_own, n2_oth, gu, hidden = saved[l]
            o0, o1 = d0, d1
            p0, p1, dgu = mlp_bwd(l, d0, d1, gu)
            h_got = other_row(hidden)
            a_got = other_row(attn)
            args = [n2_own, n2_oth, dgu]
            part_shape = (n_dp, 3 * kb, 2 * ff)
            part = call(
                wgrad_up_kernel, (1,), [whole(a.shape) for a in args],
                pl.BlockSpec((n_dp, 2 * kb, 2 * ff), lambda i, s, t: (0, 0, 0)),
                sds(part_shape, BF16), 8 * nt * half * ff, 4e6, row, args,
            )
            args = [o0, o1, hidden, h_got]
            part = call(
                wgrad_down_kernel, (1,),
                grad_specs(l)[1] + [whole(hidden.shape)] * 2 + [pl.BlockSpec(memory_space=pl.ANY)],
                pl.BlockSpec((n_dp, kb, 2 * ff), lambda i, s, t: (0, 2, 0)),
                sds(part_shape, BF16), 4 * nt * half * ff, 4e6, row, args + [part],
                alias={len(args) + 2: 0},
            )
            moved = scatter(p0, p1)
            mlp_red[l] = lax.psum_scatter(part, DP, scatter_dimension=0, tiled=False)
            d_mid, d_mid_round, g_mlp[l] = norm_bwd(moved, middle, d_own, gm[l])
            d0, d1 = gather(d_mid_round)
            got = attn_bwd(l, d0, d1, qk, v, attn, (n1_own, n1_oth) if l == 0 else ())
            p0, p1, dqkv, g_head[l] = got[:4]
            part = wgrad(
                wgrad_attn_kernel, 3 * kb, q3,
                [n1_own, n1_oth, dqkv, d0, d1, attn, a_got],
            )
            moved = scatter(p0, p1, last_p if l == 0 else None)
            attn_red[l] = lax.psum_scatter(part, DP, scatter_dimension=0, tiled=False)
            d_own, d_round, g_attn[l] = norm_bwd(moved, xin, d_mid, ga[l])
            if l == 0:
                g_attn[l] = jnp.sum(got[4], axis=0) / ga[l]
                (x,) = small_call(add_kernel, [sds(last_mid.shape, F32)], [last_mid, moved])
                outputs = to_block(x)
            if l > 0:
                d0, d1 = gather(d_round)
        d_inputs = to_block(d_own)

        gains = jnp.concatenate(
            [g.reshape(-1) for g in g_attn]
            + [g.reshape(-1) for g in g_mlp]
            + [jnp.sum(g, axis=0).reshape(-1) for g in g_head]
        )
        gains = gains.reshape(-1, HD)
        for axis, size in ((COL, n_col), (ROW, n_row), (DP, n_dp)):
            step = 1
            while step < size:
                peers = [(i, i ^ step) for i in range(size)]
                gains = gains + lax.ppermute(gains, axis, peers)
                step *= 2
        gains = gains.reshape(-1)
        lw = layers * width
        ga_out = gains[:lw].reshape(layers, width)
        gm_out = gains[lw : 2 * lw].reshape(layers, width)
        gh = gains[2 * lw :].reshape(layers, 2, HD)

        def finish(kernel, reds, shapes):
            args = []
            for z in reds:
                args += [z, other_row(z[kb : 2 * kb])]
            return call(
                kernel, (1,), [whole(a.shape) for a in args],
                [whole(o) for o in shapes], [sds(o, F32) for o in shapes], 1e5, 8e6, row, args,
            )

        g_gate, g_up, g_down = finish(
            finish_mlp_kernel, mlp_red,
            [(layers, kb, 2 * ff), (layers, kb, 2 * ff), (layers, 2 * ff // n_dp, half)],
        )
        got = []
        for z in attn_red:
            got.append(other_row(z[kb : 2 * kb]))
        args = [attn_red[0]]
        for l in range(1, layers):
            args += [attn_red[l], got[l]]
        shapes = [(layers, kb, 2 * qw), (layers, kb, 2 * kw), (layers, kb, 2 * kw)]
        outs = shapes + [(layers, 2 * ow // n_dp, half)]
        parts = call(
            finish_attn_kernel, (1,), [whole(a.shape) for a in args],
            [whole(o) for o in outs], [sds(o, F32) for o in outs], 1e5, 4e6, row, args,
        )
        g_o = parts[3]
        anywhere = pl.BlockSpec(memory_space=pl.ANY)
        g_q, g_k, g_v = call(
            finish_last_kernel, (1,), [whole(got[0].shape)] + [anywhere] * 3,
            [
                pl.BlockSpec((1, kb, o[2] // 2), lambda i, s, t: (0, 0, 1 - s[0]))
                for o in shapes
            ],
            [sds(o, F32) for o in shapes], 1e5, 1e6, row, [got[0], *parts[:3]],
            alias={3: 0, 4: 1, 5: 2},
        )
        stacked = (g_q, g_k, g_v, g_o, g_gate, g_up, g_down)
        return (
            outputs, d_inputs, *stacked, ga_out, gm_out, gh[:, 0], gh[:, 1],
        )

    return body


def solution(mesh):
    body = make_body(mesh.shape[DP], mesh.shape[ROW], mesh.shape[COL])
    act = P((DP, COL), ROW)
    seq = P((DP, ROW), None)
    w_in = P(None, ROW, COL)
    w_out = P(None, COL, ROW)
    g_in = P(None, (ROW, DP), COL)
    g_out = P(None, (COL, DP), ROW)

    return jax.shard_map(
        body,
        mesh=mesh,
        in_specs=(
            act, seq, seq, act, w_in, w_in, w_in, w_out, w_in, w_in, w_out, P(), P(), P(), P(),
        ),
        out_specs=(
            act, act, g_in, g_in, g_in, g_out, g_in, g_in, g_out, P(), P(), P(), P(),
        ),
        check_vma=False,
    )
```
